512 devices in a mesh: tm: 8 (over y), grid: 64 (over x, z, core).
Axes of the slice: x: 4, y: 8, z: 8, core: 2. Of those that a mesh axis runs over, the one named last changes fastest.
Arguments:
- panel_source: float32 [16, 524288], P('tm', 'grid'), may hold values from -6 to 6
- proj_weight: float32 [18, 524288], P(None, 'grid'), may hold values from -1.5 to 1.5
- box_slots: int32 [16, 65536], P(None, 'grid'), may hold values from 0 to 8191, as said below
- box_count: int32 [65536], P('grid'), may hold values from 0 to 16, as said below
- box_cell: int32 [65536], P('grid'), may hold values from 0 to 16383
- decay: float32 [128, 128, 128], P(None, 'grid'), may hold values from 0.85 to 1, as said below
Outputs:
- potential: float32 [16, 524288], P('tm', 'grid')
The draws below stay inside these ranges and needn't reach their ends.
Inputs may be any that keep to these rules, and one draw needn't show every extreme that they name: `box_slots`: in each device's block of 1024 boxes, the first box_count[b] slots of box b name distinct panels among that device's 8192, every panel in exactly one box; later slots hold 0. `box_count`: every device's block of boxes holds a full box and an empty one; the counts of one block sum to 8192. decay at (kx, ky, kz) equals decay at ((-kx) mod 128, (-ky) mod 128, (-kz) mod 128).
All inputs are finite; a program needn't handle non-finite values.
Results may differ from the reference program's by a relative error of at most 0.0003.
Values sent between devices are 32-bit elements; how exact they have to be, the bound alone decides.
No kernel may reach another device: no remote copies, remote signals or barrier semaphores. Data moves between devices by JAX's collectives and lax.ppermute only.
A program may use at most 128 MiB of HBM per device.

```python
import jax
import jax.numpy as jnp
from jax import lax

NX = 128
NY = 128
NZ = 128
STEN = 18
BOXCAP = 16
NB_DEV = 1024
CX = 2
P_DEV = 8192
PANELS = 524288
BOXES = 65536
STEPS = 16
N_GRID = 64


def box_layout(key):
    key = jax.random.fold_in(key, 7)
    half_cap = BOXCAP // 2
    pair_key, order_key = jax.random.split(key)
    spread = jax.random.randint(pair_key, (N_GRID, NB_DEV // 2), 0, half_cap + 1)
    spread = spread.at[:, 0].set(half_cap)
    counts = jnp.stack([half_cap + spread, half_cap - spread], axis=2).reshape(N_GRID, NB_DEV)
    offsets = jnp.cumsum(counts, axis=1) - counts

    def one_order(order_seed):
        return jax.random.permutation(order_seed, P_DEV)
    orders = jax.vmap(one_order)(jax.random.split(order_key, N_GRID))
    slot_index = jnp.arange(BOXCAP, dtype=jnp.int32)
    position = jnp.minimum(offsets[:, :, None] + slot_index[None, None, :], P_DEV - 1)
    chosen = jnp.take_along_axis(orders, position.reshape(N_GRID, -1), axis=1).reshape(N_GRID, NB_DEV, BOXCAP)
    filled = jnp.where(slot_index[None, None, :] < counts[:, :, None], chosen, 0)
    return (counts.reshape(-1).astype(jnp.int32), filled.reshape(N_GRID * NB_DEV, BOXCAP).T.astype(jnp.int32))


def draw_box_slots(key, part):
    return box_layout(key)[1]


def draw_box_count(key, part):
    return box_layout(key)[0]


def draw_decay(key, part):
    pick_key, slow_key, fast_key = jax.random.split(jax.random.fold_in(key, 11), 3)
    shape = (NX, NY, NZ)
    slow_share = 0.5
    picks = jax.random.uniform(pick_key, shape, jnp.float32)
    slow = jnp.exp(jnp.log(0.1) * jax.random.uniform(slow_key, shape, jnp.float32, 0.2, 1.0) / STEPS)
    slow = jnp.maximum(slow, 0.94)
    fast = jax.random.uniform(fast_key, shape, jnp.float32, 0.85, 0.93)
    base = jnp.where(picks < slow_share, slow, fast).astype(jnp.float32)
    mirrored = jnp.roll(jnp.flip(base, (0, 1, 2)), 1, (0, 1, 2))
    index_x = jax.lax.broadcasted_iota(jnp.int32, shape, 0)
    index_y = jax.lax.broadcasted_iota(jnp.int32, shape, 1)
    index_z = jax.lax.broadcasted_iota(jnp.int32, shape, 2)
    flat_here = (index_x * NY + index_y) * NZ + index_z
    flat_there = ((NX - index_x) % NX * NY + (NY - index_y) % NY) * NZ + (NZ - index_z) % NZ
    return jnp.where(flat_here <= flat_there, base, mirrored).astype(jnp.float32)


def set_ends(values, rng, low, largest):
    longest = values.shape.index(max(values.shape))
    spots = []
    for shift in (0, 1):
        where = [jax.random.randint(jax.random.fold_in(rng, axis), (), 0, length) for axis, length in enumerate(values.shape)]
        where[longest] = (where[longest] + shift) % values.shape[longest]
        spots.append(tuple(where))
    return values.at[spots[0]].set(low).at[spots[1]].set(largest)


def shard_levels(own_key, dims, shards, least, high):
    gain = 1.0
    for axis_at, shards_of in shards:
        draws = jax.random.uniform(jax.random.fold_in(jax.random.fold_in(own_key, 6), axis_at), (shards_of,), jnp.float32, least / len(shards), high / len(shards))
        gain = gain * jnp.repeat(jnp.exp(draws), dims[axis_at] // shards_of).reshape((-1,) + (1,) * (len(dims) - 1 - axis_at))
    return gain


def noise(key, shape, deviation, most, shards=(), kind=jnp.bfloat16):
    result = deviation * jax.random.normal(key, shape, jnp.float32)
    if shards:
        result = result * shard_levels(key, shape, shards, -0.22, 0.18)
    return jnp.clip(result, -most, most).astype(kind)


def setup_inputs(seed: int = 0) -> dict:
    key_list = jax.random.split(jax.random.key(seed), 7)
    panel_source = noise(key_list[0], (STEPS, PANELS), 1.0, 6.0, ((0, 8), (1, 64)), jnp.float32)
    proj_weight = noise(key_list[1], (STEN, PANELS), 0.25, 1.5, ((1, 64),), jnp.float32)
    box_slots = draw_box_slots(jax.random.fold_in(key_list[6], 71), 0)
    box_count = draw_box_count(jax.random.fold_in(key_list[6], 71), 0)
    box_cell = set_ends(jax.random.randint(key_list[4], (BOXES,), 0, (CX - 1) * NY * NZ), jax.random.fold_in(key_list[4], 1), 0, ((CX - 1) * NY * NZ) - 1).astype(jnp.int32)
    decay = draw_decay(jax.random.fold_in(key_list[6], 71), 0)
    return dict(panel_source=panel_source, proj_weight=proj_weight, box_slots=box_slots, box_count=box_count, box_cell=box_cell, decay=decay)


wave_step = 0.5

def laplace_symbol(length, freq_index):
    return 4.0 * jnp.sin(jnp.pi * freq_index / length) ** 2

def reference(panel_source, proj_weight, box_slots, box_count, box_cell, decay):
    slab_depth = NX // N_GRID
    per_owner = NB_DEV // N_GRID
    box_ids = jnp.arange(BOXES, dtype=jnp.int32)
    owner_index = box_ids % NB_DEV // per_owner
    slot_panel = box_slots + (box_ids // NB_DEV * P_DEV)[None, :]
    live_mask = (jnp.arange(BOXCAP, dtype=jnp.int32)[:, None] < box_count[None, :]).astype(jnp.float32)
    slot_weight = proj_weight[:, slot_panel] * live_mask[None]
    plane_index = owner_index * slab_depth + box_cell // (NY * NZ)
    row_index = box_cell // NZ % NY
    col_index = box_cell % NZ
    offsets = []
    for shift_x in range(2):
        for shift_y in (-1, 0, 1):
            for shift_z in (-1, 0, 1):
                offsets.append((plane_index + shift_x) * (NY * NZ) + (row_index + shift_y) % NY * NZ + (col_index + shift_z) % NZ)
    targets = jnp.stack(offsets)
    flat_targets = targets.reshape(-1)
    symbol = laplace_symbol(NX, jnp.arange(NX, dtype=jnp.float32))[:, None, None] + laplace_symbol(NY, jnp.arange(NY, dtype=jnp.float32))[None, :, None] + laplace_symbol(NZ, jnp.arange(NZ, dtype=jnp.float32))[None, None, :]
    phases = wave_step * jnp.sqrt(symbol)
    kernel = 1.0 / (1.0 + symbol)
    rate_cos = decay * jnp.cos(phases)
    rate_sin = decay * jnp.sin(phases)

    def advance(carried, source_row):
        plus_re, plus_im, minus_re, minus_im = carried
        box_values = lax.optimization_barrier(jnp.sum(slot_weight * source_row[slot_panel][None], axis=1))
        density = jnp.zeros((NX * NY * NZ,), jnp.float32).at[flat_targets].add(box_values.reshape(-1))
        spectrum = jnp.fft.fftn(density.reshape(NX, NY, NZ))
        spec_re = spectrum.real
        spec_im = spectrum.imag
        next_plus_re = rate_cos * plus_re - rate_sin * plus_im + spec_re
        next_plus_im = rate_cos * plus_im + rate_sin * plus_re + spec_im
        next_minus_re = rate_cos * minus_re + rate_sin * minus_im + spec_re
        next_minus_im = rate_cos * minus_im - rate_sin * minus_re + spec_im
        field_spec = lax.complex(0.5 * kernel * (next_plus_re + next_minus_re), 0.5 * kernel * (next_plus_im + next_minus_im))
        field_flat = jnp.fft.ifftn(field_spec).real.reshape(-1)
        box_field = field_flat[targets]
        slot_values = lax.optimization_barrier(jnp.sum(slot_weight * box_field[:, None, :], axis=0))
        potential_row = jnp.zeros((PANELS,), jnp.float32).at[slot_panel.reshape(-1)].add(slot_values.reshape(-1))
        return ((next_plus_re, next_plus_im, next_minus_re, next_minus_im), potential_row)
    zeros_grid = jnp.zeros((NX, NY, NZ), jnp.float32)
    final_modes, potential = lax.scan(advance, (zeros_grid, zeros_grid, zeros_grid, zeros_grid), panel_source)
    return potential
```

```python
import jax
import jax.numpy as jnp
import ml_dtypes
import numpy as np
from jax import lax
from jax.experimental import pallas as pl
from jax.experimental.pallas import tpu as pltpu
from jax.sharding import PartitionSpec as P

N = 128
STEN = 18
KROWS = 24
CELL_ROW = 18
ROWS = 2 * KROWS
WIDTH = 16 * ROWS // 128
PDEV = 8192
BOXES = 1024
F32 = jnp.float32
BF16 = jnp.bfloat16


def halves(table):
    table = np.asarray(table, np.float64).astype(np.float32)
    high = table.astype(ml_dtypes.bfloat16)
    low = (table - high.astype(np.float32)).astype(ml_dtypes.bfloat16)
    return np.stack([high, low])


def angle(rows, cols):
    return 2.0 * np.pi * (np.outer(rows, cols) % N) / N


def tables():
    index = np.arange(N)
    slot = (index // 32) * 16 + index % 16
    imag = (index // 16) % 2 == 1
    ang = angle(index, slot)
    real_z = np.cos(ang)
    imag_z = np.where(slot[None] == 0, np.cos(np.pi * index)[:, None], -np.sin(ang))
    fz = np.concatenate(
        [np.where(imag[None], imag_z, real_z), np.where(imag[None], -real_z, imag_z)], axis=1
    )
    ky = np.concatenate([2 * np.arange(64), 2 * np.arange(64) + 1])
    ay = angle(ky, index)
    fy = np.stack([np.cos(ay), np.sin(ay)])

    grid = np.arange(64)
    bd = np.zeros((2, 2, 2, 64, 2, 2, N))
    bi = np.zeros((2, 2, N, 2, 2, 2, 64))
    for dx in range(2):
        ax = angle(2 * grid + dx, index)
        cos, sin = np.cos(ax), np.sin(ax)
        for half in range(2):
            bd[dx, 0, half, :, half, 0] = cos
            bd[dx, 0, half, :, half, 1] = -sin
            bd[dx, 1, half, :, half, 0] = sin
            bd[dx, 1, half, :, half, 1] = cos
            bi[half, 0, :, dx, 0, half] = cos.T / N
            bi[half, 0, :, dx, 1, half] = sin.T / N
            bi[half, 1, :, dx, 0, half] = -sin.T / N
            bi[half, 1, :, dx, 1, half] = cos.T / N
    bd = bd.reshape(512, 512)
    bi = bi.reshape(512, 512)

    weight = np.where(slot == 0, 0.0, 2.0)[:, None] / N
    cz = np.cos(ang.T) * weight
    sz = np.sin(ang.T) * weight
    gz = np.concatenate(
        [np.where(imag[:, None], -sz, cz), np.where(imag[:, None], -cz, -sz)], axis=1
    )
    gy = np.concatenate([np.cos(ay.T), np.sin(ay.T)], axis=1) / N
    self_row = (ky == 0) | (ky == 64)
    pattern = np.where((ky <= 64)[:, None], 1.0, np.cos(np.pi * index)[None])
    c1 = np.where(self_row, 1.0, 2.0)[:, None] * pattern / N
    c2 = np.where(self_row[:, None], np.cos(np.pi * index)[None], 0.0) / N
    c3 = np.where(self_row[:, None], 0.0, -2.0 * pattern) / N
    cs = np.stack([c1, c2, c3]).astype(np.float32)

    lam = 4.0 * np.sin(np.pi * index / N) ** 2
    lz = np.broadcast_to(lam[:, None], (N, N)).astype(np.float32)
    lx = np.broadcast_to(lam[None], (8, N)).astype(np.float32)
    return dict(
        fz=halves(fz), fy=halves(fy), bd=halves(bd), bi=halves(bi), gz=halves(gz), gy=halves(gy),
        cs=cs, lz=lz, lx=lx,
    )


def split(values):
    high = values.astype(BF16)
    return high, (values - high.astype(F32)).astype(BF16)


def dot(left, right):
    return lax.dot_general(left, right, (((1,), (0,)), ((), ())), preferred_element_type=F32)


def dot_nt(left, right):
    return lax.dot_general(left, right, (((1,), (1,)), ((), ())), preferred_element_type=F32)


def dot_right(values, table):
    high, low = split(values)
    return dot(high, table[0]) + (dot(low, table[0]) + dot(high, table[1]))


def dot_left(table, values):
    high, low = split(values)
    return dot(table[0], high) + (dot(table[0], low) + dot(table[1], high))


def iota(shape, axis):
    return lax.broadcasted_iota(jnp.int32, shape, axis)


def one_hot(mask):
    return jnp.where(mask, 1.0, 0.0).astype(BF16)


def write_owner_rows(turned, out_ref):
    for part in range(WIDTH):
        out_ref[pl.ds(part, 64, stride=WIDTH), :] = turned[part * 128 : (part + 1) * 128, :].T


def read_owner_rows(in_ref, turned_ref):
    for part in range(WIDTH):
        turned_ref[part * 128 : (part + 1) * 128, :] = in_ref[pl.ds(part, 64, stride=WIDTH), :].T


def panels_kernel(source, weight, slots, count, cell, out, where, oh_ref, left_ref):
    box = iota((1, BOXES), 1)
    low_value = (((box // 4) % 4) * 64 + box // 16).astype(F32)
    high_value = (box % 4).astype(F32)
    total = jnp.zeros((128, 128), F32)
    row64 = iota((64, BOXES), 0)
    row128 = iota((128, BOXES), 0)

    def invert(s, total):
        panel = slots[pl.ds(s, 1), :]
        page = jnp.where(s < count[...], panel // 128, -1)
        hit = row64 == page
        left = jnp.concatenate(
            [jnp.where(hit, low_value, 0.0), jnp.where(hit, high_value, 0.0)], axis=0
        ).astype(BF16)
        return total + dot_nt(left, one_hot(row128 == panel % 128))

    total = lax.fori_loop(0, 16, invert, total)
    where_now = (total + 0.5).astype(jnp.int32)
    where[...] = where_now

    def spread(page, carry):
        at = pl.multiple_of(page * 128, 128)
        low = where[pl.ds(page, 1), :]
        high = where[pl.ds(64 + page, 1), :]
        oh_ref[:, pl.ds(at, 128)] = one_hot(iota((256, 128), 0) == low)
        tile = weight[:, pl.ds(at, 128)]
        tile = jnp.concatenate([tile, jnp.zeros((KROWS - STEN, 128), F32)], axis=0)
        both = jnp.concatenate(
            [tile * source[0:1, pl.ds(at, 128)], tile * source[1:2, pl.ds(at, 128)]], axis=0
        )
        first, second = split(both)
        for part, piece in enumerate((first.astype(F32), second.astype(F32))):
            for quarter in range(4):
                at_row = (part * 4 + quarter) * ROWS
                left_ref[at_row : at_row + ROWS, pl.ds(at, 128)] = jnp.where(
                    high == quarter, piece, 0.0
                ).astype(BF16)
        return carry

    lax.fori_loop(0, 64, spread, 0)
    sums = dot_nt(left_ref[...], oh_ref[...])
    sums = sums[: 4 * ROWS] + sums[4 * ROWS :]

    cells = cell[...]
    match = iota((16, BOXES), 0) == box % 16
    left = jnp.concatenate(
        [
            jnp.where(match, (cells // 128).astype(F32), 0.0),
            jnp.where(match, (cells % 128).astype(F32), 0.0),
        ],
        axis=0,
    ).astype(BF16)
    owned = dot_nt(left, one_hot(iota((64, BOXES), 0) == box // 16))
    cell_rows = owned[:16] * 128.0 + owned[16:]

    blocks = []
    at_cell = iota((ROWS, 64), 0) == CELL_ROW
    for j in range(16):
        block = sums[(j % 4) * ROWS : (j % 4 + 1) * ROWS, (j // 4) * 64 : (j // 4 + 1) * 64]
        blocks.append(jnp.where(at_cell, cell_rows[j : j + 1, :], block))
    write_owner_rows(jnp.concatenate(blocks, axis=0), out)


def slab_kernel(recv, fz, fy, out, cell_out, turned, values, left_h, left_l, right):
    read_owner_rows(recv, turned)
    lane = iota((128, 128), 1)
    row = iota((128, 128), 0)
    columns = []
    for j in range(16):
        at = j * ROWS + CELL_ROW
        columns.append(recv[pl.ds(at // 128, 64, stride=WIDTH), :][:, at % 128 : at % 128 + 1])
    for pair in range(8):
        value = jnp.concatenate(
            [
                turned[(2 * pair) * ROWS : (2 * pair + 1) * ROWS, :],
                turned[(2 * pair + 1) * ROWS : (2 * pair + 2) * ROWS, :],
            ],
            axis=1,
        )
        values[pair] = value
        cell_out[pair : pair + 1, :] = value[CELL_ROW : CELL_ROW + 1, :].astype(jnp.int32)
        column = jnp.concatenate([columns[2 * pair], columns[2 * pair + 1]], axis=0)
        column_z = column.astype(jnp.int32) % 128
        for dz in range(3):
            at = (pair * 3 + dz) * 128
            right[at : at + 128, :] = one_hot(lane == (column_z + (dz - 1)) % 128)

    def fill(pair, carry):
        cell_y = cell_out[pl.ds(pair, 1), :] // 128
        value = values[pair]
        hits = [row == (cell_y + (dy - 1)) % 128 for dy in range(3)]
        for dz in range(3):
            at = pl.multiple_of((pair * 3 + dz) * 128, 128)
            for step in range(2):
                for dx in range(2):
                    block = jnp.zeros((128, 128), F32)
                    for dy in range(3):
                        k = step * KROWS + 9 * dx + 3 * dy + dz
                        block = jnp.where(hits[dy], value[k : k + 1, :], block)
                    first, second = split(block)
                    at_row = (2 * step + dx) * 128
                    left_h[at_row : at_row + 128, pl.ds(at, 128)] = first
                    left_l[at_row : at_row + 128, pl.ds(at, 128)] = second
        return carry

    lax.fori_loop(0, 8, fill, 0)
    density = dot(left_h[...], right[...]) + dot(left_l[...], right[...])
    both = dot_right(density, fz)

    def beside(at):
        return jnp.concatenate(
            [both[t * 128 : (t + 1) * 128, at : at + 128] for t in range(4)], axis=1
        )

    even = dot_left((fy[0, 0], fy[1, 0]), beside(0))
    odd = dot_left((fy[0, 1], fy[1, 1]), beside(128))
    ky = (row % 64) * 2 + row // 64
    own = (ky == 0) | (ky == 64)
    pencils = []
    for t in range(4):
        a = even[:, t * 128 : (t + 1) * 128]
        b = odd[:, t * 128 : (t + 1) * 128]
        full = a + b
        full = jnp.where(lane == 0, jnp.where(ky <= 64, a, pltpu.roll(a, 112, 1)), full)
        second = jnp.where(own, a, jnp.where(ky < 64, b, -pltpu.roll(b, 16, 1)))
        pencils.append(jnp.where(lane == 16, second, full))
    for q in range(4):
        piece = jnp.concatenate([p[:, q * 32 : (q + 1) * 32] for p in pencils], axis=1)
        out[q * 64 : (q + 1) * 64, :] = piece[:64]
        out[(4 + q) * 64 : (5 + q) * 64, :] = piece[64:]


def column_kernel(place, recv, decay, bd, bi, lz, lx, out, turned_decay, spectra, fields):
    block = place[0]
    column = place[1]
    ky_low = block // 4
    q = block % 4
    ky = 2 * column + ky_low
    special = ((block == 0) & ((column == 0) | (column == 32))).astype(jnp.int32)
    parts = [recv[mp * 128 : (mp + 1) * 128, :].T for mp in range(4)]
    row_in_slot = iota((128, 128), 0) % 16
    lefts = []
    for dx in range(2):
        extra = jnp.concatenate(
            [
                parts[mp][(2 * n + dx) * 32 + 16 : (2 * n + dx) * 32 + 17, :]
                for mp in range(4)
                for n in range(2)
            ],
            axis=0,
        )
        extra = jnp.where(special == 1, extra, 0.0)
        for ri in range(2):
            main = jnp.concatenate(
                [
                    parts[mp][(2 * n + dx) * 32 + ri * 16 : (2 * n + dx) * 32 + ri * 16 + 16, :]
                    for mp in range(4)
                    for n in range(2)
                ],
                axis=0,
            )
            if ri == 1:
                main = jnp.where((row_in_slot + (1 - special)) == 0, 0.0, main)
                extra = jnp.zeros_like(extra)
            lefts.append(jnp.concatenate([main, extra], axis=0))
    spectra[...] = dot_right(jnp.concatenate(lefts, axis=1), bd)

    here = jnp.where(
        ky_low == 1, decay[pl.ds(1, 128, stride=2), :], decay[pl.ds(0, 128, stride=2), :]
    )
    turned_decay[...] = here.T
    slots_at = pl.multiple_of(q * 16, 16)
    moved = jnp.where((q == 0) & (ky > 64), 1, 0)
    at_first = iota((16, 128), 0) + (1 - moved) == 0
    damp_last = turned_decay[64:65, :]
    damp_main = jnp.where(at_first, damp_last, turned_decay[pl.ds(slots_at, 16), :])
    lam_xy = lx[0:1, :] + lz[pl.ds(ky, 1), :]
    lam_main = lam_xy + jnp.where(at_first, lz[64:65, :], lz[pl.ds(slots_at, 16), :])
    lam_last = lam_xy + lz[64:65, :]

    for damp, lam, base, size in ((damp_main, lam_main, 0, 16), (damp_last, lam_last, 128, 1)):
        theta = 0.5 * jnp.sqrt(lam)
        rate_cos = damp * jnp.cos(theta)
        rate_sin = damp * jnp.sin(theta)
        kernel = 1.0 / (1.0 + lam)
        state = [[jnp.zeros_like(lam)] * 2 for _ in range(2)]
        for step in range(16):
            mp, mlo, n = step // 4, (step // 2) % 2, step % 2
            at_row = base + (mp * 2 + n) * size
            for ri in range(2):
                at = (mlo * 2 + ri) * 128
                re, im = state[ri]
                state[ri] = [
                    rate_cos * re - rate_sin * im + spectra[at_row : at_row + size, at : at + 128],
                    rate_cos * im + rate_sin * re,
                ]
                fields[at_row : at_row + size, at : at + 128] = kernel * state[ri][0]
    back = dot_right(fields[...], bi)
    first_row = iota((16, 128), 0) == 0
    for mp in range(4):
        rows = []
        for n in range(2):
            for dx in range(2):
                for ri in range(2):
                    at = (dx * 2 + ri) * 128
                    at_row = (mp * 2 + n) * 16
                    piece = back[at_row : at_row + 16, at : at + 128]
                    if ri == 1:
                        added = back[128 + mp * 2 + n : 129 + mp * 2 + n, at - 128 : at]
                        piece = piece + jnp.where(first_row, added, 0.0)
                    rows.append(piece)
        out[mp * 128 : (mp + 1) * 128, :] = jnp.concatenate(rows, axis=0).T


def field_kernel(recv, cells, gz, gy, cs, out, values, left):
    pencils = []
    for t in range(4):
        halves_y = [
            jnp.concatenate(
                [
                    recv[(4 * low + q) * 64 : (4 * low + q + 1) * 64, :][:, t * 32 : (t + 1) * 32]
                    for q in range(4)
                ],
                axis=1,
            )
            for low in range(2)
        ]
        pencils.append(jnp.concatenate(halves_y, axis=0))
    both = dot_right(jnp.concatenate(pencils, axis=0), gz)
    tops, bottoms = [], []
    for t in range(4):
        real = pencils[t][:, 0:1]
        imag = pencils[t][:, 16:17]
        tops.append(both[t * 128 : (t + 1) * 128, :128] + (real * cs[0] + imag * cs[1]))
        bottoms.append(both[t * 128 : (t + 1) * 128, 128:] + imag * cs[2])
    tall = jnp.concatenate(
        [jnp.concatenate(tops, axis=1), jnp.concatenate(bottoms, axis=1)], axis=0
    )
    field = dot_left(gy, tall)
    first, second = split(
        jnp.concatenate([field[:, t * 128 : (t + 1) * 128] for t in range(4)], axis=0)
    )
    left[:, :128] = first
    left[:, 128:] = second
    row = iota((128, 128), 0)

    def read(pair, carry):
        cell = cells[pl.ds(pair, 1), :]
        cell_y = cell // 128
        cell_z = cell % 128
        hot = jnp.concatenate(
            [one_hot(row == (cell_z + (dz - 1)) % 128) for dz in range(3)], axis=1
        )
        lines = dot(left[...], jnp.concatenate([hot, hot], axis=0))
        hits = [row == (cell_y + (dy - 1)) % 128 for dy in range(3)]
        rows = []
        for step in range(2):
            for dx in range(2):
                t = 2 * step + dx
                for dy in range(3):
                    for dz in range(3):
                        line = lines[t * 128 : (t + 1) * 128, dz * 128 : (dz + 1) * 128]
                        rows.append(
                            jnp.sum(jnp.where(hits[dy], line, 0.0), axis=0, keepdims=True)
                        )
            rows.append(jnp.zeros((KROWS - STEN, 128), F32))
        values[pair] = jnp.concatenate(rows, axis=0)
        return carry

    lax.fori_loop(0, 8, read, 0)
    blocks = []
    for j in range(16):
        blocks.append(values[j // 2][:, (j % 2) * 64 : (j % 2 + 1) * 64])
    write_owner_rows(jnp.concatenate(blocks, axis=0), out)


CHUNK = 1024


def potential_kernel(recv, where, weight, out, turned, left):
    read_owner_rows(recv, turned)
    for high in range(4):
        block = jnp.concatenate(
            [turned[(4 * low + high) * ROWS : (4 * low + high + 1) * ROWS, :] for low in range(4)],
            axis=1,
        )
        first, second = split(block)
        left[high * ROWS : (high + 1) * ROWS, :] = first
        left[(4 + high) * ROWS : (5 + high) * ROWS, :] = second
    pages = CHUNK // 128

    def read(chunk, carry):
        at = pl.multiple_of(chunk * CHUNK, CHUNK)
        low = jnp.concatenate(
            [where[pl.ds(chunk * pages + i, 1), :] for i in range(pages)], axis=1
        )
        high = jnp.concatenate(
            [where[pl.ds(64 + chunk * pages + i, 1), :] for i in range(pages)], axis=1
        )
        lines = dot(left[...], one_hot(iota((256, CHUNK), 0) == low))
        lines = lines[: 4 * ROWS] + lines[4 * ROWS :]
        picked = lines[:ROWS]
        for quarter in range(1, 4):
            picked = jnp.where(
                high == quarter, lines[quarter * ROWS : (quarter + 1) * ROWS], picked
            )
        tile = weight[:, pl.ds(at, CHUNK)]
        tile = jnp.concatenate([tile, jnp.zeros((KROWS - STEN, CHUNK), F32)], axis=0)
        for step in range(2):
            out[step : step + 1, pl.ds(at, CHUNK)] = jnp.sum(
                picked[step * KROWS : (step + 1) * KROWS] * tile, axis=0, keepdims=True
            )
        return carry

    lax.fori_loop(0, PDEV // CHUNK, read, 0)


PARAMS = pltpu.CompilerParams(vmem_limit_bytes=48 * 1024 * 1024)


def f32(*shape):
    return jax.ShapeDtypeStruct(shape, F32)


def i32(*shape):
    return jax.ShapeDtypeStruct(shape, jnp.int32)


def run_panels(source, weight, slots, count, cell):
    return pl.pallas_call(
        panels_kernel,
        out_shape=(f32(64 * WIDTH, 128), i32(128, 128)),
        scratch_shapes=[
            pltpu.VMEM((256, PDEV), BF16),
            pltpu.VMEM((8 * ROWS, PDEV), BF16),
        ],
        compiler_params=PARAMS,
        name="panels",
    )(source, weight, slots, count, cell)


def run_slab(recv, fz, fy):
    return pl.pallas_call(
        slab_kernel,
        out_shape=(f32(512, 128), i32(8, 128)),
        scratch_shapes=[
            pltpu.VMEM((16 * ROWS, 64), F32),
            pltpu.VMEM((8, ROWS, 128), F32),
            pltpu.VMEM((512, 3 * BOXES), BF16),
            pltpu.VMEM((512, 3 * BOXES), BF16),
            pltpu.VMEM((3 * BOXES, 128), BF16),
        ],
        compiler_params=PARAMS,
        name="slab",
    )(recv, fz, fy)


def run_column(place, recv, decay, bd, bi, lz, lx):
    return pl.pallas_call(
        column_kernel,
        out_shape=f32(512, 128),
        in_specs=[pl.BlockSpec(memory_space=pltpu.SMEM)]
        + [pl.BlockSpec(memory_space=pltpu.VMEM)] * 6,
        scratch_shapes=[
            pltpu.VMEM((128, 128), F32),
            pltpu.VMEM((136, 512), F32),
            pltpu.VMEM((136, 512), F32),
        ],
        compiler_params=PARAMS,
        name="column",
    )(place, recv, decay, bd, bi, lz, lx)


def run_field(recv, cells, gz, gy, cs):
    return pl.pallas_call(
        field_kernel,
        out_shape=f32(64 * WIDTH, 128),
        scratch_shapes=[pltpu.VMEM((8, ROWS, 128), F32), pltpu.VMEM((512, 256), BF16)],
        compiler_params=PARAMS,
        name="field",
    )(recv, cells, gz, gy, cs)


def run_potential(recv, where, weight):
    return pl.pallas_call(
        potential_kernel,
        out_shape=f32(2, PDEV),
        scratch_shapes=[pltpu.VMEM((16 * ROWS, 64), F32), pltpu.VMEM((8 * ROWS, 256), BF16)],
        compiler_params=PARAMS,
        name="potential",
    )(recv, where, weight)


def exchange(rows, parts, axes):
    pieces = rows.reshape(parts, 1, rows.size // parts)
    pieces = lax.all_to_all(pieces, axes, split_axis=0, concat_axis=0, tiled=True)
    return pieces.reshape(rows.shape)


def body(panel_source, proj_weight, box_slots, box_count, box_cell, decay):
    table = {name: jnp.asarray(value) for name, value in tables().items()}
    place = jnp.stack([lax.axis_index("tm"), lax.axis_index("grid")]).astype(jnp.int32)
    out, where = run_panels(
        panel_source, proj_weight, box_slots, box_count.reshape(1, -1), box_cell.reshape(1, -1)
    )
    recv = exchange(out, 64, "grid")
    out, cells = run_slab(recv, table["fz"], table["fy"])
    recv = exchange(out, 512, ("tm", "grid"))
    out = run_column(
        place, recv, decay.reshape(2 * N, N), table["bd"], table["bi"], table["lz"], table["lx"]
    )
    recv = exchange(out, 512, ("tm", "grid"))
    out = run_field(recv, cells, table["gz"], table["gy"], table["cs"])
    recv = exchange(out, 64, "grid")
    return run_potential(recv, where, proj_weight)


def solution(mesh):
    return jax.shard_map(
        body,
        mesh=mesh,
        in_specs=(
            P("tm", "grid"),
            P(None, "grid"),
            P(None, "grid"),
            P("grid"),
            P("grid"),
            P(None, "grid", None),
        ),
        out_specs=P("tm", "grid"),
        check_vma=False,
    )
```

```python
import jax
import jax.numpy as jnp
import ml_dtypes
import numpy as np
from jax import lax
from jax.experimental import pallas as pl
from jax.experimental.pallas import tpu as pltpu
from jax.sharding import PartitionSpec as P

N = 128
STEN = 18
KROWS = 24
CELL_ROW = 18
ROWS = 2 * KROWS
WIDTH = 16 * ROWS // 128
PDEV = 8192
BOXES = 1024
F32 = jnp.float32
BF16 = jnp.bfloat16


def halves(table):
    table = np.asarray(table, np.float64).astype(np.float32)
    high = table.astype(ml_dtypes.bfloat16)
    low = (table - high.astype(np.float32)).astype(ml_dtypes.bfloat16)
    return np.stack([high, low])


def angle(rows, cols):
    return 2.0 * np.pi * (np.outer(rows, cols) % N) / N


def tables():
    index = np.arange(N)
    slot = (index // 32) * 16 + index % 16
    imag = (index // 16) % 2 == 1
    ang = angle(index, slot)
    real_z = np.cos(ang)
    imag_z = np.where(slot[None] == 0, np.cos(np.pi * index)[:, None], -np.sin(ang))
    fz = np.concatenate(
        [np.where(imag[None], imag_z, real_z), np.where(imag[None], -real_z, imag_z)], axis=1
    )
    ky = np.concatenate([2 * np.arange(64), 2 * np.arange(64) + 1])
    ay = angle(ky, index)
    fy = np.stack([np.cos(ay), np.sin(ay)])

    grid = np.arange(64)
    fx = np.zeros((2, 2, 64, 2, N))
    gx = np.zeros((2, N, 2, 2, 64))
    for dx in range(2):
        ax = angle(2 * grid + dx, index)
        cos, sin = np.cos(ax), np.sin(ax)
        fx[0, dx, :, 0] = cos
        fx[0, dx, :, 1] = -sin
        fx[1, dx, :, 0] = sin
        fx[1, dx, :, 1] = cos
        gx[0, :, 0, dx] = cos.T / N
        gx[0, :, 1, dx] = sin.T / N
        gx[1, :, 0, dx] = -sin.T / N
        gx[1, :, 1, dx] = cos.T / N
    fx = fx.reshape(256, 256)
    gx = gx.reshape(256, 256)

    weight = np.where(slot == 0, 0.0, 2.0)[:, None] / N
    cz = np.cos(ang.T) * weight
    sz = np.sin(ang.T) * weight
    gz = np.concatenate(
        [np.where(imag[:, None], -sz, cz), np.where(imag[:, None], -cz, -sz)], axis=1
    )
    gy = np.concatenate([np.cos(ay.T), np.sin(ay.T)], axis=1) / N
    self_row = (ky == 0) | (ky == 64)
    pattern = np.where((ky <= 64)[:, None], 1.0, np.cos(np.pi * index)[None])
    c1 = np.where(self_row, 1.0, 2.0)[:, None] * pattern / N
    c2 = np.where(self_row[:, None], np.cos(np.pi * index)[None], 0.0) / N
    c3 = np.where(self_row[:, None], 0.0, -2.0 * pattern) / N
    cs = np.stack([c1, c2, c3]).astype(np.float32)

    lam = 4.0 * np.sin(np.pi * index / N) ** 2
    lz = np.broadcast_to(lam[:, None], (N, N)).astype(np.float32)
    lx = np.broadcast_to(lam[None], (8, N)).astype(np.float32)
    return dict(
        fz=halves(fz), fy=halves(fy), fx=halves(fx), gx=halves(gx), gz=halves(gz), gy=halves(gy),
        cs=cs, lz=lz, lx=lx,
    )


def split(values):
    high = values.astype(BF16)
    return high, (values - high.astype(F32)).astype(BF16)


def dot(left, right):
    return lax.dot_general(left, right, (((1,), (0,)), ((), ())), preferred_element_type=F32)


def dot_nt(left, right):
    return lax.dot_general(left, right, (((1,), (1,)), ((), ())), preferred_element_type=F32)


def dot_right(values, table):
    high, low = split(values)
    return dot(high, table[0]) + (dot(low, table[0]) + dot(high, table[1]))


def dot_left(table, values):
    high, low = split(values)
    return dot(table[0], high) + (dot(table[0], low) + dot(table[1], high))


def iota(shape, axis):
    return lax.broadcasted_iota(jnp.int32, shape, axis)


def rows_bf16(shape, axis):
    return iota(shape, axis).astype(F32).astype(BF16)


def wide(row, size):
    sixteen = jnp.broadcast_to(row.astype(F32), (16, row.shape[1])).astype(BF16)
    return jnp.concatenate([sixteen] * (size // 16), axis=0)


def one_hot(mask):
    return jnp.where(mask, jnp.ones((), BF16), jnp.zeros((), BF16))


def write_owner_rows(turned, out_ref):
    for part in range(WIDTH):
        out_ref[pl.ds(part, 64, stride=WIDTH), :] = turned[part * 128 : (part + 1) * 128, :].T


def read_owner_rows(in_ref, turned_ref):
    for part in range(WIDTH):
        turned_ref[part * 128 : (part + 1) * 128, :] = in_ref[pl.ds(part, 64, stride=WIDTH), :].T


def panels_kernel(
    source_hbm, weight_hbm, slots_hbm, count_hbm, cell_hbm, out, where,
    source, weight, slots, count, cell, oh_ref, left_ref, sems,
):
    pairs = (
        (slots_hbm, slots), (count_hbm, count), (cell_hbm, cell), (weight_hbm, weight),
        (source_hbm, source),
    )
    copies = [pltpu.make_async_copy(a, b, sems.at[i]) for i, (a, b) in enumerate(pairs)]
    for copy in copies:
        copy.start()
    copies[0].wait()
    copies[1].wait()
    box = iota((1, BOXES), 1)
    low_value = wide(((box >> 2) & 3) * 64 + (box >> 4), 64)
    high_value = wide(box & 3, 64)
    row64 = rows_bf16((64, BOXES), 0)
    row128 = rows_bf16((128, BOXES), 0)
    none = jnp.zeros((), BF16)

    def invert(s, total):
        panel = slots[pl.ds(s, 1), :]
        page = jnp.where(s < count[...], panel >> 7, 200)
        hit = row64 == wide(page, 64)
        left = jnp.concatenate(
            [jnp.where(hit, low_value, none), jnp.where(hit, high_value, none)], axis=0
        )
        return total + dot_nt(left, one_hot(row128 == wide(panel & 127, 128)))

    total = lax.fori_loop(0, 16, invert, jnp.zeros((128, 128), F32))
    where_now = (total + 0.5).astype(jnp.int32)
    where[...] = where_now
    copies[3].wait()
    copies[4].wait()
    row256 = rows_bf16((256, 128), 0)

    def spread(page, carry):
        at = pl.multiple_of(page * 128, 128)
        low = wide(where[pl.ds(page, 1), :], 256)
        high = wide(where[pl.ds(64 + page, 1), :], ROWS)
        oh_ref[:, pl.ds(at, 128)] = one_hot(row256 == low)
        tile = weight[:, pl.ds(at, 128)]
        tile = jnp.concatenate([tile, jnp.zeros((KROWS - STEN, 128), F32)], axis=0)
        both = jnp.concatenate(
            [tile * source[0:1, pl.ds(at, 128)], tile * source[1:2, pl.ds(at, 128)]], axis=0
        )
        pieces = split(both)
        for quarter in range(4):
            hit = high == jnp.full((), quarter, BF16)
            for part, piece in enumerate(pieces):
                at_row = (part * 4 + quarter) * ROWS
                left_ref[at_row : at_row + ROWS, pl.ds(at, 128)] = jnp.where(hit, piece, none)
        return carry

    lax.fori_loop(0, 64, spread, 0)
    sums = dot_nt(left_ref[...], oh_ref[...])
    sums = sums[: 4 * ROWS] + sums[4 * ROWS :]

    copies[2].wait()
    cells = cell[...]
    match = rows_bf16((16, BOXES), 0) == wide(box & 15, 16)
    left = jnp.concatenate(
        [
            jnp.where(match, wide(cells >> 7, 16), none),
            jnp.where(match, wide(cells & 127, 16), none),
        ],
        axis=0,
    )
    owned = dot_nt(left, one_hot(row64 == wide(box >> 4, 64)))
    cell_rows = owned[:16] * 128.0 + owned[16:]

    blocks = []
    at_cell = iota((ROWS, 64), 0) == CELL_ROW
    for j in range(16):
        block = sums[(j % 4) * ROWS : (j % 4 + 1) * ROWS, (j // 4) * 64 : (j // 4 + 1) * 64]
        blocks.append(jnp.where(at_cell, cell_rows[j : j + 1, :], block))
    write_owner_rows(jnp.concatenate(blocks, axis=0), out)


def slab_kernel(recv, fz_hbm, fy_hbm, out, cell_out, fz, fy, turned, values, left_h, left_l, right, sems):
    copies = [
        pltpu.make_async_copy(fz_hbm, fz, sems.at[0]),
        pltpu.make_async_copy(fy_hbm, fy, sems.at[1]),
    ]
    for copy in copies:
        copy.start()
    read_owner_rows(recv, turned)
    lane = iota((128, 128), 1)
    row = iota((128, 128), 0)
    lane_b = rows_bf16((128, 128), 1)
    row_b = rows_bf16((128, 128), 0)
    for pair in range(8):
        value = jnp.concatenate(
            [
                turned[(2 * pair) * ROWS : (2 * pair + 1) * ROWS, :],
                turned[(2 * pair + 1) * ROWS : (2 * pair + 2) * ROWS, :],
            ],
            axis=1,
        )
        values[pair] = value
        cell_out[pair : pair + 1, :] = value[CELL_ROW : CELL_ROW + 1, :].astype(jnp.int32)
        column = []
        for j in (2 * pair, 2 * pair + 1):
            at = j * ROWS + CELL_ROW
            tile = recv[pl.ds(at // 128, 64, stride=WIDTH), :]
            column.append(jnp.broadcast_to(tile[:, at % 128 : at % 128 + 1], (64, 128)))
        column = jnp.concatenate(column, axis=0).astype(jnp.int32)
        for dz in range(3):
            at = (pair * 3 + dz) * 128
            right[at : at + 128, :] = jnp.where(
                lane == ((column + (dz - 1)) & 127), 1.0, 0.0
            ).astype(BF16)

    def fill(pair, carry):
        cell_y = cell_out[pl.ds(pair, 1), :] >> 7
        value = values[pair]
        hits = [row_b == wide((cell_y + (dy - 1)) & 127, 128) for dy in range(3)]
        pieces = split(value)
        none = jnp.zeros((128, 128), BF16)
        for dz in range(3):
            at = pl.multiple_of((pair * 3 + dz) * 128, 128)
            for step in range(2):
                for dx in range(2):
                    at_row = (2 * step + dx) * 128
                    for target, piece in ((left_h, pieces[0]), (left_l, pieces[1])):
                        block = none
                        for dy in range(3):
                            k = step * KROWS + 9 * dx + 3 * dy + dz
                            block = jnp.where(
                                hits[dy], wide(piece[k : k + 1, :].astype(F32), 128), block
                            )
                        target[at_row : at_row + 128, pl.ds(at, 128)] = block
        return carry

    lax.fori_loop(0, 8, fill, 0)
    density = dot(left_h[...], right[...]) + dot(left_l[...], right[...])
    for copy in copies:
        copy.wait()
    both = dot_right(density, fz)

    def beside(at):
        return jnp.concatenate(
            [both[t * 128 : (t + 1) * 128, at : at + 128] for t in range(4)], axis=1
        )

    even = dot_left((fy[0, 0], fy[1, 0]), beside(0))
    odd = dot_left((fy[0, 1], fy[1, 1]), beside(128))
    ky = (row % 64) * 2 + row // 64
    own = (ky == 0) | (ky == 64)
    pencils = []
    for t in range(4):
        a = even[:, t * 128 : (t + 1) * 128]
        b = odd[:, t * 128 : (t + 1) * 128]
        full = a + b
        full = jnp.where(lane == 0, jnp.where(ky <= 64, a, pltpu.roll(a, 112, 1)), full)
        second = jnp.where(own, a, jnp.where(ky < 64, b, -pltpu.roll(b, 16, 1)))
        pencils.append(jnp.where(lane == 16, second, full))
    for q in range(4):
        piece = jnp.concatenate([p[:, q * 32 : (q + 1) * 32] for p in pencils], axis=1)
        out[q * 64 : (q + 1) * 64, :] = piece[:64]
        out[(4 + q) * 64 : (5 + q) * 64, :] = piece[64:]


def column_kernel(place, recv, decay, fx, gx, lz, lx, out, turned_decay, spectra, fields):
    block = place[0]
    column = place[1]
    ky_low = block // 4
    q = block % 4
    ky = 2 * column + ky_low
    special = ((block == 0) & ((column == 0) | (column == 32))).astype(jnp.int32)
    below = iota((16, 128), 1) < 64
    first_row = iota((16, 128), 0) == 0
    mains, extras = [], []
    for mp in range(4):
        part = recv[mp * 128 : (mp + 1) * 128, :].T
        for half in range(2):
            for n in range(2):
                pieces = []
                for ri in range(2):
                    near = part[(2 * n) * 32 + ri * 16 : (2 * n) * 32 + ri * 16 + 16, :]
                    far = part[(2 * n + 1) * 32 + ri * 16 : (2 * n + 1) * 32 + ri * 16 + 16, :]
                    if half == 0:
                        far = pltpu.roll(far, 64, 1)
                    else:
                        near = pltpu.roll(near, 64, 1)
                    pieces.append(jnp.where(below, near, far))
                extras.append(jnp.where(special == 1, pieces[1][0:1], 0.0))
                pieces[1] = jnp.where(first_row & (special == 1), 0.0, pieces[1])
                mains.append(jnp.concatenate(pieces, axis=1))
    extra = jnp.concatenate(extras, axis=0)
    mains.append(jnp.concatenate([extra, jnp.zeros_like(extra)], axis=1))
    spectra[...] = dot_right(jnp.concatenate(mains, axis=0), fx)

    here = jnp.where(
        ky_low == 1, decay[pl.ds(1, 128, stride=2), :], decay[pl.ds(0, 128, stride=2), :]
    )
    turned_decay[...] = here.T
    slots_at = pl.multiple_of(q * 16, 16)
    moved = jnp.where((q == 0) & (ky > 64), 1, 0)
    at_first = iota((16, 128), 0) + (1 - moved) == 0
    damp_last = turned_decay[64:65, :]
    damp_main = jnp.where(at_first, damp_last, turned_decay[pl.ds(slots_at, 16), :])
    lam_xy = lx[0:1, :] + lz[pl.ds(ky, 1), :]
    lam_main = lam_xy + jnp.where(at_first, lz[64:65, :], lz[pl.ds(slots_at, 16), :])
    lam_last = lam_xy + lz[64:65, :]

    for damp, lam, base, size in ((damp_main, lam_main, 0, 16), (damp_last, lam_last, 256, 1)):
        theta = 0.5 * jnp.sqrt(lam)
        rate_cos = damp * jnp.cos(theta)
        rate_sin = damp * jnp.sin(theta)
        kernel = 1.0 / (1.0 + lam)
        state = [[jnp.zeros_like(lam)] * 2 for _ in range(2)]
        for step in range(16):
            at_row = base + step * size
            for ri in range(2):
                at = ri * 128
                re, im = state[ri]
                state[ri] = [
                    rate_cos * re - rate_sin * im + spectra[at_row : at_row + size, at : at + 128],
                    rate_cos * im + rate_sin * re,
                ]
                fields[at_row : at_row + size, at : at + 128] = kernel * state[ri][0]
    back = dot_right(fields[...], gx)
    for mp in range(4):
        rows = []
        for n in range(2):
            steps = [4 * mp + 2 * half + n for half in range(2)]
            pieces = []
            for ri in range(2):
                both = []
                for step in steps:
                    piece = back[step * 16 : step * 16 + 16, ri * 128 : ri * 128 + 128]
                    if ri == 1:
                        added = back[256 + step : 257 + step, 0:128]
                        piece = piece + jnp.where(first_row, added, 0.0)
                    both.append(piece)
                pieces.append(
                    (
                        jnp.where(below, both[0], pltpu.roll(both[1], 64, 1)),
                        jnp.where(below, pltpu.roll(both[0], 64, 1), both[1]),
                    )
                )
            for dx in range(2):
                for ri in range(2):
                    rows.append(pieces[ri][dx])
        out[mp * 128 : (mp + 1) * 128, :] = jnp.concatenate(rows, axis=0).T


def field_kernel(recv, cells, gz, gy, cs, out, values, left):
    pencils = []
    for t in range(4):
        halves_y = [
            jnp.concatenate(
                [
                    recv[(4 * low + q) * 64 : (4 * low + q + 1) * 64, :][:, t * 32 : (t + 1) * 32]
                    for q in range(4)
                ],
                axis=1,
            )
            for low in range(2)
        ]
        pencils.append(jnp.concatenate(halves_y, axis=0))
    both = dot_right(jnp.concatenate(pencils, axis=0), gz)
    tops, bottoms = [], []
    for t in range(4):
        real = pencils[t][:, 0:1]
        imag = pencils[t][:, 16:17]
        tops.append(both[t * 128 : (t + 1) * 128, :128] + (real * cs[0] + imag * cs[1]))
        bottoms.append(both[t * 128 : (t + 1) * 128, 128:] + imag * cs[2])
    tall = jnp.concatenate(
        [jnp.concatenate(tops, axis=1), jnp.concatenate(bottoms, axis=1)], axis=0
    )
    field = dot_left(gy, tall)
    first, second = split(
        jnp.concatenate([field[:, t * 128 : (t + 1) * 128] for t in range(4)], axis=0)
    )
    left[:, :128] = first
    left[:, 128:] = second
    row = iota((128, 128), 0)
    row_b = rows_bf16((128, 128), 0)

    def read(pair, carry):
        cell = cells[pl.ds(pair, 1), :]
        cell_y = cell >> 7
        cell_z = cell & 127
        hot = jnp.concatenate(
            [one_hot(row_b == wide((cell_z + (dz - 1)) & 127, 128)) for dz in range(3)], axis=1
        )
        lines = dot(left[...], jnp.concatenate([hot, hot], axis=0))
        hits = [row == ((cell_y + (dy - 1)) & 127) for dy in range(3)]
        rows = []
        for step in range(2):
            for dx in range(2):
                t = 2 * step + dx
                for dy in range(3):
                    for dz in range(3):
                        line = lines[t * 128 : (t + 1) * 128, dz * 128 : (dz + 1) * 128]
                        rows.append(
                            jnp.sum(jnp.where(hits[dy], line, 0.0), axis=0, keepdims=True)
                        )
            rows.append(jnp.zeros((KROWS - STEN, 128), F32))
        values[pair] = jnp.concatenate(rows, axis=0)
        return carry

    lax.fori_loop(0, 8, read, 0)
    blocks = []
    for j in range(16):
        blocks.append(values[j // 2][:, (j % 2) * 64 : (j % 2 + 1) * 64])
    write_owner_rows(jnp.concatenate(blocks, axis=0), out)


CHUNK = 1024


def potential_kernel(recv, where, weight, out, turned, left):
    read_owner_rows(recv, turned)
    for high in range(4):
        block = jnp.concatenate(
            [turned[(4 * low + high) * ROWS : (4 * low + high + 1) * ROWS, :] for low in range(4)],
            axis=1,
        )
        first, second = split(block)
        left[high * ROWS : (high + 1) * ROWS, :] = first
        left[(4 + high) * ROWS : (5 + high) * ROWS, :] = second
    pages = CHUNK // 128
    row_b = rows_bf16((256, CHUNK), 0)

    def read(chunk, carry):
        at = pl.multiple_of(chunk * CHUNK, CHUNK)
        low = jnp.concatenate(
            [where[pl.ds(chunk * pages + i, 1), :] for i in range(pages)], axis=1
        )
        high = jnp.concatenate(
            [where[pl.ds(64 + chunk * pages + i, 1), :] for i in range(pages)], axis=1
        )
        lines = dot(left[...], one_hot(row_b == wide(low, 256)))
        lines = lines[: 4 * ROWS] + lines[4 * ROWS :]
        picked = lines[:ROWS]
        for quarter in range(1, 4):
            picked = jnp.where(
                high == quarter, lines[quarter * ROWS : (quarter + 1) * ROWS], picked
            )
        tile = weight[:, pl.ds(at, CHUNK)]
        tile = jnp.concatenate([tile, jnp.zeros((KROWS - STEN, CHUNK), F32)], axis=0)
        for step in range(2):
            out[step : step + 1, pl.ds(at, CHUNK)] = jnp.sum(
                picked[step * KROWS : (step + 1) * KROWS] * tile, axis=0, keepdims=True
            )
        return carry

    lax.fori_loop(0, PDEV // CHUNK, read, 0)


PARAMS = pltpu.CompilerParams(vmem_limit_bytes=48 * 1024 * 1024)


def f32(*shape):
    return jax.ShapeDtypeStruct(shape, F32)


def i32(*shape):
    return jax.ShapeDtypeStruct(shape, jnp.int32)


def run_panels(source, weight, slots, count, cell):
    return pl.pallas_call(
        panels_kernel,
        out_shape=(f32(64 * WIDTH, 128), i32(128, 128)),
        in_specs=[pl.BlockSpec(memory_space=pltpu.HBM)] * 5,
        scratch_shapes=[
            pltpu.VMEM((2, PDEV), F32),
            pltpu.VMEM((STEN, PDEV), F32),
            pltpu.VMEM((16, BOXES), jnp.int32),
            pltpu.VMEM((1, BOXES), jnp.int32),
            pltpu.VMEM((1, BOXES), jnp.int32),
            pltpu.VMEM((256, PDEV), BF16),
            pltpu.VMEM((8 * ROWS, PDEV), BF16),
            pltpu.SemaphoreType.DMA((5,)),
        ],
        compiler_params=PARAMS,
        name="panels",
    )(source, weight, slots, count, cell)


def run_slab(recv, fz, fy):
    return pl.pallas_call(
        slab_kernel,
        out_shape=(f32(512, 128), i32(8, 128)),
        in_specs=[pl.BlockSpec(memory_space=pltpu.VMEM)]
        + [pl.BlockSpec(memory_space=pltpu.HBM)] * 2,
        scratch_shapes=[
            pltpu.VMEM((2, 128, 256), BF16),
            pltpu.VMEM((2, 2, 128, 128), BF16),
            pltpu.VMEM((16 * ROWS, 64), F32),
            pltpu.VMEM((8, ROWS, 128), F32),
            pltpu.VMEM((512, 3 * BOXES), BF16),
            pltpu.VMEM((512, 3 * BOXES), BF16),
            pltpu.VMEM((3 * BOXES, 128), BF16),
            pltpu.SemaphoreType.DMA((2,)),
        ],
        compiler_params=PARAMS,
        name="slab",
    )(recv, fz, fy)


def run_column(place, recv, decay, fx, gx, lz, lx):
    return pl.pallas_call(
        column_kernel,
        out_shape=f32(512, 128),
        in_specs=[pl.BlockSpec(memory_space=pltpu.SMEM)]
        + [pl.BlockSpec(memory_space=pltpu.VMEM)] * 6,
        scratch_shapes=[
            pltpu.VMEM((128, 128), F32),
            pltpu.VMEM((272, 256), F32),
            pltpu.VMEM((272, 256), F32),
        ],
        compiler_params=PARAMS,
        name="column",
    )(place, recv, decay, fx, gx, lz, lx)


def run_field(recv, cells, gz, gy, cs):
    return pl.pallas_call(
        field_kernel,
        out_shape=f32(64 * WIDTH, 128),
        scratch_shapes=[pltpu.VMEM((8, ROWS, 128), F32), pltpu.VMEM((512, 256), BF16)],
        compiler_params=PARAMS,
        name="field",
    )(recv, cells, gz, gy, cs)


def run_potential(recv, where, weight):
    return pl.pallas_call(
        potential_kernel,
        out_shape=f32(2, PDEV),
        scratch_shapes=[pltpu.VMEM((16 * ROWS, 64), F32), pltpu.VMEM((8 * ROWS, 256), BF16)],
        compiler_params=PARAMS,
        name="potential",
    )(recv, where, weight)


def exchange(rows, parts, axes):
    pieces = rows.reshape(parts, 1, rows.size // parts)
    pieces = lax.all_to_all(pieces, axes, split_axis=0, concat_axis=0, tiled=True)
    return pieces.reshape(rows.shape)


def body(panel_source, proj_weight, box_slots, box_count, box_cell, decay):
    table = {name: jnp.asarray(value) for name, value in tables().items()}
    place = jnp.stack([lax.axis_index("tm"), lax.axis_index("grid")]).astype(jnp.int32)
    out, where = run_panels(
        panel_source, proj_weight, box_slots, box_count.reshape(1, -1), box_cell.reshape(1, -1)
    )
    recv = exchange(out, 64, "grid")
    out, cells = run_slab(recv, table["fz"], table["fy"])
    recv = exchange(out, 512, ("tm", "grid"))
    out = run_column(
        place, recv, decay.reshape(2 * N, N), table["fx"], table["gx"], table["lz"], table["lx"]
    )
    recv = exchange(out, 512, ("tm", "grid"))
    out = run_field(recv, cells, table["gz"], table["gy"], table["cs"])
    recv = exchange(out, 64, "grid")
    return run_potential(recv, where, proj_weight)


def solution(mesh):
    return jax.shard_map(
        body,
        mesh=mesh,
        in_specs=(
            P("tm", "grid"),
            P(None, "grid"),
            P(None, "grid"),
            P("grid"),
            P("grid"),
            P(None, "grid", None),
        ),
        out_specs=P("tm", "grid"),
        check_vma=False,
    )
```

```python
import jax
import jax.numpy as jnp
import ml_dtypes
import numpy as np
from jax import lax
from jax.experimental import pallas as pl
from jax.experimental.pallas import tpu as pltpu
from jax.sharding import PartitionSpec as P

N = 128
STEN = 18
KROWS = 24
CELL_ROW = 18
ROWS = 2 * KROWS
WIDTH = 16 * ROWS // 128
PDEV = 8192
BOXES = 1024
F32 = jnp.float32
BF16 = jnp.bfloat16


def halves(table):
    table = np.asarray(table, np.float64).astype(np.float32)
    high = table.astype(ml_dtypes.bfloat16)
    low = (table - high.astype(np.float32)).astype(ml_dtypes.bfloat16)
    return np.stack([high, low])


def angle(rows, cols):
    return 2.0 * np.pi * (np.outer(rows, cols) % N) / N


def tables():
    index = np.arange(N)
    slot = (index // 32) * 16 + index % 16
    imag = (index // 16) % 2 == 1
    ang = angle(index, slot)
    real_z = np.cos(ang)
    imag_z = np.where(slot[None] == 0, np.cos(np.pi * index)[:, None], -np.sin(ang))
    fz = np.concatenate(
        [np.where(imag[None], imag_z, real_z), np.where(imag[None], -real_z, imag_z)], axis=1
    )
    ky = np.concatenate([2 * np.arange(64), 2 * np.arange(64) + 1])
    ay = angle(ky, index)
    fy = np.stack([np.cos(ay), np.sin(ay)])

    grid = np.arange(64)
    fx = np.zeros((2, 2, 64, 2, N))
    gx = np.zeros((2, N, 2, 2, 64))
    for dx in range(2):
        ax = angle(2 * grid + dx, index)
        cos, sin = np.cos(ax), np.sin(ax)
        fx[0, dx, :, 0] = cos
        fx[0, dx, :, 1] = -sin
        fx[1, dx, :, 0] = sin
        fx[1, dx, :, 1] = cos
        gx[0, :, 0, dx] = cos.T / N
        gx[0, :, 1, dx] = sin.T / N
        gx[1, :, 0, dx] = -sin.T / N
        gx[1, :, 1, dx] = cos.T / N
    fx = fx.reshape(256, 256)
    gx = gx.reshape(256, 256)

    weight = np.where(slot == 0, 0.0, 2.0)[:, None] / N
    cz = np.cos(ang.T) * weight
    sz = np.sin(ang.T) * weight
    gz = np.concatenate(
        [np.where(imag[:, None], -sz, cz), np.where(imag[:, None], -cz, -sz)], axis=1
    )
    gy = np.concatenate([np.cos(ay.T), np.sin(ay.T)], axis=1) / N
    self_row = (ky == 0) | (ky == 64)
    pattern = np.where((ky <= 64)[:, None], 1.0, np.cos(np.pi * index)[None])
    c1 = np.where(self_row, 1.0, 2.0)[:, None] * pattern / N
    c2 = np.where(self_row[:, None], np.cos(np.pi * index)[None], 0.0) / N
    c3 = np.where(self_row[:, None], 0.0, -2.0 * pattern) / N
    cs = np.stack([c1, c2, c3]).astype(np.float32)

    lam = 4.0 * np.sin(np.pi * index / N) ** 2
    lz = np.broadcast_to(lam[:, None], (N, N)).astype(np.float32)
    lx = np.broadcast_to(lam[None], (8, N)).astype(np.float32)
    return dict(
        fz=halves(fz), fy=halves(fy), fx=halves(fx), gx=halves(gx), gz=halves(gz), gy=halves(gy),
        cs=cs, lz=lz, lx=lx,
    )


def split(values):
    high = values.astype(BF16)
    return high, (values - high.astype(F32)).astype(BF16)


def dot(left, right):
    return lax.dot_general(left, right, (((1,), (0,)), ((), ())), preferred_element_type=F32)


def dot_nt(left, right):
    return lax.dot_general(left, right, (((1,), (1,)), ((), ())), preferred_element_type=F32)


def dot_right(values, table):
    high, low = split(values)
    return dot(high, table[0]) + (dot(low, table[0]) + dot(high, table[1]))


def dot_left(table, values):
    high, low = split(values)
    return dot(table[0], high) + (dot(table[0], low) + dot(table[1], high))


def iota(shape, axis):
    return lax.broadcasted_iota(jnp.int32, shape, axis)


def rows_bf16(shape, axis):
    return iota(shape, axis).astype(F32).astype(BF16)


def wide(row, size):
    sixteen = jnp.broadcast_to(row.astype(F32), (16, row.shape[1])).astype(BF16)
    return jnp.concatenate([sixteen] * (size // 16), axis=0)


def one_hot(mask):
    return jnp.where(mask, jnp.ones((), BF16), jnp.zeros((), BF16))


def write_owner_rows(turned, out_ref):
    for part in range(WIDTH):
        out_ref[pl.ds(part, 64, stride=WIDTH), :] = turned[part * 128 : (part + 1) * 128, :].T


def read_owner_rows(in_ref, turned_ref):
    for part in range(WIDTH):
        turned_ref[part * 128 : (part + 1) * 128, :] = in_ref[pl.ds(part, 64, stride=WIDTH), :].T


def panels_kernel(
    source_hbm, weight_hbm, slots_hbm, count_hbm, cell_hbm, out, where,
    source, weight, slots, count, cell, oh_ref, left_ref, sems,
):
    pairs = (
        (slots_hbm, slots), (count_hbm, count), (cell_hbm, cell), (weight_hbm, weight),
        (source_hbm, source),
    )
    copies = [pltpu.make_async_copy(a, b, sems.at[i]) for i, (a, b) in enumerate(pairs)]
    for copy in copies:
        copy.start()
    copies[0].wait()
    copies[1].wait()
    box = iota((1, BOXES), 1)
    low_value = wide(((box >> 2) & 3) * 64 + (box >> 4), 64)
    high_value = wide(box & 3, 64)
    row64 = rows_bf16((64, BOXES), 0)
    row128 = rows_bf16((128, BOXES), 0)
    none = jnp.zeros((), BF16)

    def invert(s, total):
        panel = slots[pl.ds(s, 1), :]
        page = jnp.where(s < count[...], panel >> 7, 200)
        hit = row64 == wide(page, 64)
        left = jnp.concatenate(
            [jnp.where(hit, low_value, none), jnp.where(hit, high_value, none)], axis=0
        )
        return total + dot_nt(left, one_hot(row128 == wide(panel & 127, 128)))

    total = lax.fori_loop(0, 16, invert, jnp.zeros((128, 128), F32), unroll=True)
    where_now = (total + 0.5).astype(jnp.int32)
    where[...] = where_now
    copies[3].wait()
    copies[4].wait()
    row256 = rows_bf16((256, 128), 0)

    def spread(page):
        at = page * 128
        low = wide(where_now[page : page + 1, :], 256)
        high = wide(where_now[64 + page : 65 + page, :], ROWS)
        oh_ref[:, pl.ds(at, 128)] = one_hot(row256 == low)
        tile = weight[:, pl.ds(at, 128)]
        tile = jnp.concatenate([tile, jnp.zeros((KROWS - STEN, 128), F32)], axis=0)
        both = jnp.concatenate(
            [tile * source[0:1, pl.ds(at, 128)], tile * source[1:2, pl.ds(at, 128)]], axis=0
        )
        pieces = split(both)
        for quarter in range(4):
            hit = high == jnp.full((), quarter, BF16)
            for part, piece in enumerate(pieces):
                at_row = (part * 4 + quarter) * ROWS
                left_ref[at_row : at_row + ROWS, pl.ds(at, 128)] = jnp.where(hit, piece, none)

    sums = jnp.zeros((8 * ROWS, 256), F32)
    for chunk in range(8):
        for page in range(8):
            spread(chunk * 8 + page)
        at = slice(chunk * 1024, chunk * 1024 + 1024)
        sums = sums + dot_nt(left_ref[:, at], oh_ref[:, at])
    sums = sums[: 4 * ROWS] + sums[4 * ROWS :]

    copies[2].wait()
    cells = cell[...]
    match = rows_bf16((16, BOXES), 0) == wide(box & 15, 16)
    left = jnp.concatenate(
        [
            jnp.where(match, wide(cells >> 7, 16), none),
            jnp.where(match, wide(cells & 127, 16), none),
        ],
        axis=0,
    )
    owned = dot_nt(left, one_hot(row64 == wide(box >> 4, 64)))
    cell_rows = owned[:16] * 128.0 + owned[16:]

    blocks = []
    at_cell = iota((ROWS, 64), 0) == CELL_ROW
    for j in range(16):
        block = sums[(j % 4) * ROWS : (j % 4 + 1) * ROWS, (j // 4) * 64 : (j // 4 + 1) * 64]
        blocks.append(jnp.where(at_cell, cell_rows[j : j + 1, :], block))
    write_owner_rows(jnp.concatenate(blocks, axis=0), out)


def slab_kernel(recv, fz_hbm, fy_hbm, out, cell_out, fz, fy, turned, values, left_h, left_l, right, sems):
    copies = [
        pltpu.make_async_copy(fz_hbm, fz, sems.at[0]),
        pltpu.make_async_copy(fy_hbm, fy, sems.at[1]),
    ]
    for copy in copies:
        copy.start()
    read_owner_rows(recv, turned)
    lane = iota((128, 128), 1)
    row = iota((128, 128), 0)
    lane_b = rows_bf16((128, 128), 1)
    row_b = rows_bf16((128, 128), 0)
    for pair in range(8):
        value = jnp.concatenate(
            [
                turned[(2 * pair) * ROWS : (2 * pair + 1) * ROWS, :],
                turned[(2 * pair + 1) * ROWS : (2 * pair + 2) * ROWS, :],
            ],
            axis=1,
        )
        values[pair] = value
        cell_out[pair : pair + 1, :] = value[CELL_ROW : CELL_ROW + 1, :].astype(jnp.int32)
        column = []
        for j in (2 * pair, 2 * pair + 1):
            at = j * ROWS + CELL_ROW
            tile = recv[pl.ds(at // 128, 64, stride=WIDTH), :]
            column.append(jnp.broadcast_to(tile[:, at % 128 : at % 128 + 1], (64, 128)))
        column = jnp.concatenate(column, axis=0).astype(jnp.int32)
        for dz in range(3):
            at = (pair * 3 + dz) * 128
            right[at : at + 128, :] = jnp.where(
                lane == ((column + (dz - 1)) & 127), 1.0, 0.0
            ).astype(BF16)

    def fill(pair):
        cell_y = cell_out[pair : pair + 1, :] >> 7
        value = values[pair]
        hits = [row_b == wide((cell_y + (dy - 1)) & 127, 128) for dy in range(3)]
        pieces = split(value)
        none = jnp.zeros((128, 128), BF16)
        for dz in range(3):
            at = (pair * 3 + dz) * 128
            for step in range(2):
                for dx in range(2):
                    at_row = (2 * step + dx) * 128
                    for target, piece in ((left_h, pieces[0]), (left_l, pieces[1])):
                        block = none
                        for dy in range(3):
                            k = step * KROWS + 9 * dx + 3 * dy + dz
                            block = jnp.where(
                                hits[dy], wide(piece[k : k + 1, :].astype(F32), 128), block
                            )
                        target[at_row : at_row + 128, pl.ds(at, 128)] = block

    density = jnp.zeros((512, 128), F32)
    for quarter in range(4):
        fill(2 * quarter)
        fill(2 * quarter + 1)
        at = slice(quarter * 768, quarter * 768 + 768)
        density = density + (dot(left_h[:, at], right[at, :]) + dot(left_l[:, at], right[at, :]))
    for copy in copies:
        copy.wait()
    both = dot_right(density, fz)

    def beside(at):
        return jnp.concatenate(
            [both[t * 128 : (t + 1) * 128, at : at + 128] for t in range(4)], axis=1
        )

    even = dot_left((fy[0, 0], fy[1, 0]), beside(0))
    odd = dot_left((fy[0, 1], fy[1, 1]), beside(128))
    ky = (row % 64) * 2 + row // 64
    own = (ky == 0) | (ky == 64)
    pencils = []
    for t in range(4):
        a = even[:, t * 128 : (t + 1) * 128]
        b = odd[:, t * 128 : (t + 1) * 128]
        full = a + b
        full = jnp.where(lane == 0, jnp.where(ky <= 64, a, pltpu.roll(a, 112, 1)), full)
        second = jnp.where(own, a, jnp.where(ky < 64, b, -pltpu.roll(b, 16, 1)))
        pencils.append(jnp.where(lane == 16, second, full))
    for q in range(4):
        piece = jnp.concatenate([p[:, q * 32 : (q + 1) * 32] for p in pencils], axis=1)
        out[q * 64 : (q + 1) * 64, :] = piece[:64]
        out[(4 + q) * 64 : (5 + q) * 64, :] = piece[64:]


def column_kernel(place, recv, decay, fx, gx, lz, lx, out, turned_decay, spectra, fields):
    block = place[0]
    column = place[1]
    ky_low = block // 4
    q = block % 4
    ky = 2 * column + ky_low
    special = ((block == 0) & ((column == 0) | (column == 32))).astype(jnp.int32)
    below = iota((16, 128), 1) < 64
    first_row = iota((16, 128), 0) == 0
    mains, extras = [], []
    for mp in range(4):
        part = recv[mp * 128 : (mp + 1) * 128, :].T
        for half in range(2):
            for n in range(2):
                pieces = []
                for ri in range(2):
                    near = part[(2 * n) * 32 + ri * 16 : (2 * n) * 32 + ri * 16 + 16, :]
                    far = part[(2 * n + 1) * 32 + ri * 16 : (2 * n + 1) * 32 + ri * 16 + 16, :]
                    if half == 0:
                        far = pltpu.roll(far, 64, 1)
                    else:
                        near = pltpu.roll(near, 64, 1)
                    pieces.append(jnp.where(below, near, far))
                extras.append(jnp.where(special == 1, pieces[1][0:1], 0.0))
                pieces[1] = jnp.where(first_row & (special == 1), 0.0, pieces[1])
                mains.append(jnp.concatenate(pieces, axis=1))
    extra = jnp.concatenate(extras, axis=0)
    mains.append(jnp.concatenate([extra, jnp.zeros_like(extra)], axis=1))
    spectra[...] = dot_right(jnp.concatenate(mains, axis=0), fx)

    here = jnp.where(
        ky_low == 1, decay[pl.ds(1, 128, stride=2), :], decay[pl.ds(0, 128, stride=2), :]
    )
    turned_decay[...] = here.T
    slots_at = pl.multiple_of(q * 16, 16)
    moved = jnp.where((q == 0) & (ky > 64), 1, 0)
    at_first = iota((16, 128), 0) + (1 - moved) == 0
    damp_last = turned_decay[64:65, :]
    damp_main = jnp.where(at_first, damp_last, turned_decay[pl.ds(slots_at, 16), :])
    lam_xy = lx[0:1, :] + lz[pl.ds(ky, 1), :]
    lam_main = lam_xy + jnp.where(at_first, lz[64:65, :], lz[pl.ds(slots_at, 16), :])
    lam_last = lam_xy + lz[64:65, :]

    for damp, lam, base, size in ((damp_main, lam_main, 0, 16), (damp_last, lam_last, 256, 1)):
        theta = 0.5 * jnp.sqrt(lam)
        rate_cos = damp * jnp.cos(theta)
        rate_sin = damp * jnp.sin(theta)
        kernel = 1.0 / (1.0 + lam)
        state = [[jnp.zeros_like(lam)] * 2 for _ in range(2)]
        for step in range(16):
            at_row = base + step * size
            for ri in range(2):
                at = ri * 128
                re, im = state[ri]
                state[ri] = [
                    rate_cos * re - rate_sin * im + spectra[at_row : at_row + size, at : at + 128],
                    rate_cos * im + rate_sin * re,
                ]
                fields[at_row : at_row + size, at : at + 128] = kernel * state[ri][0]
    back = dot_right(fields[...], gx)
    for mp in range(4):
        rows = []
        for n in range(2):
            steps = [4 * mp + 2 * half + n for half in range(2)]
            pieces = []
            for ri in range(2):
                both = []
                for step in steps:
                    piece = back[step * 16 : step * 16 + 16, ri * 128 : ri * 128 + 128]
                    if ri == 1:
                        added = back[256 + step : 257 + step, 0:128]
                        piece = piece + jnp.where(first_row, added, 0.0)
                    both.append(piece)
                pieces.append(
                    (
                        jnp.where(below, both[0], pltpu.roll(both[1], 64, 1)),
                        jnp.where(below, pltpu.roll(both[0], 64, 1), both[1]),
                    )
                )
            for dx in range(2):
                for ri in range(2):
                    rows.append(pieces[ri][dx])
        out[mp * 128 : (mp + 1) * 128, :] = jnp.concatenate(rows, axis=0).T


def field_kernel(recv, cells, gz, gy, cs, out, values, left):
    pencils = []
    for t in range(4):
        halves_y = [
            jnp.concatenate(
                [
                    recv[(4 * low + q) * 64 : (4 * low + q + 1) * 64, :][:, t * 32 : (t + 1) * 32]
                    for q in range(4)
                ],
                axis=1,
            )
            for low in range(2)
        ]
        pencils.append(jnp.concatenate(halves_y, axis=0))
    both = dot_right(jnp.concatenate(pencils, axis=0), gz)
    tops, bottoms = [], []
    for t in range(4):
        real = pencils[t][:, 0:1]
        imag = pencils[t][:, 16:17]
        tops.append(both[t * 128 : (t + 1) * 128, :128] + (real * cs[0] + imag * cs[1]))
        bottoms.append(both[t * 128 : (t + 1) * 128, 128:] + imag * cs[2])
    tall = jnp.concatenate(
        [jnp.concatenate(tops, axis=1), jnp.concatenate(bottoms, axis=1)], axis=0
    )
    field = dot_left(gy, tall)
    first, second = split(
        jnp.concatenate([field[:, t * 128 : (t + 1) * 128] for t in range(4)], axis=0)
    )
    left[:, :128] = first
    left[:, 128:] = second
    row = iota((128, 128), 0)
    row_b = rows_bf16((128, 128), 0)

    def read(pair, carry):
        cell = cells[pl.ds(pair, 1), :]
        cell_y = cell >> 7
        cell_z = cell & 127
        hot = jnp.concatenate(
            [one_hot(row_b == wide((cell_z + (dz - 1)) & 127, 128)) for dz in range(3)], axis=1
        )
        lines = dot(left[...], jnp.concatenate([hot, hot], axis=0))
        hits = [row == ((cell_y + (dy - 1)) & 127) for dy in range(3)]
        rows = []
        for step in range(2):
            for dx in range(2):
                t = 2 * step + dx
                for dy in range(3):
                    for dz in range(3):
                        line = lines[t * 128 : (t + 1) * 128, dz * 128 : (dz + 1) * 128]
                        rows.append(
                            jnp.sum(jnp.where(hits[dy], line, 0.0), axis=0, keepdims=True)
                        )
            rows.append(jnp.zeros((KROWS - STEN, 128), F32))
        values[pair] = jnp.concatenate(rows, axis=0)
        return carry

    lax.fori_loop(0, 8, read, 0, unroll=True)
    blocks = []
    for j in range(16):
        blocks.append(values[j // 2][:, (j % 2) * 64 : (j % 2 + 1) * 64])
    write_owner_rows(jnp.concatenate(blocks, axis=0), out)


CHUNK = 1024


def potential_kernel(recv, where, weight, out, turned, left):
    read_owner_rows(recv, turned)
    for high in range(4):
        block = jnp.concatenate(
            [turned[(4 * low + high) * ROWS : (4 * low + high + 1) * ROWS, :] for low in range(4)],
            axis=1,
        )
        first, second = split(block)
        left[high * ROWS : (high + 1) * ROWS, :] = first
        left[(4 + high) * ROWS : (5 + high) * ROWS, :] = second
    pages = CHUNK // 128
    row_b = rows_bf16((256, CHUNK), 0)

    def read(chunk, carry):
        at = pl.multiple_of(chunk * CHUNK, CHUNK)
        low = jnp.concatenate(
            [where[pl.ds(chunk * pages + i, 1), :] for i in range(pages)], axis=1
        )
        high = jnp.concatenate(
            [where[pl.ds(64 + chunk * pages + i, 1), :] for i in range(pages)], axis=1
        )
        lines = dot(left[...], one_hot(row_b == wide(low, 256)))
        lines = lines[: 4 * ROWS] + lines[4 * ROWS :]
        picked = lines[:ROWS]
        for quarter in range(1, 4):
            picked = jnp.where(
                high == quarter, lines[quarter * ROWS : (quarter + 1) * ROWS], picked
            )
        tile = weight[:, pl.ds(at, CHUNK)]
        tile = jnp.concatenate([tile, jnp.zeros((KROWS - STEN, CHUNK), F32)], axis=0)
        for step in range(2):
            out[step : step + 1, pl.ds(at, CHUNK)] = jnp.sum(
                picked[step * KROWS : (step + 1) * KROWS] * tile, axis=0, keepdims=True
            )
        return carry

    lax.fori_loop(0, PDEV // CHUNK, read, 0, unroll=True)


PARAMS = pltpu.CompilerParams(vmem_limit_bytes=48 * 1024 * 1024)


def f32(*shape):
    return jax.ShapeDtypeStruct(shape, F32)


def i32(*shape):
    return jax.ShapeDtypeStruct(shape, jnp.int32)


def run_panels(source, weight, slots, count, cell):
    return pl.pallas_call(
        panels_kernel,
        out_shape=(f32(64 * WIDTH, 128), i32(128, 128)),
        in_specs=[pl.BlockSpec(memory_space=pltpu.HBM)] * 5,
        scratch_shapes=[
            pltpu.VMEM((2, PDEV), F32),
            pltpu.VMEM((STEN, PDEV), F32),
            pltpu.VMEM((16, BOXES), jnp.int32),
            pltpu.VMEM((1, BOXES), jnp.int32),
            pltpu.VMEM((1, BOXES), jnp.int32),
            pltpu.VMEM((256, PDEV), BF16),
            pltpu.VMEM((8 * ROWS, PDEV), BF16),
            pltpu.SemaphoreType.DMA((5,)),
        ],
        compiler_params=PARAMS,
        name="panels",
    )(*(pltpu.with_memory_space_constraint(x, pltpu.HBM) for x in (source, weight, slots, count, cell)))


def run_slab(recv, fz, fy):
    return pl.pallas_call(
        slab_kernel,
        out_shape=(f32(512, 128), i32(8, 128)),
        in_specs=[pl.BlockSpec(memory_space=pltpu.VMEM)]
        + [pl.BlockSpec(memory_space=pltpu.HBM)] * 2,
        scratch_shapes=[
            pltpu.VMEM((2, 128, 256), BF16),
            pltpu.VMEM((2, 2, 128, 128), BF16),
            pltpu.VMEM((16 * ROWS, 64), F32),
            pltpu.VMEM((8, ROWS, 128), F32),
            pltpu.VMEM((512, 3 * BOXES), BF16),
            pltpu.VMEM((512, 3 * BOXES), BF16),
            pltpu.VMEM((3 * BOXES, 128), BF16),
            pltpu.SemaphoreType.DMA((2,)),
        ],
        compiler_params=PARAMS,
        name="slab",
    )(recv, fz, fy)


def run_column(place, recv, decay, fx, gx, lz, lx):
    return pl.pallas_call(
        column_kernel,
        out_shape=f32(512, 128),
        in_specs=[pl.BlockSpec(memory_space=pltpu.SMEM)]
        + [pl.BlockSpec(memory_space=pltpu.VMEM)] * 6,
        scratch_shapes=[
            pltpu.VMEM((128, 128), F32),
            pltpu.VMEM((272, 256), F32),
            pltpu.VMEM((272, 256), F32),
        ],
        compiler_params=PARAMS,
        name="column",
    )(place, recv, decay, fx, gx, lz, lx)


def run_field(recv, cells, gz, gy, cs):
    return pl.pallas_call(
        field_kernel,
        out_shape=f32(64 * WIDTH, 128),
        scratch_shapes=[pltpu.VMEM((8, ROWS, 128), F32), pltpu.VMEM((512, 256), BF16)],
        compiler_params=PARAMS,
        name="field",
    )(recv, cells, gz, gy, cs)


def run_potential(recv, where, weight):
    return pl.pallas_call(
        potential_kernel,
        out_shape=f32(2, PDEV),
        scratch_shapes=[pltpu.VMEM((16 * ROWS, 64), F32), pltpu.VMEM((8 * ROWS, 256), BF16)],
        compiler_params=PARAMS,
        name="potential",
    )(recv, where, weight)


def exchange(rows, parts, axes):
    pieces = rows.reshape(parts, 1, rows.size // parts)
    pieces = lax.all_to_all(pieces, axes, split_axis=0, concat_axis=0, tiled=True)
    return pieces.reshape(rows.shape)


def body(panel_source, proj_weight, box_slots, box_count, box_cell, decay):
    table = {name: jnp.asarray(value) for name, value in tables().items()}
    place = jnp.stack([lax.axis_index("tm"), lax.axis_index("grid")]).astype(jnp.int32)
    out, where = run_panels(
        panel_source, proj_weight, box_slots, box_count.reshape(1, -1), box_cell.reshape(1, -1)
    )
    recv = exchange(out, 64, "grid")
    out, cells = run_slab(recv, table["fz"], table["fy"])
    recv = exchange(out, 512, ("tm", "grid"))
    out = run_column(
        place, recv, decay.reshape(2 * N, N), table["fx"], table["gx"], table["lz"], table["lx"]
    )
    recv = exchange(out, 512, ("tm", "grid"))
    out = run_field(recv, cells, table["gz"], table["gy"], table["cs"])
    recv = exchange(out, 64, "grid")
    return run_potential(recv, where, proj_weight)


def solution(mesh):
    return jax.shard_map(
        body,
        mesh=mesh,
        in_specs=(
            P("tm", "grid"),
            P(None, "grid"),
            P(None, "grid"),
            P("grid"),
            P("grid"),
            P(None, "grid", None),
        ),
        out_specs=P("tm", "grid"),
        check_vma=False,
    )
```

```python
import jax
import jax.numpy as jnp
import ml_dtypes
import numpy as np
from jax import lax
from jax.experimental import pallas as pl
from jax.experimental.pallas import tpu as pltpu
from jax.sharding import PartitionSpec as P

N = 128
STEN = 18
KROWS = 20
CELL_ROW = 18
ROWS = 2 * KROWS
WIDTH = 16 * ROWS // 128
PDEV = 8192
BOXES = 1024
F32 = jnp.float32
BF16 = jnp.bfloat16


def stacked(table, axis):
    table = np.asarray(table, np.float64).astype(np.float32)
    high = table.astype(ml_dtypes.bfloat16)
    low = (table - high.astype(np.float32)).astype(ml_dtypes.bfloat16)
    return np.concatenate([high, high, low], axis=axis)


def angle(rows, cols):
    return 2.0 * np.pi * (np.outer(rows, cols) % N) / N


def tables():
    index = np.arange(N)
    slot = (index // 32) * 16 + index % 16
    imag = (index // 16) % 2 == 1
    ang = angle(index, slot)
    real_z = np.cos(ang)
    imag_z = np.where(slot[None] == 0, np.cos(np.pi * index)[:, None], -np.sin(ang))
    fz = np.concatenate(
        [np.where(imag[None], imag_z, real_z), np.where(imag[None], -real_z, imag_z)], axis=1
    )
    ky = np.concatenate([2 * np.arange(64), 2 * np.arange(64) + 1])
    ay = angle(ky, index)
    fy = np.stack([np.cos(ay), np.sin(ay)])

    grid = np.arange(64)
    fx = np.zeros((2, 2, 64, 2, N))
    gx = np.zeros((2, N, 2, 2, 64))
    for dx in range(2):
        ax = angle(2 * grid + dx, index)
        cos, sin = np.cos(ax), np.sin(ax)
        fx[0, dx, :, 0] = cos
        fx[0, dx, :, 1] = -sin
        fx[1, dx, :, 0] = sin
        fx[1, dx, :, 1] = cos
        gx[0, :, 0, dx] = cos.T / N
        gx[0, :, 1, dx] = sin.T / N
        gx[1, :, 0, dx] = -sin.T / N
        gx[1, :, 1, dx] = cos.T / N
    fx = fx.reshape(256, 256)
    gx = gx.reshape(256, 256)

    weight = np.where(slot == 0, 0.0, 2.0)[:, None] / N
    cz = np.cos(ang.T) * weight
    sz = np.sin(ang.T) * weight
    gz = np.concatenate(
        [np.where(imag[:, None], -sz, cz), np.where(imag[:, None], -cz, -sz)], axis=1
    )
    gy = np.concatenate([np.cos(ay.T), np.sin(ay.T)], axis=1) / N
    self_row = (ky == 0) | (ky == 64)
    pattern = np.where((ky <= 64)[:, None], 1.0, np.cos(np.pi * index)[None])
    c1 = np.where(self_row, 1.0, 2.0)[:, None] * pattern / N
    c2 = np.where(self_row[:, None], np.cos(np.pi * index)[None], 0.0) / N
    c3 = np.where(self_row[:, None], 0.0, -2.0 * pattern) / N
    cs = np.stack([c1, c2, c3]).astype(np.float32)

    lam = 4.0 * np.sin(np.pi * index / N) ** 2
    lz = np.broadcast_to(lam[:, None], (N, N)).astype(np.float32)
    lx = np.broadcast_to(lam[None], (8, N)).astype(np.float32)
    return dict(
        fz=stacked(fz, 0), fy=stacked(fy, 2), fx=stacked(fx, 0), gx=stacked(gx, 0),
        gz=stacked(gz, 0), gy=stacked(gy, 1),
        cs=cs, lz=lz, lx=lx,
    )


def split(values):
    high = values.astype(BF16)
    return high, (values - high.astype(F32)).astype(BF16)


def halves(values):
    high = values.astype(BF16).astype(F32)
    return jnp.concatenate([high, values - high], axis=0).astype(BF16)


def doubled(tile):
    tile = jnp.concatenate([tile, jnp.zeros((KROWS - STEN, tile.shape[1]), F32)], axis=0)
    return jnp.concatenate([tile, tile], axis=0)


def dot(left, right):
    return lax.dot_general(left, right, (((1,), (0,)), ((), ())), preferred_element_type=F32)


def dot_nt(left, right):
    return lax.dot_general(left, right, (((1,), (1,)), ((), ())), preferred_element_type=F32)


def dot_right(values, table):
    high, low = split(values)
    return dot(jnp.concatenate([high, low, high], axis=1), table[...])


def dot_left(table, values):
    high, low = split(values)
    return dot(table, jnp.concatenate([high, low, high], axis=0))


def iota(shape, axis):
    return lax.broadcasted_iota(jnp.int32, shape, axis)


def rows_bf16(shape, axis):
    return iota(shape, axis).astype(F32).astype(BF16)


def wide(row, size):
    sixteen = jnp.broadcast_to(row.astype(F32), (16, row.shape[1])).astype(BF16)
    return jnp.concatenate([sixteen] * (size // 16), axis=0)


def one_hot(mask):
    return jnp.where(mask, jnp.ones((), BF16), jnp.zeros((), BF16))


def write_owner_rows(turned, out_ref):
    for part in range(WIDTH):
        out_ref[pl.ds(part, 64, stride=WIDTH), :] = turned[part * 128 : (part + 1) * 128, :].T


def read_owner_rows(in_ref, turned_ref):
    for part in range(WIDTH):
        turned_ref[part * 128 : (part + 1) * 128, :] = in_ref[pl.ds(part, 64, stride=WIDTH), :].T


def panels_kernel(
    source_hbm, weight_hbm, slots_hbm, count_hbm, cell_hbm, out, where,
    source, weight, slots, count, cell, oh_ref, left_ref, sems,
):
    pairs = (
        (slots_hbm, slots), (count_hbm, count), (cell_hbm, cell), (weight_hbm, weight),
        (source_hbm, source),
    )
    copies = [pltpu.make_async_copy(a, b, sems.at[i]) for i, (a, b) in enumerate(pairs)]
    for copy in copies:
        copy.start()
    copies[0].wait()
    copies[1].wait()
    box = iota((1, BOXES), 1)
    low_value = wide(((box >> 2) & 3) * 64 + (box >> 4), 64)
    high_value = wide(box & 3, 64)
    row64 = rows_bf16((64, BOXES), 0)
    row128 = rows_bf16((128, BOXES), 0)
    none = jnp.zeros((), BF16)

    def invert(s, total):
        panel = slots[pl.ds(s, 1), :]
        page = jnp.where(s < count[...], panel >> 7, 200)
        hit = row64 == wide(page, 64)
        left = jnp.concatenate(
            [jnp.where(hit, low_value, none), jnp.where(hit, high_value, none)], axis=0
        )
        return total + dot_nt(left, one_hot(row128 == wide(panel & 127, 128)))

    total = lax.fori_loop(0, 16, invert, jnp.zeros((128, 128), F32), unroll=True)
    where_now = (total + 0.5).astype(jnp.int32)
    where[...] = where_now
    copies[3].wait()
    copies[4].wait()
    row256 = rows_bf16((256, 128), 0)
    first_step = iota((ROWS, 128), 0) < KROWS

    def spread(page):
        at = page * 128
        low = wide(where_now[page : page + 1, :], 256)
        high = wide(where_now[64 + page : 65 + page, :], 2 * ROWS)
        oh_ref[:, pl.ds(at, 128)] = one_hot(row256 == low)
        both = doubled(weight[:, at : at + 128]) * jnp.where(
            first_step, source[0:1, at : at + 128], source[1:2, at : at + 128]
        )
        pieces = halves(both)
        for quarter in range(4):
            left_ref[quarter * 2 * ROWS : (quarter + 1) * 2 * ROWS, at : at + 128] = jnp.where(
                high == jnp.full((), quarter, BF16), pieces, none
            )

    sums = jnp.zeros((8 * ROWS, 256), F32)
    for chunk in range(8):
        for page in range(8):
            spread(chunk * 8 + page)
        at = slice(chunk * 1024, chunk * 1024 + 1024)
        sums = sums + dot_nt(left_ref[:, at], oh_ref[:, at])

    copies[2].wait()
    cells = cell[...]
    match = rows_bf16((16, BOXES), 0) == wide(box & 15, 16)
    left = jnp.concatenate(
        [
            jnp.where(match, wide(cells >> 7, 16), none),
            jnp.where(match, wide(cells & 127, 16), none),
        ],
        axis=0,
    )
    owned = dot_nt(left, one_hot(row64 == wide(box >> 4, 64)))
    cell_rows = owned[:16] * 128.0 + owned[16:]

    blocks = []
    at_cell = iota((ROWS, 64), 0) == CELL_ROW
    for j in range(16):
        at = (j % 4) * 2 * ROWS
        block = sums[at : at + 2 * ROWS, (j // 4) * 64 : (j // 4 + 1) * 64]
        block = block[:ROWS] + block[ROWS:]
        blocks.append(jnp.where(at_cell, cell_rows[j : j + 1, :], block))
    write_owner_rows(jnp.concatenate(blocks, axis=0), out)


def slab_kernel(recv, fz_hbm, fy_hbm, out, cell_out, fz, fy, turned, values, left_h, left_l, right, sems):
    copies = [
        pltpu.make_async_copy(fz_hbm, fz, sems.at[0]),
        pltpu.make_async_copy(fy_hbm, fy, sems.at[1]),
    ]
    for copy in copies:
        copy.start()
    read_owner_rows(recv, turned)
    lane = iota((128, 128), 1)
    row = iota((128, 128), 0)
    lane_b = rows_bf16((128, 128), 1)
    row_b = rows_bf16((128, 128), 0)
    for pair in range(8):
        value = jnp.concatenate(
            [
                turned[(2 * pair) * ROWS : (2 * pair + 1) * ROWS, :],
                turned[(2 * pair + 1) * ROWS : (2 * pair + 2) * ROWS, :],
            ],
            axis=1,
        )
        high = value.astype(BF16).astype(F32)
        values[0, pair] = high
        values[1, pair] = value - high
        cell_out[pair : pair + 1, :] = value[CELL_ROW : CELL_ROW + 1, :].astype(jnp.int32)
        column = []
        for j in (2 * pair, 2 * pair + 1):
            at = j * ROWS + CELL_ROW
            tile = recv[pl.ds(at // 128, 64, stride=WIDTH), :]
            column.append(jnp.broadcast_to(tile[:, at % 128 : at % 128 + 1], (64, 128)))
        column = jnp.concatenate(column, axis=0).astype(jnp.int32)
        for dz in range(3):
            at = (pair * 3 + dz) * 128
            right[at : at + 128, :] = jnp.where(
                lane == ((column + (dz - 1)) & 127), 1.0, 0.0
            ).astype(BF16)

    def fill(pair):
        cell_y = cell_out[pair : pair + 1, :] >> 7
        hits = [row_b == wide((cell_y + (dy - 1)) & 127, 128) for dy in range(3)]
        none = jnp.zeros((128, 128), BF16)
        for dz in range(3):
            at = (pair * 3 + dz) * 128
            for step in range(2):
                for dx in range(2):
                    at_row = (2 * step + dx) * 128
                    for part, target in ((0, left_h), (1, left_l)):
                        block = none
                        for dy in range(3):
                            k = step * KROWS + 9 * dx + 3 * dy + dz
                            block = jnp.where(
                                hits[dy], wide(values[part, pair, k : k + 1, :], 128), block
                            )
                        target[at_row : at_row + 128, pl.ds(at, 128)] = block

    density = jnp.zeros((512, 128), F32)
    for quarter in range(4):
        fill(2 * quarter)
        fill(2 * quarter + 1)
        at = slice(quarter * 768, quarter * 768 + 768)
        density = density + (dot(left_h[:, at], right[at, :]) + dot(left_l[:, at], right[at, :]))
    for copy in copies:
        copy.wait()
    both = dot_right(density, fz)

    def beside(at):
        return jnp.concatenate(
            [both[t * 128 : (t + 1) * 128, at : at + 128] for t in range(4)], axis=1
        )

    even = dot_left(fy[0], beside(0))
    odd = dot_left(fy[1], beside(128))
    ky = (row % 64) * 2 + row // 64
    own = (ky == 0) | (ky == 64)
    pencils = []
    for t in range(4):
        a = even[:, t * 128 : (t + 1) * 128]
        b = odd[:, t * 128 : (t + 1) * 128]
        full = a + b
        full = jnp.where(lane == 0, jnp.where(ky <= 64, a, pltpu.roll(a, 112, 1)), full)
        second = jnp.where(own, a, jnp.where(ky < 64, b, -pltpu.roll(b, 16, 1)))
        pencils.append(jnp.where(lane == 16, second, full))
    for q in range(4):
        piece = jnp.concatenate([p[:, q * 32 : (q + 1) * 32] for p in pencils], axis=1)
        out[q * 64 : (q + 1) * 64, :] = piece[:64]
        out[(4 + q) * 64 : (5 + q) * 64, :] = piece[64:]


def column_kernel(place, recv, decay, fx, gx, lz, lx, out, turned_decay, spectra, fields):
    block = place[0]
    column = place[1]
    ky_low = block // 4
    q = block % 4
    ky = 2 * column + ky_low
    special = ((block == 0) & ((column == 0) | (column == 32))).astype(jnp.int32)
    below = iota((16, 128), 1) < 64
    first_row = iota((16, 128), 0) == 0
    mains, extras = [], []
    for mp in range(4):
        part = recv[mp * 128 : (mp + 1) * 128, :].T
        for half in range(2):
            for n in range(2):
                pieces = []
                for ri in range(2):
                    near = part[(2 * n) * 32 + ri * 16 : (2 * n) * 32 + ri * 16 + 16, :]
                    far = part[(2 * n + 1) * 32 + ri * 16 : (2 * n + 1) * 32 + ri * 16 + 16, :]
                    if half == 0:
                        far = pltpu.roll(far, 64, 1)
                    else:
                        near = pltpu.roll(near, 64, 1)
                    pieces.append(jnp.where(below, near, far))
                extras.append(jnp.where(special == 1, pieces[1][0:1], 0.0))
                pieces[1] = jnp.where(first_row & (special == 1), 0.0, pieces[1])
                mains.append(jnp.concatenate(pieces, axis=1))
    extra = jnp.concatenate(extras, axis=0)
    mains.append(jnp.concatenate([extra, jnp.zeros_like(extra)], axis=1))
    spectra[...] = dot_right(jnp.concatenate(mains, axis=0), fx)

    here = jnp.where(
        ky_low == 1, decay[pl.ds(1, 128, stride=2), :], decay[pl.ds(0, 128, stride=2), :]
    )
    turned_decay[...] = here.T
    slots_at = pl.multiple_of(q * 16, 16)
    moved = jnp.where((q == 0) & (ky > 64), 1, 0)
    at_first = iota((16, 128), 0) + (1 - moved) == 0
    damp_last = turned_decay[64:65, :]
    damp_main = jnp.where(at_first, damp_last, turned_decay[pl.ds(slots_at, 16), :])
    lam_xy = lx[0:1, :] + lz[pl.ds(ky, 1), :]
    lam_main = lam_xy + jnp.where(at_first, lz[64:65, :], lz[pl.ds(slots_at, 16), :])
    lam_last = lam_xy + lz[64:65, :]

    for damp, lam, base, size in ((damp_main, lam_main, 0, 16), (damp_last, lam_last, 256, 1)):
        theta = 0.5 * jnp.sqrt(lam)
        rate_cos = damp * jnp.cos(theta)
        rate_sin = damp * jnp.sin(theta)
        kernel = 1.0 / (1.0 + lam)
        state = [[jnp.zeros_like(lam)] * 2 for _ in range(2)]
        for step in range(16):
            at_row = base + step * size
            for ri in range(2):
                at = ri * 128
                re, im = state[ri]
                state[ri] = [
                    rate_cos * re - rate_sin * im + spectra[at_row : at_row + size, at : at + 128],
                    rate_cos * im + rate_sin * re,
                ]
                fields[at_row : at_row + size, at : at + 128] = kernel * state[ri][0]
    back = dot_right(fields[...], gx)
    for mp in range(4):
        rows = []
        for n in range(2):
            steps = [4 * mp + 2 * half + n for half in range(2)]
            pieces = []
            for ri in range(2):
                both = []
                for step in steps:
                    piece = back[step * 16 : step * 16 + 16, ri * 128 : ri * 128 + 128]
                    if ri == 1:
                        added = back[256 + step : 257 + step, 0:128]
                        piece = piece + jnp.where(first_row, added, 0.0)
                    both.append(piece)
                pieces.append(
                    (
                        jnp.where(below, both[0], pltpu.roll(both[1], 64, 1)),
                        jnp.where(below, pltpu.roll(both[0], 64, 1), both[1]),
                    )
                )
            for dx in range(2):
                for ri in range(2):
                    rows.append(pieces[ri][dx])
        out[mp * 128 : (mp + 1) * 128, :] = jnp.concatenate(rows, axis=0).T


def field_kernel(recv, cells, gz, gy, cs, out, values, left):
    pencils = []
    for t in range(4):
        halves_y = [
            jnp.concatenate(
                [
                    recv[(4 * low + q) * 64 : (4 * low + q + 1) * 64, :][:, t * 32 : (t + 1) * 32]
                    for q in range(4)
                ],
                axis=1,
            )
            for low in range(2)
        ]
        pencils.append(jnp.concatenate(halves_y, axis=0))
    both = dot_right(jnp.concatenate(pencils, axis=0), gz)
    tops, bottoms = [], []
    for t in range(4):
        real = pencils[t][:, 0:1]
        imag = pencils[t][:, 16:17]
        tops.append(both[t * 128 : (t + 1) * 128, :128] + (real * cs[0] + imag * cs[1]))
        bottoms.append(both[t * 128 : (t + 1) * 128, 128:] + imag * cs[2])
    tall = jnp.concatenate(
        [jnp.concatenate(tops, axis=1), jnp.concatenate(bottoms, axis=1)], axis=0
    )
    field = dot_left(gy[...], tall)
    first, second = split(
        jnp.concatenate([field[:, t * 128 : (t + 1) * 128] for t in range(4)], axis=0)
    )
    left[:, :128] = first
    left[:, 128:] = second
    row = iota((128, 128), 0)
    row_b = rows_bf16((128, 128), 0)

    def read(pair, carry):
        cell = cells[pl.ds(pair, 1), :]
        cell_y = cell >> 7
        cell_z = cell & 127
        hot = jnp.concatenate(
            [one_hot(row_b == wide((cell_z + (dz - 1)) & 127, 128)) for dz in range(3)], axis=1
        )
        lines = dot(left[...], jnp.concatenate([hot, hot], axis=0))
        hits = [row == ((cell_y + (dy - 1)) & 127) for dy in range(3)]
        rows = []
        for step in range(2):
            for dx in range(2):
                t = 2 * step + dx
                for dy in range(3):
                    for dz in range(3):
                        line = lines[t * 128 : (t + 1) * 128, dz * 128 : (dz + 1) * 128]
                        rows.append(
                            jnp.sum(jnp.where(hits[dy], line, 0.0), axis=0, keepdims=True)
                        )
            rows.append(jnp.zeros((KROWS - STEN, 128), F32))
        values[pair] = jnp.concatenate(rows, axis=0)
        return carry

    lax.fori_loop(0, 8, read, 0, unroll=True)
    blocks = []
    for j in range(16):
        blocks.append(values[j // 2][:, (j % 2) * 64 : (j % 2 + 1) * 64])
    write_owner_rows(jnp.concatenate(blocks, axis=0), out)


CHUNK = 1024


def potential_kernel(recv, where, weight, out, turned, left):
    read_owner_rows(recv, turned)
    for high in range(4):
        block = jnp.concatenate(
            [turned[(4 * low + high) * ROWS : (4 * low + high + 1) * ROWS, :] for low in range(4)],
            axis=1,
        )
        left[high * 2 * ROWS : (high + 1) * 2 * ROWS, :] = halves(block)
    pages = CHUNK // 128
    row_b = rows_bf16((256, CHUNK), 0)

    def read(chunk, carry):
        at = pl.multiple_of(chunk * CHUNK, CHUNK)
        low = jnp.concatenate(
            [where[pl.ds(chunk * pages + i, 1), :] for i in range(pages)], axis=1
        )
        high = jnp.concatenate(
            [where[pl.ds(64 + chunk * pages + i, 1), :] for i in range(pages)], axis=1
        )
        lines = dot(left[...], one_hot(row_b == wide(low, 256)))
        picked = lines[: 2 * ROWS]
        for quarter in range(1, 4):
            at_row = quarter * 2 * ROWS
            picked = jnp.where(high == quarter, lines[at_row : at_row + 2 * ROWS], picked)
        terms = (picked[:ROWS] + picked[ROWS:]) * doubled(weight[:, pl.ds(at, CHUNK)])
        for step in range(2):
            out[step : step + 1, pl.ds(at, CHUNK)] = jnp.sum(
                terms[step * KROWS : (step + 1) * KROWS], axis=0, keepdims=True
            )
        return carry

    lax.fori_loop(0, PDEV // CHUNK, read, 0, unroll=True)


PARAMS = pltpu.CompilerParams(vmem_limit_bytes=48 * 1024 * 1024)


def f32(*shape):
    return jax.ShapeDtypeStruct(shape, F32)


def i32(*shape):
    return jax.ShapeDtypeStruct(shape, jnp.int32)


def run_panels(source, weight, slots, count, cell):
    return pl.pallas_call(
        panels_kernel,
        out_shape=(f32(64 * WIDTH, 128), i32(128, 128)),
        in_specs=[pl.BlockSpec(memory_space=pltpu.HBM)] * 5,
        scratch_shapes=[
            pltpu.VMEM((2, PDEV), F32),
            pltpu.VMEM((STEN, PDEV), F32),
            pltpu.VMEM((16, BOXES), jnp.int32),
            pltpu.VMEM((1, BOXES), jnp.int32),
            pltpu.VMEM((1, BOXES), jnp.int32),
            pltpu.VMEM((256, PDEV), BF16),
            pltpu.VMEM((8 * ROWS, PDEV), BF16),
            pltpu.SemaphoreType.DMA((5,)),
        ],
        compiler_params=PARAMS,
        name="panels",
    )(*(pltpu.with_memory_space_constraint(x, pltpu.HBM) for x in (source, weight, slots, count, cell)))


def run_slab(recv, fz, fy):
    return pl.pallas_call(
        slab_kernel,
        out_shape=(f32(512, 128), i32(8, 128)),
        in_specs=[pl.BlockSpec(memory_space=pltpu.VMEM)]
        + [pl.BlockSpec(memory_space=pltpu.HBM)] * 2,
        scratch_shapes=[
            pltpu.VMEM((384, 256), BF16),
            pltpu.VMEM((2, 128, 384), BF16),
            pltpu.VMEM((16 * ROWS, 64), F32),
            pltpu.VMEM((2, 8, ROWS, 128), F32),
            pltpu.VMEM((512, 3 * BOXES), BF16),
            pltpu.VMEM((512, 3 * BOXES), BF16),
            pltpu.VMEM((3 * BOXES, 128), BF16),
            pltpu.SemaphoreType.DMA((2,)),
        ],
        compiler_params=PARAMS,
        name="slab",
    )(recv, fz, fy)


def run_column(place, recv, decay, fx, gx, lz, lx):
    return pl.pallas_call(
        column_kernel,
        out_shape=f32(512, 128),
        in_specs=[pl.BlockSpec(memory_space=pltpu.SMEM)]
        + [pl.BlockSpec(memory_space=pltpu.VMEM)] * 6,
        scratch_shapes=[
            pltpu.VMEM((128, 128), F32),
            pltpu.VMEM((272, 256), F32),
            pltpu.VMEM((272, 256), F32),
        ],
        compiler_params=PARAMS,
        name="column",
    )(place, recv, decay, fx, gx, lz, lx)


def run_field(recv, cells, gz, gy, cs):
    return pl.pallas_call(
        field_kernel,
        out_shape=f32(64 * WIDTH, 128),
        scratch_shapes=[pltpu.VMEM((8, ROWS, 128), F32), pltpu.VMEM((512, 256), BF16)],
        compiler_params=PARAMS,
        name="field",
    )(recv, cells, gz, gy, cs)


def run_potential(recv, where, weight):
    return pl.pallas_call(
        potential_kernel,
        out_shape=f32(2, PDEV),
        scratch_shapes=[pltpu.VMEM((16 * ROWS, 64), F32), pltpu.VMEM((8 * ROWS, 256), BF16)],
        compiler_params=PARAMS,
        name="potential",
    )(recv, where, weight)


def exchange(rows, parts, axes):
    pieces = rows.reshape(parts, 1, rows.size // parts)
    pieces = lax.all_to_all(pieces, axes, split_axis=0, concat_axis=0, tiled=True)
    return pieces.reshape(rows.shape)


def body(panel_source, proj_weight, box_slots, box_count, box_cell, decay):
    table = {name: jnp.asarray(value) for name, value in tables().items()}
    place = jnp.stack([lax.axis_index("tm"), lax.axis_index("grid")]).astype(jnp.int32)
    out, where = run_panels(
        panel_source, proj_weight, box_slots, box_count.reshape(1, -1), box_cell.reshape(1, -1)
    )
    recv = exchange(out, 64, "grid")
    out, cells = run_slab(recv, table["fz"], table["fy"])
    recv = exchange(out, 512, ("tm", "grid"))
    out = run_column(
        place, recv, decay.reshape(2 * N, N), table["fx"], table["gx"], table["lz"], table["lx"]
    )
    recv = exchange(out, 512, ("tm", "grid"))
    out = run_field(recv, cells, table["gz"], table["gy"], table["cs"])
    recv = exchange(out, 64, "grid")
    return run_potential(recv, where, proj_weight)


def solution(mesh):
    return jax.shard_map(
        body,
        mesh=mesh,
        in_specs=(
            P("tm", "grid"),
            P(None, "grid"),
            P(None, "grid"),
            P("grid"),
            P("grid"),
            P(None, "grid", None),
        ),
        out_specs=P("tm", "grid"),
        check_vma=False,
    )
```

```python
import jax
import jax.numpy as jnp
import ml_dtypes
import numpy as np
from jax import lax
from jax.experimental import pallas as pl
from jax.experimental.pallas import tpu as pltpu
from jax.sharding import PartitionSpec as P

N = 128
STEN = 18
KROWS = 20
CELL_ROW = 18
ROWS = 2 * KROWS
WIDTH = 16 * ROWS // 128
PDEV = 8192
BOXES = 1024
F32 = jnp.float32
BF16 = jnp.bfloat16


def stacked(table, axis):
    table = np.asarray(table, np.float64).astype(np.float32)
    high = table.astype(ml_dtypes.bfloat16)
    low = (table - high.astype(np.float32)).astype(ml_dtypes.bfloat16)
    return np.concatenate([high, high, low], axis=axis)


def angle(rows, cols):
    return 2.0 * np.pi * (np.outer(rows, cols) % N) / N


def tables():
    index = np.arange(N)
    slot = (index // 32) * 16 + index % 16
    imag = (index // 16) % 2 == 1
    ang = angle(index, slot)
    real_z = np.cos(ang)
    imag_z = np.where(slot[None] == 0, np.cos(np.pi * index)[:, None], -np.sin(ang))
    fz = np.concatenate(
        [np.where(imag[None], imag_z, real_z), np.where(imag[None], -real_z, imag_z)], axis=1
    )
    ky = np.concatenate([2 * np.arange(64), 2 * np.arange(64) + 1])
    ay = angle(ky, index)
    fy = np.stack([np.cos(ay), np.sin(ay)])

    grid = np.arange(64)
    fx = np.zeros((2, 2, 64, 2, N))
    gx = np.zeros((2, N, 2, 2, 64))
    for dx in range(2):
        ax = angle(2 * grid + dx, index)
        cos, sin = np.cos(ax), np.sin(ax)
        fx[0, dx, :, 0] = cos
        fx[0, dx, :, 1] = -sin
        fx[1, dx, :, 0] = sin
        fx[1, dx, :, 1] = cos
        gx[0, :, 0, dx] = cos.T / N
        gx[0, :, 1, dx] = sin.T / N
        gx[1, :, 0, dx] = -sin.T / N
        gx[1, :, 1, dx] = cos.T / N
    fx = fx.reshape(256, 256)
    gx = gx.reshape(256, 256)

    weight = np.where(slot == 0, 0.0, 2.0)[:, None] / N
    cz = np.cos(ang.T) * weight
    sz = np.sin(ang.T) * weight
    gz = np.concatenate(
        [np.where(imag[:, None], -sz, cz), np.where(imag[:, None], -cz, -sz)], axis=1
    )
    gy = np.concatenate([np.cos(ay.T), np.sin(ay.T)], axis=1) / N
    self_row = (ky == 0) | (ky == 64)
    pattern = np.where((ky <= 64)[:, None], 1.0, np.cos(np.pi * index)[None])
    c1 = np.where(self_row, 1.0, 2.0)[:, None] * pattern / N
    c2 = np.where(self_row[:, None], np.cos(np.pi * index)[None], 0.0) / N
    c3 = np.where(self_row[:, None], 0.0, -2.0 * pattern) / N
    cs = np.stack([c1, c2, c3]).astype(np.float32)

    lam = 4.0 * np.sin(np.pi * index / N) ** 2
    lz = np.broadcast_to(lam[:, None], (N, N)).astype(np.float32)
    lx = np.broadcast_to(lam[None], (8, N)).astype(np.float32)
    return dict(
        fz=stacked(fz, 0), fy=stacked(fy, 2), fx=stacked(fx, 0), gx=stacked(gx, 0),
        gz=stacked(gz, 0), gy=stacked(gy, 1),
        cs=cs, lz=lz, lx=lx,
    )


def split(values):
    high = values.astype(BF16)
    return high, (values - high.astype(F32)).astype(BF16)


def halves(values):
    high = values.astype(BF16).astype(F32)
    return jnp.concatenate([high, values - high], axis=0).astype(BF16)


def doubled(tile):
    tile = jnp.concatenate([tile, jnp.zeros((KROWS - STEN, tile.shape[1]), F32)], axis=0)
    return jnp.concatenate([tile, tile], axis=0)


def dot(left, right):
    return lax.dot_general(left, right, (((1,), (0,)), ((), ())), preferred_element_type=F32)


def dot_nt(left, right):
    return lax.dot_general(left, right, (((1,), (1,)), ((), ())), preferred_element_type=F32)


def dot_right(values, table):
    high, low = split(values)
    return dot(jnp.concatenate([high, low, high], axis=1), table[...])


def dot_left(table, values):
    high, low = split(values)
    return dot(table, jnp.concatenate([high, low, high], axis=0))


def iota(shape, axis):
    return lax.broadcasted_iota(jnp.int32, shape, axis)


def rows_bf16(shape, axis):
    return iota(shape, axis).astype(F32).astype(BF16)


def wide(row, size):
    sixteen = jnp.broadcast_to(row.astype(F32), (16, row.shape[1])).astype(BF16)
    return jnp.concatenate([sixteen] * (size // 16), axis=0)


def one_hot(mask):
    return jnp.where(mask, jnp.ones((), BF16), jnp.zeros((), BF16))


def write_owner_rows(turned, out_ref):
    for part in range(WIDTH):
        out_ref[pl.ds(part, 64, stride=WIDTH), :] = turned[part * 128 : (part + 1) * 128, :].T


def read_owner_rows(in_ref, turned_ref):
    for part in range(WIDTH):
        turned_ref[part * 128 : (part + 1) * 128, :] = in_ref[pl.ds(part, 64, stride=WIDTH), :].T


PAGES = 8


def panels_kernel(
    source_hbm, weight_hbm, slots_hbm, count_hbm, cell_hbm, out, where,
    source, weight, slots, count, cell, oh_ref, left_ref, sems,
):
    pairs = (
        (slots_hbm, slots), (count_hbm, count), (cell_hbm, cell), (weight_hbm, weight),
        (source_hbm, source),
    )
    copies = [pltpu.make_async_copy(a, b, sems.at[i]) for i, (a, b) in enumerate(pairs)]
    for copy in copies:
        copy.start()
    copies[0].wait()
    copies[1].wait()
    box = iota((1, BOXES), 1)
    low_value = wide(((box >> 2) & 3) * 64 + (box >> 4), 64)
    high_value = wide(box & 3, 64)
    row64 = rows_bf16((64, BOXES), 0)
    row128 = rows_bf16((128, BOXES), 0)
    none = jnp.zeros((), BF16)

    def invert(s, total):
        panel = slots[pl.ds(s, 1), :]
        page = jnp.where(s < count[...], panel >> 7, 200)
        hit = row64 == wide(page, 64)
        left = jnp.concatenate(
            [jnp.where(hit, low_value, none), jnp.where(hit, high_value, none)], axis=0
        )
        return total + dot_nt(left, one_hot(row128 == wide(panel & 127, 128)))

    total = lax.fori_loop(0, 16, invert, jnp.zeros((128, 128), F32), unroll=True)
    where_now = (total + 0.5).astype(jnp.int32)
    where[...] = where_now
    copies[3].wait()
    copies[4].wait()
    lane256 = rows_bf16((128, 256), 1)
    low_columns = where_now[:64].astype(F32).T.astype(BF16)
    first_step = iota((ROWS, 128), 0) < KROWS

    def spread(page):
        at = page * 128
        low = jnp.broadcast_to(low_columns[:, page : page + 1], (128, 256))
        high = wide(where_now[64 + page : 65 + page, :], 2 * ROWS)
        oh_ref[at : at + 128, :] = one_hot(lane256 == low)
        both = doubled(weight[:, at : at + 128]) * jnp.where(
            first_step, source[0:1, at : at + 128], source[1:2, at : at + 128]
        )
        pieces = halves(both)
        for quarter in range(4):
            left_ref[quarter * 2 * ROWS : (quarter + 1) * 2 * ROWS, at : at + 128] = jnp.where(
                high == jnp.full((), quarter, BF16), pieces, none
            )

    sums = jnp.zeros((8 * ROWS, 256), F32)
    for chunk in range(64 // PAGES):
        for page in range(PAGES):
            spread(chunk * PAGES + page)
        at = slice(chunk * PAGES * 128, (chunk + 1) * PAGES * 128)
        sums = sums + dot(left_ref[:, at], oh_ref[at, :])

    copies[2].wait()
    cells = cell[...]
    match = rows_bf16((16, BOXES), 0) == wide(box & 15, 16)
    left = jnp.concatenate(
        [
            jnp.where(match, wide(cells >> 7, 16), none),
            jnp.where(match, wide(cells & 127, 16), none),
        ],
        axis=0,
    )
    owned = dot_nt(left, one_hot(row64 == wide(box >> 4, 64)))
    cell_rows = owned[:16] * 128.0 + owned[16:]

    blocks = []
    at_cell = iota((ROWS, 64), 0) == CELL_ROW
    for j in range(16):
        at = (j % 4) * 2 * ROWS
        block = sums[at : at + 2 * ROWS, (j // 4) * 64 : (j // 4 + 1) * 64]
        block = block[:ROWS] + block[ROWS:]
        blocks.append(jnp.where(at_cell, cell_rows[j : j + 1, :], block))
    write_owner_rows(jnp.concatenate(blocks, axis=0), out)


PAIRS = 2
HALF = 80


def slab_kernel(recv, fz_hbm, fy_hbm, out, cell_out, fz, fy, turned, values, left_h, left_l, right, sems):
    copies = [
        pltpu.make_async_copy(fz_hbm, fz, sems.at[0]),
        pltpu.make_async_copy(fy_hbm, fy, sems.at[1]),
    ]
    for copy in copies:
        copy.start()
    read_owner_rows(recv, turned)
    lane = iota((128, 128), 1)
    row = iota((128, 128), 0)
    row_b = rows_bf16((HALF, 128), 0)
    lane_b = rows_bf16((128, 256), 1)
    none = jnp.zeros((HALF, 128), BF16)
    spots = []
    for pair in range(8):
        value = jnp.concatenate(
            [
                turned[(2 * pair) * ROWS : (2 * pair + 1) * ROWS, :],
                turned[(2 * pair + 1) * ROWS : (2 * pair + 2) * ROWS, :],
            ],
            axis=1,
        )
        high = value.astype(BF16).astype(F32)
        values[0, pair] = high
        values[1, pair] = value - high
        cell = value[CELL_ROW : CELL_ROW + 1, :].astype(jnp.int32)
        cell_out[pair : pair + 1, :] = cell
        for dz in range(3):
            spots.append((cell >> 13) * 128 + ((cell + (dz - 1)) & 127))
    spots = jnp.concatenate(spots, axis=0).astype(F32).T.astype(BF16)

    def fill(pair):
        cell_y = (cell_out[pair : pair + 1, :] >> 7) & 63
        at_y = [jnp.where(cell_y == 0, 65, cell_y - 1), cell_y, cell_y + 1]
        hits = [row_b == wide(y, HALF) for y in at_y]
        for dz in range(3):
            column = pair * 3 + dz
            at = column * 128
            right[at : at + 128, :] = one_hot(
                lane_b == jnp.broadcast_to(spots[:, column : column + 1], (128, 256))
            )
            for step in range(2):
                for dx in range(2):
                    at_row = (2 * step + dx) * HALF
                    for part, target in ((0, left_h), (1, left_l)):
                        block = none
                        for dy in range(3):
                            k = step * KROWS + 9 * dx + 3 * dy + dz
                            block = jnp.where(
                                hits[dy], wide(values[part, pair, k : k + 1, :], HALF), block
                            )
                        target[at_row : at_row + HALF, at : at + 128] = block

    halved = jnp.zeros((4 * HALF, 256), F32)
    for group in range(8 // PAIRS):
        for pair in range(PAIRS):
            fill(PAIRS * group + pair)
        at = slice(group * PAIRS * 384, (group + 1) * PAIRS * 384)
        halved = halved + (dot(left_h[:, at], right[at, :]) + dot(left_l[:, at], right[at, :]))
    row64 = iota((64, 128), 0)
    planes = []
    for t in range(4):
        for half in range(2):
            here = slice(half * 128, half * 128 + 128)
            other = slice(128 - half * 128, 256 - half * 128)
            part = halved[t * HALF : t * HALF + 64, here]
            part = part + jnp.where(
                row64 == 0, halved[t * HALF + 64 : t * HALF + 65, other], 0.0
            )
            part = part + jnp.where(
                row64 == 63, halved[t * HALF + 65 : t * HALF + 66, other], 0.0
            )
            planes.append(part)
    density = jnp.concatenate(planes, axis=0)
    for copy in copies:
        copy.wait()
    both = dot_right(density, fz)

    def beside(at):
        return jnp.concatenate(
            [both[t * 128 : (t + 1) * 128, at : at + 128] for t in range(4)], axis=1
        )

    even = dot_left(fy[0], beside(0))
    odd = dot_left(fy[1], beside(128))
    ky = (row & 63) * 2 + (row >> 6)
    own = (ky == 0) | (ky == 64)
    pencils = []
    for t in range(4):
        a = even[:, t * 128 : (t + 1) * 128]
        b = odd[:, t * 128 : (t + 1) * 128]
        full = a + b
        full = jnp.where(lane == 0, jnp.where(ky <= 64, a, pltpu.roll(a, 112, 1)), full)
        second = jnp.where(own, a, jnp.where(ky < 64, b, -pltpu.roll(b, 16, 1)))
        pencils.append(jnp.where(lane == 16, second, full))
    for q in range(4):
        piece = jnp.concatenate([p[:, q * 32 : (q + 1) * 32] for p in pencils], axis=1)
        out[q * 64 : (q + 1) * 64, :] = piece[:64]
        out[(4 + q) * 64 : (5 + q) * 64, :] = piece[64:]


def column_kernel(place, recv, decay, fx, gx, lz, lx, out, turned_decay, spectra, fields):
    block = place[0]
    column = place[1]
    ky_low = block // 4
    q = block % 4
    ky = 2 * column + ky_low
    special = ((block == 0) & ((column == 0) | (column == 32))).astype(jnp.int32)
    below = iota((16, 128), 1) < 64
    first_row = iota((16, 128), 0) == 0
    mains, extras = [], []
    for mp in range(4):
        part = recv[mp * 128 : (mp + 1) * 128, :].T
        for half in range(2):
            for n in range(2):
                pieces = []
                for ri in range(2):
                    near = part[(2 * n) * 32 + ri * 16 : (2 * n) * 32 + ri * 16 + 16, :]
                    far = part[(2 * n + 1) * 32 + ri * 16 : (2 * n + 1) * 32 + ri * 16 + 16, :]
                    if half == 0:
                        far = pltpu.roll(far, 64, 1)
                    else:
                        near = pltpu.roll(near, 64, 1)
                    pieces.append(jnp.where(below, near, far))
                extras.append(jnp.where(special == 1, pieces[1][0:1], 0.0))
                pieces[1] = jnp.where(first_row & (special == 1), 0.0, pieces[1])
                mains.append(jnp.concatenate(pieces, axis=1))
    extra = jnp.concatenate(extras, axis=0)
    mains.append(jnp.concatenate([extra, jnp.zeros_like(extra)], axis=1))
    spectra[...] = dot_right(jnp.concatenate(mains, axis=0), fx)

    here = jnp.where(
        ky_low == 1, decay[pl.ds(1, 128, stride=2), :], decay[pl.ds(0, 128, stride=2), :]
    )
    turned_decay[...] = here.T
    slots_at = pl.multiple_of(q * 16, 16)
    moved = jnp.where((q == 0) & (ky > 64), 1, 0)
    at_first = iota((16, 128), 0) + (1 - moved) == 0
    damp_last = turned_decay[64:65, :]
    damp_main = jnp.where(at_first, damp_last, turned_decay[pl.ds(slots_at, 16), :])
    lam_xy = lx[0:1, :] + lz[pl.ds(ky, 1), :]
    lam_main = lam_xy + jnp.where(at_first, lz[64:65, :], lz[pl.ds(slots_at, 16), :])
    lam_last = lam_xy + lz[64:65, :]

    for damp, lam, base, size in ((damp_main, lam_main, 0, 16), (damp_last, lam_last, 256, 1)):
        theta = 0.5 * jnp.sqrt(lam)
        rate_cos = damp * jnp.cos(theta)
        rate_sin = damp * jnp.sin(theta)
        kernel = 1.0 / (1.0 + lam)
        state = [[jnp.zeros_like(lam)] * 2 for _ in range(2)]
        for step in range(16):
            at_row = base + step * size
            for ri in range(2):
                at = ri * 128
                re, im = state[ri]
                state[ri] = [
                    rate_cos * re - rate_sin * im + spectra[at_row : at_row + size, at : at + 128],
                    rate_cos * im + rate_sin * re,
                ]
                fields[at_row : at_row + size, at : at + 128] = kernel * state[ri][0]
    back = dot_right(fields[...], gx)
    for mp in range(4):
        rows = []
        for n in range(2):
            steps = [4 * mp + 2 * half + n for half in range(2)]
            pieces = []
            for ri in range(2):
                both = []
                for step in steps:
                    piece = back[step * 16 : step * 16 + 16, ri * 128 : ri * 128 + 128]
                    if ri == 1:
                        added = back[256 + step : 257 + step, 0:128]
                        piece = piece + jnp.where(first_row, added, 0.0)
                    both.append(piece)
                pieces.append(
                    (
                        jnp.where(below, both[0], pltpu.roll(both[1], 64, 1)),
                        jnp.where(below, pltpu.roll(both[0], 64, 1), both[1]),
                    )
                )
            for dx in range(2):
                for ri in range(2):
                    rows.append(pieces[ri][dx])
        out[mp * 128 : (mp + 1) * 128, :] = jnp.concatenate(rows, axis=0).T


def field_kernel(recv, cells, gz, gy, cs, out, values, left):
    pencils = []
    for t in range(4):
        halves_y = [
            jnp.concatenate(
                [
                    recv[(4 * low + q) * 64 : (4 * low + q + 1) * 64, :][:, t * 32 : (t + 1) * 32]
                    for q in range(4)
                ],
                axis=1,
            )
            for low in range(2)
        ]
        pencils.append(jnp.concatenate(halves_y, axis=0))
    both = dot_right(jnp.concatenate(pencils, axis=0), gz)
    tops, bottoms = [], []
    for t in range(4):
        real = pencils[t][:, 0:1]
        imag = pencils[t][:, 16:17]
        tops.append(both[t * 128 : (t + 1) * 128, :128] + (real * cs[0] + imag * cs[1]))
        bottoms.append(both[t * 128 : (t + 1) * 128, 128:] + imag * cs[2])
    tall = jnp.concatenate(
        [jnp.concatenate(tops, axis=1), jnp.concatenate(bottoms, axis=1)], axis=0
    )
    field = dot_left(gy[...], tall)
    first, second = split(
        jnp.concatenate([field[:, t * 128 : (t + 1) * 128] for t in range(4)], axis=0)
    )
    left[:, :128] = first
    left[:, 128:] = second
    row = iota((128, 128), 0)
    row_b = rows_bf16((128, 128), 0)

    def read(pair, carry):
        cell = cells[pl.ds(pair, 1), :]
        cell_y = cell >> 7
        cell_z = cell & 127
        hot = jnp.concatenate(
            [one_hot(row_b == wide((cell_z + (dz - 1)) & 127, 128)) for dz in range(3)], axis=1
        )
        lines = dot(left[...], jnp.concatenate([hot, hot], axis=0))
        hits = [row == ((cell_y + (dy - 1)) & 127) for dy in range(3)]
        rows = []
        for step in range(2):
            for dx in range(2):
                t = 2 * step + dx
                for dy in range(3):
                    for dz in range(3):
                        line = lines[t * 128 : (t + 1) * 128, dz * 128 : (dz + 1) * 128]
                        rows.append(
                            jnp.sum(jnp.where(hits[dy], line, 0.0), axis=0, keepdims=True)
                        )
            rows.append(jnp.zeros((KROWS - STEN, 128), F32))
        values[pair] = jnp.concatenate(rows, axis=0)
        return carry

    lax.fori_loop(0, 8, read, 0, unroll=True)
    blocks = []
    for j in range(16):
        blocks.append(values[j // 2][:, (j % 2) * 64 : (j % 2 + 1) * 64])
    write_owner_rows(jnp.concatenate(blocks, axis=0), out)


CHUNK = 1024


def potential_kernel(recv, where, weight, out, turned, left):
    read_owner_rows(recv, turned)
    for high in range(4):
        block = jnp.concatenate(
            [turned[(4 * low + high) * ROWS : (4 * low + high + 1) * ROWS, :] for low in range(4)],
            axis=1,
        )
        left[high * 2 * ROWS : (high + 1) * 2 * ROWS, :] = halves(block)
    pages = CHUNK // 128
    row_b = rows_bf16((256, CHUNK), 0)

    def read(chunk, carry):
        at = pl.multiple_of(chunk * CHUNK, CHUNK)
        low = jnp.concatenate(
            [where[pl.ds(chunk * pages + i, 1), :] for i in range(pages)], axis=1
        )
        high = jnp.concatenate(
            [where[pl.ds(64 + chunk * pages + i, 1), :] for i in range(pages)], axis=1
        )
        lines = dot(left[...], one_hot(row_b == wide(low, 256)))
        picked = lines[: 2 * ROWS]
        for quarter in range(1, 4):
            at_row = quarter * 2 * ROWS
            picked = jnp.where(high == quarter, lines[at_row : at_row + 2 * ROWS], picked)
        terms = (picked[:ROWS] + picked[ROWS:]) * doubled(weight[:, pl.ds(at, CHUNK)])
        for step in range(2):
            out[step : step + 1, pl.ds(at, CHUNK)] = jnp.sum(
                terms[step * KROWS : (step + 1) * KROWS], axis=0, keepdims=True
            )
        return carry

    lax.fori_loop(0, PDEV // CHUNK, read, 0, unroll=True)


PARAMS = pltpu.CompilerParams(vmem_limit_bytes=48 * 1024 * 1024)


def f32(*shape):
    return jax.ShapeDtypeStruct(shape, F32)


def i32(*shape):
    return jax.ShapeDtypeStruct(shape, jnp.int32)


def run_panels(source, weight, slots, count, cell):
    return pl.pallas_call(
        panels_kernel,
        out_shape=(f32(64 * WIDTH, 128), i32(128, 128)),
        in_specs=[pl.BlockSpec(memory_space=pltpu.HBM)] * 5,
        scratch_shapes=[
            pltpu.VMEM((2, PDEV), F32),
            pltpu.VMEM((STEN, PDEV), F32),
            pltpu.VMEM((16, BOXES), jnp.int32),
            pltpu.VMEM((1, BOXES), jnp.int32),
            pltpu.VMEM((1, BOXES), jnp.int32),
            pltpu.VMEM((PDEV, 256), BF16),
            pltpu.VMEM((8 * ROWS, PDEV), BF16),
            pltpu.SemaphoreType.DMA((5,)),
        ],
        compiler_params=PARAMS,
        name="panels",
    )(*(pltpu.with_memory_space_constraint(x, pltpu.HBM) for x in (source, weight, slots, count, cell)))


def run_slab(recv, fz, fy):
    return pl.pallas_call(
        slab_kernel,
        out_shape=(f32(512, 128), i32(8, 128)),
        in_specs=[pl.BlockSpec(memory_space=pltpu.VMEM)]
        + [pl.BlockSpec(memory_space=pltpu.HBM)] * 2,
        scratch_shapes=[
            pltpu.VMEM((384, 256), BF16),
            pltpu.VMEM((2, 128, 384), BF16),
            pltpu.VMEM((16 * ROWS, 64), F32),
            pltpu.VMEM((2, 8, ROWS, 128), F32),
            pltpu.VMEM((4 * HALF, 3 * BOXES), BF16),
            pltpu.VMEM((4 * HALF, 3 * BOXES), BF16),
            pltpu.VMEM((3 * BOXES, 256), BF16),
            pltpu.SemaphoreType.DMA((2,)),
        ],
        compiler_params=PARAMS,
        name="slab",
    )(recv, fz, fy)


def run_column(place, recv, decay, fx, gx, lz, lx):
    return pl.pallas_call(
        column_kernel,
        out_shape=f32(512, 128),
        in_specs=[pl.BlockSpec(memory_space=pltpu.SMEM)]
        + [pl.BlockSpec(memory_space=pltpu.VMEM)] * 6,
        scratch_shapes=[
            pltpu.VMEM((128, 128), F32),
            pltpu.VMEM((272, 256), F32),
            pltpu.VMEM((272, 256), F32),
        ],
        compiler_params=PARAMS,
        name="column",
    )(place, recv, decay, fx, gx, lz, lx)


def run_field(recv, cells, gz, gy, cs):
    return pl.pallas_call(
        field_kernel,
        out_shape=f32(64 * WIDTH, 128),
        scratch_shapes=[pltpu.VMEM((8, ROWS, 128), F32), pltpu.VMEM((512, 256), BF16)],
        compiler_params=PARAMS,
        name="field",
    )(recv, cells, gz, gy, cs)


def run_potential(recv, where, weight):
    return pl.pallas_call(
        potential_kernel,
        out_shape=f32(2, PDEV),
        scratch_shapes=[pltpu.VMEM((16 * ROWS, 64), F32), pltpu.VMEM((8 * ROWS, 256), BF16)],
        compiler_params=PARAMS,
        name="potential",
    )(recv, where, weight)


def exchange(rows, parts, axes):
    pieces = rows.reshape(parts, 1, rows.size // parts)
    pieces = lax.all_to_all(pieces, axes, split_axis=0, concat_axis=0, tiled=True)
    return pieces.reshape(rows.shape)


def body(panel_source, proj_weight, box_slots, box_count, box_cell, decay):
    table = {name: jnp.asarray(value) for name, value in tables().items()}
    place = jnp.stack([lax.axis_index("tm"), lax.axis_index("grid")]).astype(jnp.int32)
    out, where = run_panels(
        panel_source, proj_weight, box_slots, box_count.reshape(1, -1), box_cell.reshape(1, -1)
    )
    recv = exchange(out, 64, "grid")
    out, cells = run_slab(recv, table["fz"], table["fy"])
    recv = exchange(out, 512, ("tm", "grid"))
    out = run_column(
        place, recv, decay.reshape(2 * N, N), table["fx"], table["gx"], table["lz"], table["lx"]
    )
    recv = exchange(out, 512, ("tm", "grid"))
    out = run_field(recv, cells, table["gz"], table["gy"], table["cs"])
    recv = exchange(out, 64, "grid")
    return run_potential(recv, where, proj_weight)


def solution(mesh):
    return jax.shard_map(
        body,
        mesh=mesh,
        in_specs=(
            P("tm", "grid"),
            P(None, "grid"),
            P(None, "grid"),
            P("grid"),
            P("grid"),
            P(None, "grid", None),
        ),
        out_specs=P("tm", "grid"),
        check_vma=False,
    )
```

```python
import jax
import jax.numpy as jnp
import ml_dtypes
import numpy as np
from jax import lax
from jax.experimental import pallas as pl
from jax.experimental.pallas import tpu as pltpu
from jax.sharding import PartitionSpec as P

N = 128
STEN = 18
KROWS = 20
CELL_ROW = 18
ROWS = 2 * KROWS
WIDTH = 16 * ROWS // 128
PDEV = 8192
BOXES = 1024
F32 = jnp.float32
BF16 = jnp.bfloat16


def stacked(table, axis):
    table = np.asarray(table, np.float64).astype(np.float32)
    high = table.astype(ml_dtypes.bfloat16)
    low = (table - high.astype(np.float32)).astype(ml_dtypes.bfloat16)
    return np.concatenate([high, high, low], axis=axis)


def angle(rows, cols):
    return 2.0 * np.pi * (np.outer(rows, cols) % N) / N


def tables():
    index = np.arange(N)
    slot = (index // 32) * 16 + index % 16
    imag = (index // 16) % 2 == 1
    ang = angle(index, slot)
    real_z = np.cos(ang)
    imag_z = np.where(slot[None] == 0, np.cos(np.pi * index)[:, None], -np.sin(ang))
    fz = np.concatenate(
        [np.where(imag[None], imag_z, real_z), np.where(imag[None], -real_z, imag_z)], axis=1
    )
    ky = np.concatenate([2 * np.arange(64), 2 * np.arange(64) + 1])
    ay = angle(ky, index)
    fy = np.stack([np.cos(ay), np.sin(ay)])

    grid = np.arange(64)
    fx = np.zeros((2, 2, 64, 2, N))
    gx = np.zeros((2, N, 2, 2, 64))
    for dx in range(2):
        ax = angle(2 * grid + dx, index)
        cos, sin = np.cos(ax), np.sin(ax)
        fx[0, dx, :, 0] = cos
        fx[0, dx, :, 1] = -sin
        fx[1, dx, :, 0] = sin
        fx[1, dx, :, 1] = cos
        gx[0, :, 0, dx] = cos.T / N
        gx[0, :, 1, dx] = sin.T / N
        gx[1, :, 0, dx] = -sin.T / N
        gx[1, :, 1, dx] = cos.T / N
    fx = fx.reshape(256, 256)
    gx = gx.reshape(256, 256)

    weight = np.where(slot == 0, 0.0, 2.0)[:, None] / N
    cz = np.cos(ang.T) * weight
    sz = np.sin(ang.T) * weight
    gz = np.concatenate(
        [np.where(imag[:, None], -sz, cz), np.where(imag[:, None], -cz, -sz)], axis=1
    )
    gy = np.concatenate([np.cos(ay.T), np.sin(ay.T)], axis=1) / N
    self_row = (ky == 0) | (ky == 64)
    pattern = np.where((ky <= 64)[:, None], 1.0, np.cos(np.pi * index)[None])
    c1 = np.where(self_row, 1.0, 2.0)[:, None] * pattern / N
    c2 = np.where(self_row[:, None], np.cos(np.pi * index)[None], 0.0) / N
    c3 = np.where(self_row[:, None], 0.0, -2.0 * pattern) / N
    cs = np.stack([c1, c2, c3]).astype(np.float32)

    lam = 4.0 * np.sin(np.pi * index / N) ** 2
    lz = np.broadcast_to(lam[:, None], (N, N)).astype(np.float32)
    lx = np.broadcast_to(lam[None], (8, N)).astype(np.float32)
    return dict(
        fz=stacked(fz, 0), fy=stacked(fy, 2), fx=stacked(fx, 0), gx=stacked(gx, 0),
        gz=stacked(gz, 0), gy=stacked(gy, 1),
        cs=cs, lz=lz, lx=lx,
    )


def split(values):
    high = values.astype(BF16)
    return high, (values - high.astype(F32)).astype(BF16)


def halves(values):
    high = values.astype(BF16).astype(F32)
    return jnp.concatenate([high, values - high], axis=0).astype(BF16)


def doubled(tile):
    tile = jnp.concatenate([tile, jnp.zeros((KROWS - STEN, tile.shape[1]), F32)], axis=0)
    return jnp.concatenate([tile, tile], axis=0)


def dot(left, right):
    return lax.dot_general(left, right, (((1,), (0,)), ((), ())), preferred_element_type=F32)


def dot_nt(left, right):
    return lax.dot_general(left, right, (((1,), (1,)), ((), ())), preferred_element_type=F32)


def dot_right(values, table):
    high, low = split(values)
    return dot(jnp.concatenate([high, low, high], axis=1), table[...])


def dot_left(table, values):
    high, low = split(values)
    return dot(table, jnp.concatenate([high, low, high], axis=0))


def iota(shape, axis):
    return lax.broadcasted_iota(jnp.int32, shape, axis)


def rows_bf16(shape, axis):
    return iota(shape, axis).astype(F32).astype(BF16)


def wide(row, size):
    sixteen = jnp.broadcast_to(row.astype(F32), (16, row.shape[1])).astype(BF16)
    return jnp.concatenate([sixteen] * (size // 16), axis=0)


def one_hot(mask):
    return jnp.where(mask, jnp.ones((), BF16), jnp.zeros((), BF16))


def write_owner_rows(turned, out_ref):
    for part in range(WIDTH):
        out_ref[pl.ds(part, 64, stride=WIDTH), :] = turned[part * 128 : (part + 1) * 128, :].T


def read_owner_rows(in_ref, turned_ref):
    for part in range(WIDTH):
        turned_ref[part * 128 : (part + 1) * 128, :] = in_ref[pl.ds(part, 64, stride=WIDTH), :].T


PAGES = 8


def panels_kernel(
    source_hbm, weight_hbm, slots_hbm, count_hbm, cell_hbm, out, where,
    source, weight, slots, count, cell, oh_ref, left_ref, sems,
):
    pairs = (
        (slots_hbm, slots), (count_hbm, count), (cell_hbm, cell), (weight_hbm, weight),
        (source_hbm, source),
    )
    copies = [pltpu.make_async_copy(a, b, sems.at[i]) for i, (a, b) in enumerate(pairs)]
    for copy in copies:
        copy.start()
    copies[0].wait()
    copies[1].wait()
    box = iota((1, BOXES), 1)
    low_value = wide(((box >> 2) & 3) * 64 + (box >> 4), 64)
    high_value = wide(box & 3, 64)
    row64 = rows_bf16((64, BOXES), 0)
    row128 = rows_bf16((128, BOXES), 0)
    none = jnp.zeros((), BF16)

    def invert(s, total):
        panel = slots[pl.ds(s, 1), :]
        page = jnp.where(s < count[...], panel >> 7, 200)
        hit = row64 == wide(page, 64)
        left = jnp.concatenate(
            [jnp.where(hit, low_value, none), jnp.where(hit, high_value, none)], axis=0
        )
        return total + dot_nt(left, one_hot(row128 == wide(panel & 127, 128)))

    total = lax.fori_loop(0, 16, invert, jnp.zeros((128, 128), F32), unroll=True)
    where_now = (total + 0.5).astype(jnp.int32)
    where[...] = where_now
    copies[3].wait()
    copies[4].wait()
    lane256 = rows_bf16((128, 256), 1)
    low_columns = where_now[:64].astype(F32).T.astype(BF16)
    first_step = iota((ROWS, 128), 0) < KROWS

    def spread(page):
        at = page * 128
        low = jnp.broadcast_to(low_columns[:, page : page + 1], (128, 256))
        high = wide(where_now[64 + page : 65 + page, :], 2 * ROWS)
        oh_ref[at : at + 128, :] = one_hot(lane256 == low)
        both = doubled(weight[:, at : at + 128]) * jnp.where(
            first_step, source[0:1, at : at + 128], source[1:2, at : at + 128]
        )
        pieces = halves(both)
        for quarter in range(4):
            left_ref[quarter * 2 * ROWS : (quarter + 1) * 2 * ROWS, at : at + 128] = jnp.where(
                high == jnp.full((), quarter, BF16), pieces, none
            )

    sums = jnp.zeros((8 * ROWS, 256), F32)
    for chunk in range(64 // PAGES):
        for page in range(PAGES):
            spread(chunk * PAGES + page)
        at = slice(chunk * PAGES * 128, (chunk + 1) * PAGES * 128)
        sums = sums + dot(left_ref[:, at], oh_ref[at, :])

    copies[2].wait()
    cells = cell[...]
    match = rows_bf16((16, BOXES), 0) == wide(box & 15, 16)
    left = jnp.concatenate(
        [
            jnp.where(match, wide(cells >> 7, 16), none),
            jnp.where(match, wide(cells & 127, 16), none),
        ],
        axis=0,
    )
    owned = dot_nt(left, one_hot(row64 == wide(box >> 4, 64)))
    cell_rows = owned[:16] * 128.0 + owned[16:]

    blocks = []
    at_cell = iota((ROWS, 64), 0) == CELL_ROW
    for j in range(16):
        at = (j % 4) * 2 * ROWS
        block = sums[at : at + 2 * ROWS, (j // 4) * 64 : (j // 4 + 1) * 64]
        block = block[:ROWS] + block[ROWS:]
        blocks.append(jnp.where(at_cell, cell_rows[j : j + 1, :], block))
    write_owner_rows(jnp.concatenate(blocks, axis=0), out)


PAIRS = 2
HALF = 80


def slab_kernel(recv, fz_hbm, fy_hbm, out, cell_out, fz, fy, turned, values, left_h, left_l, right, sems):
    copies = [
        pltpu.make_async_copy(fz_hbm, fz, sems.at[0]),
        pltpu.make_async_copy(fy_hbm, fy, sems.at[1]),
    ]
    for copy in copies:
        copy.start()
    read_owner_rows(recv, turned)
    lane = iota((128, 128), 1)
    row = iota((128, 128), 0)
    row_b = rows_bf16((HALF, 128), 0)
    lane_b = rows_bf16((128, 256), 1)
    none = jnp.zeros((HALF, 128), BF16)
    spots = []
    for pair in range(8):
        value = jnp.concatenate(
            [
                turned[(2 * pair) * ROWS : (2 * pair + 1) * ROWS, :],
                turned[(2 * pair + 1) * ROWS : (2 * pair + 2) * ROWS, :],
            ],
            axis=1,
        )
        high = value.astype(BF16).astype(F32)
        values[0, pair] = high
        values[1, pair] = value - high
        cell = value[CELL_ROW : CELL_ROW + 1, :].astype(jnp.int32)
        cell_out[pair : pair + 1, :] = cell
        for dz in range(3):
            spots.append((cell >> 13) * 128 + ((cell + (dz - 1)) & 127))
    spots = jnp.concatenate(spots, axis=0).astype(F32).T.astype(BF16)

    def fill(pair):
        cell_y = (cell_out[pair : pair + 1, :] >> 7) & 63
        at_y = [jnp.where(cell_y == 0, 65, cell_y - 1), cell_y, cell_y + 1]
        hits = [row_b == wide(y, HALF) for y in at_y]
        for dz in range(3):
            column = pair * 3 + dz
            at = column * 128
            right[at : at + 128, :] = one_hot(
                lane_b == jnp.broadcast_to(spots[:, column : column + 1], (128, 256))
            )
            for step in range(2):
                for dx in range(2):
                    at_row = (2 * step + dx) * HALF
                    for part, target in ((0, left_h), (1, left_l)):
                        block = none
                        for dy in range(3):
                            k = step * KROWS + 9 * dx + 3 * dy + dz
                            block = jnp.where(
                                hits[dy], wide(values[part, pair, k : k + 1, :], HALF), block
                            )
                        target[at_row : at_row + HALF, at : at + 128] = block

    halved = jnp.zeros((4 * HALF, 256), F32)
    for group in range(8 // PAIRS):
        for pair in range(PAIRS):
            fill(PAIRS * group + pair)
        at = slice(group * PAIRS * 384, (group + 1) * PAIRS * 384)
        halved = halved + (dot(left_h[:, at], right[at, :]) + dot(left_l[:, at], right[at, :]))
    row64 = iota((64, 128), 0)
    planes = []
    for t in range(4):
        for half in range(2):
            here = slice(half * 128, half * 128 + 128)
            other = slice(128 - half * 128, 256 - half * 128)
            part = halved[t * HALF : t * HALF + 64, here]
            part = part + jnp.where(
                row64 == 0, halved[t * HALF + 64 : t * HALF + 65, other], 0.0
            )
            part = part + jnp.where(
                row64 == 63, halved[t * HALF + 65 : t * HALF + 66, other], 0.0
            )
            planes.append(part)
    density = jnp.concatenate(planes, axis=0)
    for copy in copies:
        copy.wait()
    both = dot_right(density, fz)

    def beside(at):
        return jnp.concatenate(
            [both[t * 128 : (t + 1) * 128, at : at + 128] for t in range(4)], axis=1
        )

    even = dot_left(fy[0], beside(0))
    odd = dot_left(fy[1], beside(128))
    ky = (row & 63) * 2 + (row >> 6)
    own = (ky == 0) | (ky == 64)
    pencils = []
    for t in range(4):
        a = even[:, t * 128 : (t + 1) * 128]
        b = odd[:, t * 128 : (t + 1) * 128]
        full = a + b
        full = jnp.where(lane == 0, jnp.where(ky <= 64, a, pltpu.roll(a, 112, 1)), full)
        second = jnp.where(own, a, jnp.where(ky < 64, b, -pltpu.roll(b, 16, 1)))
        pencils.append(jnp.where(lane == 16, second, full))
    for q in range(4):
        piece = jnp.concatenate([p[:, q * 32 : (q + 1) * 32] for p in pencils], axis=1)
        out[q * 64 : (q + 1) * 64, :] = piece[:64]
        out[(4 + q) * 64 : (5 + q) * 64, :] = piece[64:]


def column_kernel(place, recv, decay, fx, gx, lz, lx, out, turned_decay, spectra, fields):
    block = place[0]
    column = place[1]
    ky_low = block // 4
    q = block % 4
    ky = 2 * column + ky_low
    special = ((block == 0) & ((column == 0) | (column == 32))).astype(jnp.int32)
    below = iota((16, 128), 1) < 64
    first_row = iota((16, 128), 0) == 0
    mains, extras = [], []
    for mp in range(4):
        part = recv[mp * 128 : (mp + 1) * 128, :].T
        for half in range(2):
            for n in range(2):
                pieces = []
                for ri in range(2):
                    near = part[(2 * n) * 32 + ri * 16 : (2 * n) * 32 + ri * 16 + 16, :]
                    far = part[(2 * n + 1) * 32 + ri * 16 : (2 * n + 1) * 32 + ri * 16 + 16, :]
                    if half == 0:
                        far = pltpu.roll(far, 64, 1)
                    else:
                        near = pltpu.roll(near, 64, 1)
                    pieces.append(jnp.where(below, near, far))
                extras.append(jnp.where(special == 1, pieces[1][0:1], 0.0))
                pieces[1] = jnp.where(first_row & (special == 1), 0.0, pieces[1])
                mains.append(jnp.concatenate(pieces, axis=1))
    extra = jnp.concatenate(extras, axis=0)
    mains.append(jnp.concatenate([extra, jnp.zeros_like(extra)], axis=1))
    spectra[...] = dot_right(jnp.concatenate(mains, axis=0), fx)

    here = jnp.where(
        ky_low == 1, decay[pl.ds(1, 128, stride=2), :], decay[pl.ds(0, 128, stride=2), :]
    )
    turned_decay[...] = here.T
    slots_at = pl.multiple_of(q * 16, 16)
    moved = jnp.where((q == 0) & (ky > 64), 1, 0)
    at_first = iota((16, 128), 0) + (1 - moved) == 0
    damp_last = turned_decay[64:65, :]
    damp_main = jnp.where(at_first, damp_last, turned_decay[pl.ds(slots_at, 16), :])
    lam_xy = lx[0:1, :] + lz[pl.ds(ky, 1), :]
    lam_main = lam_xy + jnp.where(at_first, lz[64:65, :], lz[pl.ds(slots_at, 16), :])
    lam_last = lam_xy + lz[64:65, :]

    for damp, lam, base, size in ((damp_main, lam_main, 0, 16), (damp_last, lam_last, 256, 1)):
        theta = 0.5 * jnp.sqrt(lam)
        rate_cos = damp * jnp.cos(theta)
        rate_sin = damp * jnp.sin(theta)
        kernel = 1.0 / (1.0 + lam)
        state = [[jnp.zeros_like(lam)] * 2 for _ in range(2)]
        for step in range(16):
            at_row = base + step * size
            for ri in range(2):
                at = ri * 128
                re, im = state[ri]
                state[ri] = [
                    rate_cos * re - rate_sin * im + spectra[at_row : at_row + size, at : at + 128],
                    rate_cos * im + rate_sin * re,
                ]
                fields[at_row : at_row + size, at : at + 128] = kernel * state[ri][0]
    back = dot_right(fields[...], gx)
    for mp in range(4):
        rows = []
        for n in range(2):
            steps = [4 * mp + 2 * half + n for half in range(2)]
            pieces = []
            for ri in range(2):
                both = []
                for step in steps:
                    piece = back[step * 16 : step * 16 + 16, ri * 128 : ri * 128 + 128]
                    if ri == 1:
                        added = back[256 + step : 257 + step, 0:128]
                        piece = piece + jnp.where(first_row, added, 0.0)
                    both.append(piece)
                pieces.append(
                    (
                        jnp.where(below, both[0], pltpu.roll(both[1], 64, 1)),
                        jnp.where(below, pltpu.roll(both[0], 64, 1), both[1]),
                    )
                )
            for dx in range(2):
                for ri in range(2):
                    rows.append(pieces[ri][dx])
        out[mp * 128 : (mp + 1) * 128, :] = jnp.concatenate(rows, axis=0).T


READ = 72


def field_kernel(recv, cells, gz, gy, cs, out, values, left):
    pencils = []
    for t in range(4):
        halves_y = [
            jnp.concatenate(
                [
                    recv[(4 * low + q) * 64 : (4 * low + q + 1) * 64, :][:, t * 32 : (t + 1) * 32]
                    for q in range(4)
                ],
                axis=1,
            )
            for low in range(2)
        ]
        pencils.append(jnp.concatenate(halves_y, axis=0))
    both = dot_right(jnp.concatenate(pencils, axis=0), gz)
    tops, bottoms = [], []
    for t in range(4):
        real = pencils[t][:, 0:1]
        imag = pencils[t][:, 16:17]
        tops.append(both[t * 128 : (t + 1) * 128, :128] + (real * cs[0] + imag * cs[1]))
        bottoms.append(both[t * 128 : (t + 1) * 128, 128:] + imag * cs[2])
    tall = jnp.concatenate(
        [jnp.concatenate(tops, axis=1), jnp.concatenate(bottoms, axis=1)], axis=0
    )
    field = dot_left(gy[...], tall)
    rows = []
    for t in range(4):
        plane = field[:, t * 128 : (t + 1) * 128]
        tops = jnp.concatenate([plane[:64], plane[64:]], axis=1)
        after = jnp.concatenate([plane[64:65], plane[0:1]], axis=1)
        before = jnp.concatenate([plane[127:128], plane[63:64]], axis=1)
        rows += [tops, after, before, jnp.zeros((READ - 66, 256), F32)]
    left[...] = jnp.concatenate(split(jnp.concatenate(rows, axis=0)), axis=1)
    row = iota((READ, 128), 0)
    row_b = rows_bf16((256, 128), 0)

    def read(pair, carry):
        cell = cells[pl.ds(pair, 1), :]
        cell_y = (cell >> 7) & 63
        hot = jnp.concatenate(
            [
                one_hot(row_b == wide((cell >> 13) * 128 + ((cell + (dz - 1)) & 127), 256))
                for dz in range(3)
            ],
            axis=1,
        )
        lines = dot(left[...], jnp.concatenate([hot, hot], axis=0))
        hits = [row == y for y in (jnp.where(cell_y == 0, 65, cell_y - 1), cell_y, cell_y + 1)]
        rows = []
        for step in range(2):
            for dx in range(2):
                t = 2 * step + dx
                for dy in range(3):
                    for dz in range(3):
                        line = lines[t * READ : (t + 1) * READ, dz * 128 : (dz + 1) * 128]
                        rows.append(
                            jnp.sum(jnp.where(hits[dy], line, 0.0), axis=0, keepdims=True)
                        )
            rows.append(jnp.zeros((KROWS - STEN, 128), F32))
        values[pair] = jnp.concatenate(rows, axis=0)
        return carry

    lax.fori_loop(0, 8, read, 0, unroll=True)
    blocks = []
    for j in range(16):
        blocks.append(values[j // 2][:, (j % 2) * 64 : (j % 2 + 1) * 64])
    write_owner_rows(jnp.concatenate(blocks, axis=0), out)


CHUNK = 1024


def potential_kernel(recv, where, weight, out, turned, left):
    read_owner_rows(recv, turned)
    for high in range(4):
        block = jnp.concatenate(
            [turned[(4 * low + high) * ROWS : (4 * low + high + 1) * ROWS, :] for low in range(4)],
            axis=1,
        )
        left[high * 2 * ROWS : (high + 1) * 2 * ROWS, :] = halves(block)
    pages = CHUNK // 128
    row_b = rows_bf16((256, CHUNK), 0)

    def read(chunk, carry):
        at = pl.multiple_of(chunk * CHUNK, CHUNK)
        low = jnp.concatenate(
            [where[pl.ds(chunk * pages + i, 1), :] for i in range(pages)], axis=1
        )
        high = jnp.concatenate(
            [where[pl.ds(64 + chunk * pages + i, 1), :] for i in range(pages)], axis=1
        )
        lines = dot(left[...], one_hot(row_b == wide(low, 256)))
        picked = lines[: 2 * ROWS]
        for quarter in range(1, 4):
            at_row = quarter * 2 * ROWS
            picked = jnp.where(high == quarter, lines[at_row : at_row + 2 * ROWS], picked)
        terms = (picked[:ROWS] + picked[ROWS:]) * doubled(weight[:, pl.ds(at, CHUNK)])
        for step in range(2):
            out[step : step + 1, pl.ds(at, CHUNK)] = jnp.sum(
                terms[step * KROWS : (step + 1) * KROWS], axis=0, keepdims=True
            )
        return carry

    lax.fori_loop(0, PDEV // CHUNK, read, 0, unroll=True)


PARAMS = pltpu.CompilerParams(vmem_limit_bytes=48 * 1024 * 1024)


def f32(*shape):
    return jax.ShapeDtypeStruct(shape, F32)


def i32(*shape):
    return jax.ShapeDtypeStruct(shape, jnp.int32)


def run_panels(source, weight, slots, count, cell):
    return pl.pallas_call(
        panels_kernel,
        out_shape=(f32(64 * WIDTH, 128), i32(128, 128)),
        in_specs=[pl.BlockSpec(memory_space=pltpu.HBM)] * 5,
        scratch_shapes=[
            pltpu.VMEM((2, PDEV), F32),
            pltpu.VMEM((STEN, PDEV), F32),
            pltpu.VMEM((16, BOXES), jnp.int32),
            pltpu.VMEM((1, BOXES), jnp.int32),
            pltpu.VMEM((1, BOXES), jnp.int32),
            pltpu.VMEM((PDEV, 256), BF16),
            pltpu.VMEM((8 * ROWS, PDEV), BF16),
            pltpu.SemaphoreType.DMA((5,)),
        ],
        compiler_params=PARAMS,
        name="panels",
    )(*(pltpu.with_memory_space_constraint(x, pltpu.HBM) for x in (source, weight, slots, count, cell)))


def run_slab(recv, fz, fy):
    return pl.pallas_call(
        slab_kernel,
        out_shape=(f32(512, 128), i32(8, 128)),
        in_specs=[pl.BlockSpec(memory_space=pltpu.VMEM)]
        + [pl.BlockSpec(memory_space=pltpu.HBM)] * 2,
        scratch_shapes=[
            pltpu.VMEM((384, 256), BF16),
            pltpu.VMEM((2, 128, 384), BF16),
            pltpu.VMEM((16 * ROWS, 64), F32),
            pltpu.VMEM((2, 8, ROWS, 128), F32),
            pltpu.VMEM((4 * HALF, 3 * BOXES), BF16),
            pltpu.VMEM((4 * HALF, 3 * BOXES), BF16),
            pltpu.VMEM((3 * BOXES, 256), BF16),
            pltpu.SemaphoreType.DMA((2,)),
        ],
        compiler_params=PARAMS,
        name="slab",
    )(recv, fz, fy)


def run_column(place, recv, decay, fx, gx, lz, lx):
    return pl.pallas_call(
        column_kernel,
        out_shape=f32(512, 128),
        in_specs=[pl.BlockSpec(memory_space=pltpu.SMEM)]
        + [pl.BlockSpec(memory_space=pltpu.VMEM)] * 6,
        scratch_shapes=[
            pltpu.VMEM((128, 128), F32),
            pltpu.VMEM((272, 256), F32),
            pltpu.VMEM((272, 256), F32),
        ],
        compiler_params=PARAMS,
        name="column",
    )(place, recv, decay, fx, gx, lz, lx)


def run_field(recv, cells, gz, gy, cs):
    return pl.pallas_call(
        field_kernel,
        out_shape=f32(64 * WIDTH, 128),
        scratch_shapes=[pltpu.VMEM((8, ROWS, 128), F32), pltpu.VMEM((4 * READ, 512), BF16)],
        compiler_params=PARAMS,
        name="field",
    )(recv, cells, gz, gy, cs)


def run_potential(recv, where, weight):
    return pl.pallas_call(
        potential_kernel,
        out_shape=f32(2, PDEV),
        scratch_shapes=[pltpu.VMEM((16 * ROWS, 64), F32), pltpu.VMEM((8 * ROWS, 256), BF16)],
        compiler_params=PARAMS,
        name="potential",
    )(recv, where, weight)


def exchange(rows, parts, axes):
    pieces = rows.reshape(parts, 1, rows.size // parts)
    pieces = lax.all_to_all(pieces, axes, split_axis=0, concat_axis=0, tiled=True)
    return pieces.reshape(rows.shape)


def body(panel_source, proj_weight, box_slots, box_count, box_cell, decay):
    table = {name: jnp.asarray(value) for name, value in tables().items()}
    place = jnp.stack([lax.axis_index("tm"), lax.axis_index("grid")]).astype(jnp.int32)
    box_count, place = lax.optimization_barrier((box_count, place))
    out, where = run_panels(
        panel_source, proj_weight, box_slots, box_count.reshape(1, -1), box_cell.reshape(1, -1)
    )
    recv = exchange(out, 64, "grid")
    out, cells = run_slab(recv, table["fz"], table["fy"])
    recv = exchange(out, 512, ("tm", "grid"))
    out = run_column(
        place, recv, decay.reshape(2 * N, N), table["fx"], table["gx"], table["lz"], table["lx"]
    )
    recv = exchange(out, 512, ("tm", "grid"))
    out = run_field(recv, cells, table["gz"], table["gy"], table["cs"])
    recv = exchange(out, 64, "grid")
    return run_potential(recv, where, proj_weight)


def solution(mesh):
    return jax.shard_map(
        body,
        mesh=mesh,
        in_specs=(
            P("tm", "grid"),
            P(None, "grid"),
            P(None, "grid"),
            P("grid"),
            P("grid"),
            P(None, "grid", None),
        ),
        out_specs=P("tm", "grid"),
        check_vma=False,
    )
```

```python
import jax
import jax.numpy as jnp
import ml_dtypes
import numpy as np
from jax import lax
from jax.experimental import pallas as pl
from jax.experimental.pallas import tpu as pltpu
from jax.sharding import PartitionSpec as P

N = 128
STEN = 18
KROWS = 20
CELL_ROW = 18
ROWS = 2 * KROWS
WIDTH = 16 * ROWS // 128
PDEV = 8192
BOXES = 1024
F32 = jnp.float32
BF16 = jnp.bfloat16


def stacked(table, axis):
    table = np.asarray(table, np.float64).astype(np.float32)
    high = table.astype(ml_dtypes.bfloat16)
    low = (table - high.astype(np.float32)).astype(ml_dtypes.bfloat16)
    return np.concatenate([high, high, low], axis=axis)


def angle(rows, cols):
    return 2.0 * np.pi * (np.outer(rows, cols) % N) / N


def tables():
    index = np.arange(N)
    slot = (index // 32) * 16 + index % 16
    imag = (index // 16) % 2 == 1
    ang = angle(index, slot)
    real_z = np.cos(ang)
    imag_z = np.where(slot[None] == 0, np.cos(np.pi * index)[:, None], -np.sin(ang))
    fz = np.concatenate(
        [np.where(imag[None], imag_z, real_z), np.where(imag[None], -real_z, imag_z)], axis=1
    )
    ky = np.concatenate([2 * np.arange(64), 2 * np.arange(64) + 1])
    ay = angle(ky, index)
    fy = np.stack([np.cos(ay), np.sin(ay)])

    grid = np.arange(64)
    fx = np.zeros((2, 2, 64, 2, N))
    gx = np.zeros((2, N, 2, 2, 64))
    for dx in range(2):
        ax = angle(2 * grid + dx, index)
        cos, sin = np.cos(ax), np.sin(ax)
        fx[0, dx, :, 0] = cos
        fx[0, dx, :, 1] = -sin
        fx[1, dx, :, 0] = sin
        fx[1, dx, :, 1] = cos
        gx[0, :, 0, dx] = cos.T / N
        gx[0, :, 1, dx] = sin.T / N
        gx[1, :, 0, dx] = -sin.T / N
        gx[1, :, 1, dx] = cos.T / N
    fx = fx.reshape(256, 256)
    gx = gx.reshape(256, 256)

    weight = np.where(slot == 0, 0.0, 2.0)[:, None] / N
    cz = np.cos(ang.T) * weight
    sz = np.sin(ang.T) * weight
    gz = np.concatenate(
        [np.where(imag[:, None], -sz, cz), np.where(imag[:, None], -cz, -sz)], axis=1
    )
    gy = np.concatenate([np.cos(ay.T), np.sin(ay.T)], axis=1) / N
    self_row = (ky == 0) | (ky == 64)
    pattern = np.where((ky <= 64)[:, None], 1.0, np.cos(np.pi * index)[None])
    c1 = np.where(self_row, 1.0, 2.0)[:, None] * pattern / N
    c2 = np.where(self_row[:, None], np.cos(np.pi * index)[None], 0.0) / N
    c3 = np.where(self_row[:, None], 0.0, -2.0 * pattern) / N
    cs = np.stack([c1, c2, c3]).astype(np.float32)

    lam = 4.0 * np.sin(np.pi * index / N) ** 2
    lz = np.broadcast_to(lam[:, None], (N, N)).astype(np.float32)
    lx = np.broadcast_to(lam[None], (8, N)).astype(np.float32)
    return dict(
        fz=stacked(fz, 0), fy=stacked(fy, 2), fx=stacked(fx, 0), gx=stacked(gx, 0),
        gz=stacked(gz, 0), gy=stacked(gy, 1),
        cs=cs, lz=lz, lx=lx,
    )


def split(values):
    high = values.astype(BF16)
    return high, (values - high.astype(F32)).astype(BF16)


def halves(values):
    high = values.astype(BF16).astype(F32)
    return jnp.concatenate([high, values - high], axis=0).astype(BF16)


def doubled(tile):
    tile = jnp.concatenate([tile, jnp.zeros((KROWS - STEN, tile.shape[1]), F32)], axis=0)
    return jnp.concatenate([tile, tile], axis=0)


def dot(left, right):
    return lax.dot_general(left, right, (((1,), (0,)), ((), ())), preferred_element_type=F32)


def dot_nt(left, right):
    return lax.dot_general(left, right, (((1,), (1,)), ((), ())), preferred_element_type=F32)


def dot_right(values, table):
    high, low = split(values)
    return dot(jnp.concatenate([high, low, high], axis=1), table[...])


def dot_left(table, values):
    high, low = split(values)
    return dot(table, jnp.concatenate([high, low, high], axis=0))


def iota(shape, axis):
    return lax.broadcasted_iota(jnp.int32, shape, axis)


def rows_bf16(shape, axis):
    return iota(shape, axis).astype(F32).astype(BF16)


def wide(row, size):
    sixteen = jnp.broadcast_to(row.astype(F32), (16, row.shape[1])).astype(BF16)
    return jnp.concatenate([sixteen] * (size // 16), axis=0)


def one_hot(mask):
    return jnp.where(mask, jnp.ones((), BF16), jnp.zeros((), BF16))


def write_owner_rows(turned, out_ref):
    for part in range(WIDTH):
        out_ref[pl.ds(part, 64, stride=WIDTH), :] = turned[part * 128 : (part + 1) * 128, :].T


def read_owner_rows(in_ref, turned_ref):
    for part in range(WIDTH):
        turned_ref[part * 128 : (part + 1) * 128, :] = in_ref[pl.ds(part, 64, stride=WIDTH), :].T


PAGES = 8


def panels_kernel(
    source_hbm, weight_hbm, slots_hbm, count_hbm, cell_hbm, out, where,
    source, weight, slots, count, cell, oh_ref, left_ref, sems,
):
    pairs = (
        (slots_hbm, slots), (count_hbm, count), (cell_hbm, cell), (weight_hbm, weight),
        (source_hbm, source),
    )
    copies = [pltpu.make_async_copy(a, b, sems.at[i]) for i, (a, b) in enumerate(pairs)]
    for copy in copies:
        copy.start()
    copies[0].wait()
    copies[1].wait()
    box = iota((1, BOXES), 1)
    low_value = wide(((box >> 2) & 3) * 64 + (box >> 4), 64)
    high_value = wide(box & 3, 64)
    row64 = rows_bf16((64, BOXES), 0)
    row128 = rows_bf16((128, BOXES), 0)
    none = jnp.zeros((), BF16)

    def invert(s, total):
        panel = slots[pl.ds(s, 1), :]
        page = jnp.where(s < count[...], panel >> 7, 200)
        hit = row64 == wide(page, 64)
        left = jnp.concatenate(
            [jnp.where(hit, low_value, none), jnp.where(hit, high_value, none)], axis=0
        )
        return total + dot_nt(left, one_hot(row128 == wide(panel & 127, 128)))

    total = lax.fori_loop(0, 16, invert, jnp.zeros((128, 128), F32), unroll=True)
    where_now = (total + 0.5).astype(jnp.int32)
    where[...] = where_now
    copies[3].wait()
    copies[4].wait()
    lane256 = rows_bf16((128, 256), 1)
    low_columns = where_now[:64].astype(F32).T.astype(BF16)
    first_step = iota((ROWS, 128), 0) < KROWS

    def spread(page):
        at = page * 128
        low = jnp.broadcast_to(low_columns[:, page : page + 1], (128, 256))
        high = wide(where_now[64 + page : 65 + page, :], 2 * ROWS)
        oh_ref[at : at + 128, :] = one_hot(lane256 == low)
        both = doubled(weight[:, at : at + 128]) * jnp.where(
            first_step, source[0:1, at : at + 128], source[1:2, at : at + 128]
        )
        pieces = halves(both)
        for quarter in range(4):
            left_ref[quarter * 2 * ROWS : (quarter + 1) * 2 * ROWS, at : at + 128] = jnp.where(
                high == jnp.full((), quarter, BF16), pieces, none
            )

    sums = jnp.zeros((8 * ROWS, 256), F32)
    for chunk in range(64 // PAGES):
        for page in range(PAGES):
            spread(chunk * PAGES + page)
        at = slice(chunk * PAGES * 128, (chunk + 1) * PAGES * 128)
        sums = sums + dot(left_ref[:, at], oh_ref[at, :])

    copies[2].wait()
    cells = cell[...]
    match = rows_bf16((16, BOXES), 0) == wide(box & 15, 16)
    left = jnp.concatenate(
        [
            jnp.where(match, wide(cells >> 7, 16), none),
            jnp.where(match, wide(cells & 127, 16), none),
        ],
        axis=0,
    )
    owned = dot_nt(left, one_hot(row64 == wide(box >> 4, 64)))
    cell_rows = owned[:16] * 128.0 + owned[16:]

    blocks = []
    at_cell = iota((ROWS, 64), 0) == CELL_ROW
    for j in range(16):
        at = (j % 4) * 2 * ROWS
        block = sums[at : at + 2 * ROWS, (j // 4) * 64 : (j // 4 + 1) * 64]
        block = block[:ROWS] + block[ROWS:]
        blocks.append(jnp.where(at_cell, cell_rows[j : j + 1, :], block))
    write_owner_rows(jnp.concatenate(blocks, axis=0), out)


PAIRS = 2
HALF = 80


def slab_kernel(recv, fz_hbm, fy_hbm, out, cell_out, fz, fy, turned, values, left_h, left_l, right, sems):
    copies = [
        pltpu.make_async_copy(fz_hbm, fz, sems.at[0]),
        pltpu.make_async_copy(fy_hbm, fy, sems.at[1]),
    ]
    for copy in copies:
        copy.start()
    read_owner_rows(recv, turned)
    lane = iota((128, 128), 1)
    row = iota((128, 128), 0)
    row_b = rows_bf16((HALF, 128), 0)
    lane_b = rows_bf16((128, 256), 1)
    none = jnp.zeros((HALF, 128), BF16)
    spots = []
    for pair in range(8):
        value = jnp.concatenate(
            [
                turned[(2 * pair) * ROWS : (2 * pair + 1) * ROWS, :],
                turned[(2 * pair + 1) * ROWS : (2 * pair + 2) * ROWS, :],
            ],
            axis=1,
        )
        high = value.astype(BF16).astype(F32)
        values[0, pair] = high
        values[1, pair] = value - high
        cell = value[CELL_ROW : CELL_ROW + 1, :].astype(jnp.int32)
        cell_out[pair : pair + 1, :] = cell
        for dz in range(3):
            spots.append((cell >> 13) * 128 + ((cell + (dz - 1)) & 127))
    spots = jnp.concatenate(spots, axis=0).astype(F32).T.astype(BF16)

    def fill(pair):
        cell_y = (cell_out[pair : pair + 1, :] >> 7) & 63
        at_y = [jnp.where(cell_y == 0, 65, cell_y - 1), cell_y, cell_y + 1]
        hits = [row_b == wide(y, HALF) for y in at_y]
        for dz in range(3):
            column = pair * 3 + dz
            at = column * 128
            right[at : at + 128, :] = one_hot(
                lane_b == jnp.broadcast_to(spots[:, column : column + 1], (128, 256))
            )
            for step in range(2):
                for dx in range(2):
                    at_row = (2 * step + dx) * HALF
                    for part, target in ((0, left_h), (1, left_l)):
                        block = none
                        for dy in range(3):
                            k = step * KROWS + 9 * dx + 3 * dy + dz
                            block = jnp.where(
                                hits[dy], wide(values[part, pair, k : k + 1, :], HALF), block
                            )
                        target[at_row : at_row + HALF, at : at + 128] = block

    halved = jnp.zeros((4 * HALF, 256), F32)
    for group in range(8 // PAIRS):
        for pair in range(PAIRS):
            fill(PAIRS * group + pair)
        at = slice(group * PAIRS * 384, (group + 1) * PAIRS * 384)
        halved = halved + (dot(left_h[:, at], right[at, :]) + dot(left_l[:, at], right[at, :]))
    row64 = iota((64, 128), 0)
    planes = []
    for t in range(4):
        for half in range(2):
            here = slice(half * 128, half * 128 + 128)
            other = slice(128 - half * 128, 256 - half * 128)
            part = halved[t * HALF : t * HALF + 64, here]
            part = part + jnp.where(
                row64 == 0, halved[t * HALF + 64 : t * HALF + 65, other], 0.0
            )
            part = part + jnp.where(
                row64 == 63, halved[t * HALF + 65 : t * HALF + 66, other], 0.0
            )
            planes.append(part)
    density = jnp.concatenate(planes, axis=0)
    for copy in copies:
        copy.wait()
    both = dot_right(density, fz)

    def beside(at):
        return jnp.concatenate(
            [both[t * 128 : (t + 1) * 128, at : at + 128] for t in range(4)], axis=1
        )

    even = dot_left(fy[0], beside(0))
    odd = dot_left(fy[1], beside(128))
    ky = (row & 63) * 2 + (row >> 6)
    own = (ky == 0) | (ky == 64)
    pencils = []
    for t in range(4):
        a = even[:, t * 128 : (t + 1) * 128]
        b = odd[:, t * 128 : (t + 1) * 128]
        full = a + b
        full = jnp.where(lane == 0, jnp.where(ky <= 64, a, pltpu.roll(a, 112, 1)), full)
        second = jnp.where(own, a, jnp.where(ky < 64, b, -pltpu.roll(b, 16, 1)))
        pencils.append(jnp.where(lane == 16, second, full))
    for q in range(4):
        piece = jnp.concatenate([p[:, q * 32 : (q + 1) * 32] for p in pencils], axis=1)
        out[q * 64 : (q + 1) * 64, :] = piece[:64]
        out[(4 + q) * 64 : (5 + q) * 64, :] = piece[64:]


def column_kernel(place, recv, decay, fx, gx, lz, lx, out, turned_decay, spectra, fields):
    block = place[0]
    column = place[1]
    ky_low = block // 4
    q = block % 4
    ky = 2 * column + ky_low
    special = ((block == 0) & ((column == 0) | (column == 32))).astype(jnp.int32)
    below = iota((16, 128), 1) < 64
    first_row = iota((16, 128), 0) == 0
    mains, extras = [], []
    for mp in range(4):
        part = recv[mp * 128 : (mp + 1) * 128, :].T
        for half in range(2):
            for n in range(2):
                pieces = []
                for ri in range(2):
                    near = part[(2 * n) * 32 + ri * 16 : (2 * n) * 32 + ri * 16 + 16, :]
                    far = part[(2 * n + 1) * 32 + ri * 16 : (2 * n + 1) * 32 + ri * 16 + 16, :]
                    if half == 0:
                        far = pltpu.roll(far, 64, 1)
                    else:
                        near = pltpu.roll(near, 64, 1)
                    pieces.append(jnp.where(below, near, far))
                extras.append(jnp.where(special == 1, pieces[1][0:1], 0.0))
                pieces[1] = jnp.where(first_row & (special == 1), 0.0, pieces[1])
                mains.append(jnp.concatenate(pieces, axis=1))
    extra = jnp.concatenate(extras, axis=0)
    mains.append(jnp.concatenate([extra, jnp.zeros_like(extra)], axis=1))
    spectra[...] = dot_right(jnp.concatenate(mains, axis=0), fx)

    here = jnp.where(
        ky_low == 1, decay[pl.ds(1, 128, stride=2), :], decay[pl.ds(0, 128, stride=2), :]
    )
    turned_decay[...] = here.T
    slots_at = pl.multiple_of(q * 16, 16)
    moved = jnp.where((q == 0) & (ky > 64), 1, 0)
    at_first = iota((16, 128), 0) + (1 - moved) == 0
    damp_last = turned_decay[64:65, :]
    damp_main = jnp.where(at_first, damp_last, turned_decay[pl.ds(slots_at, 16), :])
    lam_xy = lx[0:1, :] + lz[pl.ds(ky, 1), :]
    lam_main = lam_xy + jnp.where(at_first, lz[64:65, :], lz[pl.ds(slots_at, 16), :])
    lam_last = lam_xy + lz[64:65, :]

    for damp, lam, base, size in ((damp_main, lam_main, 0, 16), (damp_last, lam_last, 256, 1)):
        theta = 0.5 * jnp.sqrt(lam)
        rate_cos = damp * jnp.cos(theta)
        rate_sin = damp * jnp.sin(theta)
        kernel = 1.0 / (1.0 + lam)
        state = [[jnp.zeros_like(lam)] * 2 for _ in range(2)]
        for step in range(16):
            at_row = base + step * size
            for ri in range(2):
                at = ri * 128
                re, im = state[ri]
                state[ri] = [
                    rate_cos * re - rate_sin * im + spectra[at_row : at_row + size, at : at + 128],
                    rate_cos * im + rate_sin * re,
                ]
                fields[at_row : at_row + size, at : at + 128] = kernel * state[ri][0]
    back = dot_right(fields[...], gx)
    for mp in range(4):
        rows = []
        for n in range(2):
            steps = [4 * mp + 2 * half + n for half in range(2)]
            pieces = []
            for ri in range(2):
                both = []
                for step in steps:
                    piece = back[step * 16 : step * 16 + 16, ri * 128 : ri * 128 + 128]
                    if ri == 1:
                        added = back[256 + step : 257 + step, 0:128]
                        piece = piece + jnp.where(first_row, added, 0.0)
                    both.append(piece)
                pieces.append(
                    (
                        jnp.where(below, both[0], pltpu.roll(both[1], 64, 1)),
                        jnp.where(below, pltpu.roll(both[0], 64, 1), both[1]),
                    )
                )
            for dx in range(2):
                for ri in range(2):
                    rows.append(pieces[ri][dx])
        out[mp * 128 : (mp + 1) * 128, :] = jnp.concatenate(rows, axis=0).T


READ = 72


def field_kernel(recv, cells, gz, gy, cs, out, values, left):
    pencils = []
    for t in range(4):
        halves_y = [
            jnp.concatenate(
                [
                    recv[(4 * low + q) * 64 : (4 * low + q + 1) * 64, :][:, t * 32 : (t + 1) * 32]
                    for q in range(4)
                ],
                axis=1,
            )
            for low in range(2)
        ]
        pencils.append(jnp.concatenate(halves_y, axis=0))
    both = dot_right(jnp.concatenate(pencils, axis=0), gz)
    tops, bottoms = [], []
    for t in range(4):
        real = pencils[t][:, 0:1]
        imag = pencils[t][:, 16:17]
        tops.append(both[t * 128 : (t + 1) * 128, :128] + (real * cs[0] + imag * cs[1]))
        bottoms.append(both[t * 128 : (t + 1) * 128, 128:] + imag * cs[2])
    tall = jnp.concatenate(
        [jnp.concatenate(tops, axis=1), jnp.concatenate(bottoms, axis=1)], axis=0
    )
    field = dot_left(gy[...], tall)
    rows = []
    for t in range(4):
        plane = field[:, t * 128 : (t + 1) * 128]
        tops = jnp.concatenate([plane[:64], plane[64:]], axis=1)
        after = jnp.concatenate([plane[64:65], plane[0:1]], axis=1)
        before = jnp.concatenate([plane[127:128], plane[63:64]], axis=1)
        rows += [tops, after, before, jnp.zeros((READ - 66, 256), F32)]
    left[...] = jnp.concatenate(split(jnp.concatenate(rows, axis=0)), axis=1)
    row = iota((READ, 128), 0)
    row_b = rows_bf16((256, 128), 0)

    def read(pair, carry):
        cell = cells[pl.ds(pair, 1), :]
        cell_y = (cell >> 7) & 63
        hot = jnp.concatenate(
            [
                one_hot(row_b == wide((cell >> 13) * 128 + ((cell + (dz - 1)) & 127), 256))
                for dz in range(3)
            ],
            axis=1,
        )
        lines = dot(left[...], jnp.concatenate([hot, hot], axis=0))
        hits = [row == y for y in (jnp.where(cell_y == 0, 65, cell_y - 1), cell_y, cell_y + 1)]
        rows = []
        for step in range(2):
            for dx in range(2):
                t = 2 * step + dx
                for dy in range(3):
                    for dz in range(3):
                        line = lines[t * READ : (t + 1) * READ, dz * 128 : (dz + 1) * 128]
                        rows.append(
                            jnp.sum(jnp.where(hits[dy], line, 0.0), axis=0, keepdims=True)
                        )
            rows.append(jnp.zeros((KROWS - STEN, 128), F32))
        values[pair] = jnp.concatenate(rows, axis=0)
        return carry

    lax.fori_loop(0, 8, read, 0, unroll=True)
    blocks = []
    for j in range(16):
        blocks.append(values[j // 2][:, (j % 2) * 64 : (j % 2 + 1) * 64])
    write_owner_rows(jnp.concatenate(blocks, axis=0), out)


BY_PRODUCT = 6


def potential_kernel(recv, where, weight, out, turned, left):
    read_owner_rows(recv, turned)
    for high in range(4):
        block = jnp.concatenate(
            [turned[(4 * low + high) * ROWS : (4 * low + high + 1) * ROWS, :] for low in range(4)],
            axis=1,
        )
        left[high * 2 * ROWS : (high + 1) * 2 * ROWS, :] = halves(block)
    boxes = [
        jnp.concatenate(
            [
                turned[(2 * tile) * ROWS : (2 * tile + 1) * ROWS, :],
                turned[(2 * tile + 1) * ROWS : (2 * tile + 2) * ROWS, :],
            ],
            axis=1,
        )
        for tile in range(8)
    ]
    lows = where[:64]
    highs = where[64:]
    lanes = (highs & 1) * 64 + (lows & 63)
    tiles = (lows >> 6) * 2 + (highs >> 1)
    row_b = rows_bf16((256, BY_PRODUCT * 128), 0)

    def put(picked, at):
        terms = picked * doubled(weight[:, at])
        for step in range(2):
            out[step : step + 1, at] = jnp.sum(
                terms[step * KROWS : (step + 1) * KROWS], axis=0, keepdims=True
            )

    for first in range(0, 64, 8):
        pages = range(first, first + BY_PRODUCT)
        low = jnp.concatenate([lows[page : page + 1, :] for page in pages], axis=1)
        high = jnp.concatenate([highs[page : page + 1, :] for page in pages], axis=1)
        lines = dot(left[...], one_hot(row_b == wide(low, 256)))
        for page in range(first + BY_PRODUCT, first + 8):
            lane = jnp.broadcast_to(lanes[page : page + 1, :], (ROWS, 128))
            tile = tiles[page : page + 1, :]
            picked = jnp.take_along_axis(boxes[0], lane, axis=1)
            for other in range(1, 8):
                picked = jnp.where(
                    tile == other, jnp.take_along_axis(boxes[other], lane, axis=1), picked
                )
            put(picked, slice(page * 128, page * 128 + 128))
        picked = lines[: 2 * ROWS]
        for quarter in range(1, 4):
            at_row = quarter * 2 * ROWS
            picked = jnp.where(high == quarter, lines[at_row : at_row + 2 * ROWS], picked)
        put(picked[:ROWS] + picked[ROWS:], slice(first * 128, (first + BY_PRODUCT) * 128))


PARAMS = pltpu.CompilerParams(vmem_limit_bytes=48 * 1024 * 1024)


def f32(*shape):
    return jax.ShapeDtypeStruct(shape, F32)


def i32(*shape):
    return jax.ShapeDtypeStruct(shape, jnp.int32)


def run_panels(source, weight, slots, count, cell):
    return pl.pallas_call(
        panels_kernel,
        out_shape=(f32(64 * WIDTH, 128), i32(128, 128)),
        in_specs=[pl.BlockSpec(memory_space=pltpu.HBM)] * 5,
        scratch_shapes=[
            pltpu.VMEM((2, PDEV), F32),
            pltpu.VMEM((STEN, PDEV), F32),
            pltpu.VMEM((16, BOXES), jnp.int32),
            pltpu.VMEM((1, BOXES), jnp.int32),
            pltpu.VMEM((1, BOXES), jnp.int32),
            pltpu.VMEM((PDEV, 256), BF16),
            pltpu.VMEM((8 * ROWS, PDEV), BF16),
            pltpu.SemaphoreType.DMA((5,)),
        ],
        compiler_params=PARAMS,
        name="panels",
    )(*(pltpu.with_memory_space_constraint(x, pltpu.HBM) for x in (source, weight, slots, count, cell)))


def run_slab(recv, fz, fy):
    return pl.pallas_call(
        slab_kernel,
        out_shape=(f32(512, 128), i32(8, 128)),
        in_specs=[pl.BlockSpec(memory_space=pltpu.VMEM)]
        + [pl.BlockSpec(memory_space=pltpu.HBM)] * 2,
        scratch_shapes=[
            pltpu.VMEM((384, 256), BF16),
            pltpu.VMEM((2, 128, 384), BF16),
            pltpu.VMEM((16 * ROWS, 64), F32),
            pltpu.VMEM((2, 8, ROWS, 128), F32),
            pltpu.VMEM((4 * HALF, 3 * BOXES), BF16),
            pltpu.VMEM((4 * HALF, 3 * BOXES), BF16),
            pltpu.VMEM((3 * BOXES, 256), BF16),
            pltpu.SemaphoreType.DMA((2,)),
        ],
        compiler_params=PARAMS,
        name="slab",
    )(recv, fz, fy)


def run_column(place, recv, decay, fx, gx, lz, lx):
    return pl.pallas_call(
        column_kernel,
        out_shape=f32(512, 128),
        in_specs=[pl.BlockSpec(memory_space=pltpu.SMEM)]
        + [pl.BlockSpec(memory_space=pltpu.VMEM)] * 6,
        scratch_shapes=[
            pltpu.VMEM((128, 128), F32),
            pltpu.VMEM((272, 256), F32),
            pltpu.VMEM((272, 256), F32),
        ],
        compiler_params=PARAMS,
        name="column",
    )(place, recv, decay, fx, gx, lz, lx)


def run_field(recv, cells, gz, gy, cs):
    return pl.pallas_call(
        field_kernel,
        out_shape=f32(64 * WIDTH, 128),
        scratch_shapes=[pltpu.VMEM((8, ROWS, 128), F32), pltpu.VMEM((4 * READ, 512), BF16)],
        compiler_params=PARAMS,
        name="field",
    )(recv, cells, gz, gy, cs)


def run_potential(recv, where, weight):
    return pl.pallas_call(
        potential_kernel,
        out_shape=f32(2, PDEV),
        scratch_shapes=[pltpu.VMEM((16 * ROWS, 64), F32), pltpu.VMEM((8 * ROWS, 256), BF16)],
        compiler_params=PARAMS,
        name="potential",
    )(recv, where, weight)


def exchange(rows, parts, axes):
    pieces = rows.reshape(parts, 1, rows.size // parts)
    pieces = lax.all_to_all(pieces, axes, split_axis=0, concat_axis=0, tiled=True)
    return pieces.reshape(rows.shape)


def body(panel_source, proj_weight, box_slots, box_count, box_cell, decay):
    table = {name: jnp.asarray(value) for name, value in tables().items()}
    place = jnp.stack([lax.axis_index("tm"), lax.axis_index("grid")]).astype(jnp.int32)
    box_count, place = lax.optimization_barrier((box_count, place))
    out, where = run_panels(
        panel_source, proj_weight, box_slots, box_count.reshape(1, -1), box_cell.reshape(1, -1)
    )
    recv = exchange(out, 64, "grid")
    out, cells = run_slab(recv, table["fz"], table["fy"])
    recv = exchange(out, 512, ("tm", "grid"))
    out = run_column(
        place, recv, decay.reshape(2 * N, N), table["fx"], table["gx"], table["lz"], table["lx"]
    )
    recv = exchange(out, 512, ("tm", "grid"))
    out = run_field(recv, cells, table["gz"], table["gy"], table["cs"])
    recv = exchange(out, 64, "grid")
    return run_potential(recv, where, proj_weight)


def solution(mesh):
    return jax.shard_map(
        body,
        mesh=mesh,
        in_specs=(
            P("tm", "grid"),
            P(None, "grid"),
            P(None, "grid"),
            P("grid"),
            P("grid"),
            P(None, "grid", None),
        ),
        out_specs=P("tm", "grid"),
        check_vma=False,
    )
```

```python
import jax
import jax.numpy as jnp
import ml_dtypes
import numpy as np
from jax import lax
from jax.experimental import pallas as pl
from jax.experimental.pallas import tpu as pltpu
from jax.sharding import PartitionSpec as P

N = 128
STEN = 18
KROWS = 20
CELL_ROW = 18
ROWS = 2 * KROWS
WIDTH = 16 * ROWS // 128
PDEV = 8192
BOXES = 1024
F32 = jnp.float32
BF16 = jnp.bfloat16


def stacked(table, axis):
    table = np.asarray(table, np.float64).astype(np.float32)
    high = table.astype(ml_dtypes.bfloat16)
    low = (table - high.astype(np.float32)).astype(ml_dtypes.bfloat16)
    return np.concatenate([high, high, low], axis=axis)


def angle(rows, cols):
    return 2.0 * np.pi * (np.outer(rows, cols) % N) / N


def tables():
    index = np.arange(N)
    slot = (index // 32) * 16 + index % 16
    imag = (index // 16) % 2 == 1
    ang = angle(index, slot)
    real_z = np.cos(ang)
    imag_z = np.where(slot[None] == 0, np.cos(np.pi * index)[:, None], -np.sin(ang))
    fz = np.concatenate(
        [np.where(imag[None], imag_z, real_z), np.where(imag[None], -real_z, imag_z)], axis=1
    )
    ky = np.concatenate([2 * np.arange(64), 2 * np.arange(64) + 1])
    ay = angle(ky, index)
    fy = np.stack([np.cos(ay), np.sin(ay)])

    grid = np.arange(64)
    fx = np.zeros((2, 2, 64, 2, N))
    gx = np.zeros((2, N, 2, 2, 64))
    for dx in range(2):
        ax = angle(2 * grid + dx, index)
        cos, sin = np.cos(ax), np.sin(ax)
        fx[0, dx, :, 0] = cos
        fx[0, dx, :, 1] = -sin
        fx[1, dx, :, 0] = sin
        fx[1, dx, :, 1] = cos
        gx[0, :, 0, dx] = cos.T / N
        gx[0, :, 1, dx] = sin.T / N
        gx[1, :, 0, dx] = -sin.T / N
        gx[1, :, 1, dx] = cos.T / N
    fx = fx.reshape(256, 256)
    gx = gx.reshape(256, 256)

    weight = np.where(slot == 0, 0.0, 2.0)[:, None] / N
    cz = np.cos(ang.T) * weight
    sz = np.sin(ang.T) * weight
    gz = np.concatenate(
        [np.where(imag[:, None], -sz, cz), np.where(imag[:, None], -cz, -sz)], axis=1
    )
    gy = np.concatenate([np.cos(ay.T), np.sin(ay.T)], axis=1) / N
    self_row = (ky == 0) | (ky == 64)
    pattern = np.where((ky <= 64)[:, None], 1.0, np.cos(np.pi * index)[None])
    c1 = np.where(self_row, 1.0, 2.0)[:, None] * pattern / N
    c2 = np.where(self_row[:, None], np.cos(np.pi * index)[None], 0.0) / N
    c3 = np.where(self_row[:, None], 0.0, -2.0 * pattern) / N
    cs = np.stack([c1, c2, c3]).astype(np.float32)

    lam = 4.0 * np.sin(np.pi * index / N) ** 2
    lz = np.broadcast_to(lam[:, None], (N, N)).astype(np.float32)
    lx = np.broadcast_to(lam[None], (8, N)).astype(np.float32)
    return dict(
        fz=stacked(fz, 0), fy=stacked(fy, 2), fx=stacked(fx, 0), gx=stacked(gx, 0),
        gz=stacked(gz, 0), gy=stacked(gy, 1),
        cs=cs, lz=lz, lx=lx,
    )


def split(values):
    high = values.astype(BF16)
    return high, (values - high.astype(F32)).astype(BF16)


def halves(values):
    high = values.astype(BF16).astype(F32)
    return jnp.concatenate([high, values - high], axis=0).astype(BF16)


def doubled(tile):
    tile = jnp.concatenate([tile, jnp.zeros((KROWS - STEN, tile.shape[1]), F32)], axis=0)
    return jnp.concatenate([tile, tile], axis=0)


def dot(left, right):
    return lax.dot_general(left, right, (((1,), (0,)), ((), ())), preferred_element_type=F32)


def dot_nt(left, right):
    return lax.dot_general(left, right, (((1,), (1,)), ((), ())), preferred_element_type=F32)


def dot_right(values, table):
    high, low = split(values)
    return dot(jnp.concatenate([high, low, high], axis=1), table[...])


def dot_left(table, values):
    high, low = split(values)
    return dot(table, jnp.concatenate([high, low, high], axis=0))


def iota(shape, axis):
    return lax.broadcasted_iota(jnp.int32, shape, axis)


def rows_bf16(shape, axis):
    return iota(shape, axis).astype(F32).astype(BF16)


def wide(row, size):
    sixteen = jnp.broadcast_to(row.astype(F32), (16, row.shape[1])).astype(BF16)
    return jnp.concatenate([sixteen] * (size // 16), axis=0)


def one_hot(mask):
    return jnp.where(mask, jnp.ones((), BF16), jnp.zeros((), BF16))


def write_owner_rows(turned, out_ref):
    for part in range(WIDTH):
        out_ref[pl.ds(part, 64, stride=WIDTH), :] = turned[part * 128 : (part + 1) * 128, :].T


def read_owner_rows(in_ref, turned_ref):
    for part in range(WIDTH):
        turned_ref[part * 128 : (part + 1) * 128, :] = in_ref[pl.ds(part, 64, stride=WIDTH), :].T


PAGES = 8


def panels_kernel(
    source_hbm, weight_hbm, slots_hbm, count_hbm, cell_hbm, out, where,
    source, weight, slots, count, cell, oh_ref, left_ref, sems,
):
    pairs = (
        (slots_hbm, slots), (count_hbm, count), (cell_hbm, cell), (weight_hbm, weight),
        (source_hbm, source),
    )
    copies = [pltpu.make_async_copy(a, b, sems.at[i]) for i, (a, b) in enumerate(pairs)]
    for copy in copies:
        copy.start()
    copies[0].wait()
    copies[1].wait()
    box = iota((1, BOXES), 1)
    low_value = wide(((box >> 2) & 3) * 64 + (box >> 4), 64)
    high_value = wide(box & 3, 64)
    row64 = rows_bf16((64, BOXES), 0)
    row128 = rows_bf16((128, BOXES), 0)
    none = jnp.zeros((), BF16)

    def invert(s, total):
        panel = slots[pl.ds(s, 1), :]
        page = jnp.where(s < count[...], panel >> 7, 200)
        hit = row64 == wide(page, 64)
        left = jnp.concatenate(
            [jnp.where(hit, low_value, none), jnp.where(hit, high_value, none)], axis=0
        )
        return total + dot_nt(left, one_hot(row128 == wide(panel & 127, 128)))

    total = lax.fori_loop(0, 16, invert, jnp.zeros((128, 128), F32), unroll=True)
    where_now = (total + 0.5).astype(jnp.int32)
    where[...] = where_now
    copies[3].wait()
    copies[4].wait()
    lane256 = rows_bf16((128, 256), 1)
    low_columns = where_now[:64].astype(F32).T.astype(BF16)
    first_step = iota((ROWS, 128), 0) < KROWS

    def spread(page):
        at = page * 128
        low = jnp.broadcast_to(low_columns[:, page : page + 1], (128, 256))
        high = wide(where_now[64 + page : 65 + page, :], 2 * ROWS)
        oh_ref[at : at + 128, :] = one_hot(lane256 == low)
        both = doubled(weight[:, at : at + 128]) * jnp.where(
            first_step, source[0:1, at : at + 128], source[1:2, at : at + 128]
        )
        pieces = halves(both)
        for quarter in range(4):
            left_ref[quarter * 2 * ROWS : (quarter + 1) * 2 * ROWS, at : at + 128] = jnp.where(
                high == jnp.full((), quarter, BF16), pieces, none
            )

    sums = jnp.zeros((8 * ROWS, 256), F32)
    for chunk in range(64 // PAGES):
        for page in range(PAGES):
            spread(chunk * PAGES + page)
        at = slice(chunk * PAGES * 128, (chunk + 1) * PAGES * 128)
        sums = sums + dot(left_ref[:, at], oh_ref[at, :])

    copies[2].wait()
    cells = cell[...]
    match = rows_bf16((16, BOXES), 0) == wide(box & 15, 16)
    left = jnp.concatenate(
        [
            jnp.where(match, wide(cells >> 7, 16), none),
            jnp.where(match, wide(cells & 127, 16), none),
        ],
        axis=0,
    )
    owned = dot_nt(left, one_hot(row64 == wide(box >> 4, 64)))
    cell_rows = owned[:16] * 128.0 + owned[16:]

    blocks = []
    at_cell = iota((ROWS, 64), 0) == CELL_ROW
    for j in range(16):
        at = (j % 4) * 2 * ROWS
        block = sums[at : at + 2 * ROWS, (j // 4) * 64 : (j // 4 + 1) * 64]
        block = block[:ROWS] + block[ROWS:]
        blocks.append(jnp.where(at_cell, cell_rows[j : j + 1, :], block))
    write_owner_rows(jnp.concatenate(blocks, axis=0), out)


PAIRS = 2
HALF = 80


def slab_kernel(recv, fz_hbm, fy_hbm, out, cell_out, fz, fy, turned, values, left_h, left_l, right, sems):
    copies = [
        pltpu.make_async_copy(fz_hbm, fz, sems.at[0]),
        pltpu.make_async_copy(fy_hbm, fy, sems.at[1]),
    ]
    for copy in copies:
        copy.start()
    read_owner_rows(recv, turned)
    lane = iota((128, 128), 1)
    row = iota((128, 128), 0)
    row_b = rows_bf16((HALF, 128), 0)
    lane_b = rows_bf16((128, 256), 1)
    none = jnp.zeros((HALF, 128), BF16)
    spots = []
    for pair in range(8):
        value = jnp.concatenate(
            [
                turned[(2 * pair) * ROWS : (2 * pair + 1) * ROWS, :],
                turned[(2 * pair + 1) * ROWS : (2 * pair + 2) * ROWS, :],
            ],
            axis=1,
        )
        high = value.astype(BF16).astype(F32)
        values[0, pair] = high
        values[1, pair] = value - high
        cell = value[CELL_ROW : CELL_ROW + 1, :].astype(jnp.int32)
        cell_out[pair : pair + 1, :] = cell
        for dz in range(3):
            spots.append((cell >> 13) * 128 + ((cell + (dz - 1)) & 127))
    spots = jnp.concatenate(spots, axis=0).astype(F32).T.astype(BF16)

    def fill(pair):
        cell_y = (cell_out[pair : pair + 1, :] >> 7) & 63
        at_y = [jnp.where(cell_y == 0, 65, cell_y - 1), cell_y, cell_y + 1]
        hits = [row_b == wide(y, HALF) for y in at_y]
        for dz in range(3):
            column = pair * 3 + dz
            at = column * 128
            right[at : at + 128, :] = one_hot(
                lane_b == jnp.broadcast_to(spots[:, column : column + 1], (128, 256))
            )
            for step in range(2):
                for dx in range(2):
                    at_row = (2 * step + dx) * HALF
                    for part, target in ((0, left_h), (1, left_l)):
                        block = none
                        for dy in range(3):
                            k = step * KROWS + 9 * dx + 3 * dy + dz
                            block = jnp.where(
                                hits[dy], wide(values[part, pair, k : k + 1, :], HALF), block
                            )
                        target[at_row : at_row + HALF, at : at + 128] = block

    halved = jnp.zeros((4 * HALF, 256), F32)
    for group in range(8 // PAIRS):
        for pair in range(PAIRS):
            fill(PAIRS * group + pair)
        at = slice(group * PAIRS * 384, (group + 1) * PAIRS * 384)
        halved = halved + (dot(left_h[:, at], right[at, :]) + dot(left_l[:, at], right[at, :]))
    row64 = iota((64, 128), 0)
    planes = []
    for t in range(4):
        for half in range(2):
            here = slice(half * 128, half * 128 + 128)
            other = slice(128 - half * 128, 256 - half * 128)
            part = halved[t * HALF : t * HALF + 64, here]
            part = part + jnp.where(
                row64 == 0, halved[t * HALF + 64 : t * HALF + 65, other], 0.0
            )
            part = part + jnp.where(
                row64 == 63, halved[t * HALF + 65 : t * HALF + 66, other], 0.0
            )
            planes.append(part)
    density = jnp.concatenate(planes, axis=0)
    for copy in copies:
        copy.wait()
    both = dot_right(density, fz)

    def beside(at):
        return jnp.concatenate(
            [both[t * 128 : (t + 1) * 128, at : at + 128] for t in range(4)], axis=1
        )

    even = dot_left(fy[0], beside(0))
    odd = dot_left(fy[1], beside(128))
    ky = (row & 63) * 2 + (row >> 6)
    own = (ky == 0) | (ky == 64)
    pencils = []
    for t in range(4):
        a = even[:, t * 128 : (t + 1) * 128]
        b = odd[:, t * 128 : (t + 1) * 128]
        full = a + b
        full = jnp.where(lane == 0, jnp.where(ky <= 64, a, pltpu.roll(a, 112, 1)), full)
        second = jnp.where(own, a, jnp.where(ky < 64, b, -pltpu.roll(b, 16, 1)))
        pencils.append(jnp.where(lane == 16, second, full))
    for q in range(4):
        piece = jnp.concatenate([p[:, q * 32 : (q + 1) * 32] for p in pencils], axis=1)
        out[q * 64 : (q + 1) * 64, :] = piece[:64]
        out[(4 + q) * 64 : (5 + q) * 64, :] = piece[64:]


def column_kernel(place, recv, decay, fx, gx, lz, lx, out, turned_decay, spectra, fields):
    block = place[0]
    column = place[1]
    ky_low = block // 4
    q = block % 4
    ky = 2 * column + ky_low
    special = ((block == 0) & ((column == 0) | (column == 32))).astype(jnp.int32)
    below = iota((16, 128), 1) < 64
    first_row = iota((16, 128), 0) == 0
    mains, extras = [], []
    for mp in range(4):
        part = recv[mp * 128 : (mp + 1) * 128, :].T
        for half in range(2):
            for n in range(2):
                pieces = []
                for ri in range(2):
                    near = part[(2 * n) * 32 + ri * 16 : (2 * n) * 32 + ri * 16 + 16, :]
                    far = part[(2 * n + 1) * 32 + ri * 16 : (2 * n + 1) * 32 + ri * 16 + 16, :]
                    if half == 0:
                        far = pltpu.roll(far, 64, 1)
                    else:
                        near = pltpu.roll(near, 64, 1)
                    pieces.append(jnp.where(below, near, far))
                extras.append(jnp.where(special == 1, pieces[1][0:1], 0.0))
                pieces[1] = jnp.where(first_row & (special == 1), 0.0, pieces[1])
                mains.append(jnp.concatenate(pieces, axis=1))
    extra = jnp.concatenate(extras, axis=0)
    mains.append(jnp.concatenate([extra, jnp.zeros_like(extra)], axis=1))
    spectra[...] = dot_right(jnp.concatenate(mains, axis=0), fx)

    here = jnp.where(
        ky_low == 1, decay[pl.ds(1, 128, stride=2), :], decay[pl.ds(0, 128, stride=2), :]
    )
    turned_decay[...] = here.T
    slots_at = pl.multiple_of(q * 16, 16)
    moved = jnp.where((q == 0) & (ky > 64), 1, 0)
    at_first = iota((16, 128), 0) + (1 - moved) == 0
    damp_last = turned_decay[64:65, :]
    damp_main = jnp.where(at_first, damp_last, turned_decay[pl.ds(slots_at, 16), :])
    lam_xy = lx[0:1, :] + lz[pl.ds(ky, 1), :]
    lam_main = lam_xy + jnp.where(at_first, lz[64:65, :], lz[pl.ds(slots_at, 16), :])
    lam_last = lam_xy + lz[64:65, :]

    for damp, lam, base, size in ((damp_main, lam_main, 0, 16), (damp_last, lam_last, 256, 1)):
        theta = 0.5 * jnp.sqrt(lam)
        rate_cos = damp * jnp.cos(theta)
        rate_sin = damp * jnp.sin(theta)
        kernel = 1.0 / (1.0 + lam)
        state = [[jnp.zeros_like(lam)] * 2 for _ in range(2)]
        for step in range(16):
            at_row = base + step * size
            for ri in range(2):
                at = ri * 128
                re, im = state[ri]
                state[ri] = [
                    rate_cos * re - rate_sin * im + spectra[at_row : at_row + size, at : at + 128],
                    rate_cos * im + rate_sin * re,
                ]
                fields[at_row : at_row + size, at : at + 128] = kernel * state[ri][0]
    back = dot_right(fields[...], gx)
    for mp in range(4):
        rows = []
        for n in range(2):
            steps = [4 * mp + 2 * half + n for half in range(2)]
            pieces = []
            for ri in range(2):
                both = []
                for step in steps:
                    piece = back[step * 16 : step * 16 + 16, ri * 128 : ri * 128 + 128]
                    if ri == 1:
                        added = back[256 + step : 257 + step, 0:128]
                        piece = piece + jnp.where(first_row, added, 0.0)
                    both.append(piece)
                pieces.append(
                    (
                        jnp.where(below, both[0], pltpu.roll(both[1], 64, 1)),
                        jnp.where(below, pltpu.roll(both[0], 64, 1), both[1]),
                    )
                )
            for dx in range(2):
                for ri in range(2):
                    rows.append(pieces[ri][dx])
        out[mp * 128 : (mp + 1) * 128, :] = jnp.concatenate(rows, axis=0).T


READ = 72
BY_GATHER = (1, 3, 6)


def field_kernel(recv, cells, gz, gy, cs, out, left):
    pencils = []
    for t in range(4):
        halves_y = [
            jnp.concatenate(
                [
                    recv[(4 * low + q) * 64 : (4 * low + q + 1) * 64, :][:, t * 32 : (t + 1) * 32]
                    for q in range(4)
                ],
                axis=1,
            )
            for low in range(2)
        ]
        pencils.append(jnp.concatenate(halves_y, axis=0))
    both = dot_right(jnp.concatenate(pencils, axis=0), gz)
    tops, bottoms = [], []
    for t in range(4):
        real = pencils[t][:, 0:1]
        imag = pencils[t][:, 16:17]
        tops.append(both[t * 128 : (t + 1) * 128, :128] + (real * cs[0] + imag * cs[1]))
        bottoms.append(both[t * 128 : (t + 1) * 128, 128:] + imag * cs[2])
    tall = jnp.concatenate(
        [jnp.concatenate(tops, axis=1), jnp.concatenate(bottoms, axis=1)], axis=0
    )
    field = dot_left(gy[...], tall)
    rows = []
    for t in range(4):
        plane = field[:, t * 128 : (t + 1) * 128]
        tops = jnp.concatenate([plane[:64], plane[64:]], axis=1)
        after = jnp.concatenate([plane[64:65], plane[0:1]], axis=1)
        before = jnp.concatenate([plane[127:128], plane[63:64]], axis=1)
        rows += [tops, after, before, jnp.zeros((READ - 66, 256), F32)]
    table = jnp.concatenate(rows, axis=0)
    left[...] = jnp.concatenate(split(table), axis=1)
    row = iota((READ, 128), 0)
    row_b = rows_bf16((256, 128), 0)

    def read(pair):
        cell = cells[pair : pair + 1, :]
        cell_y = (cell >> 7) & 63
        gathered = (1,) if pair in BY_GATHER else ()
        products = [dz for dz in range(3) if dz not in gathered]
        hot = jnp.concatenate(
            [
                one_hot(row_b == wide((cell >> 13) * 128 + ((cell + (dz - 1)) & 127), 256))
                for dz in products
            ],
            axis=1,
        )
        lines = dot(left[...], jnp.concatenate([hot, hot], axis=0))
        columns = [None] * 3
        for place, dz in enumerate(products):
            columns[dz] = lines[:, place * 128 : (place + 1) * 128]
        for dz in gathered:
            lane = jnp.broadcast_to((cell + (dz - 1)) & 127, (4 * READ, 128))
            columns[dz] = jnp.where(
                (cell >> 13) == 1,
                jnp.take_along_axis(table[:, 128:], lane, axis=1),
                jnp.take_along_axis(table[:, :128], lane, axis=1),
            )
        hits = [row == y for y in (jnp.where(cell_y == 0, 65, cell_y - 1), cell_y, cell_y + 1)]
        rows = []
        for step in range(2):
            for dx in range(2):
                t = 2 * step + dx
                for dy in range(3):
                    for dz in range(3):
                        line = columns[dz][t * READ : (t + 1) * READ, :]
                        rows.append(
                            jnp.sum(jnp.where(hits[dy], line, 0.0), axis=0, keepdims=True)
                        )
            rows.append(jnp.zeros((KROWS - STEN, 128), F32))
        return jnp.concatenate(rows, axis=0)

    values = [read(pair) for pair in range(8)]
    blocks = []
    for j in range(16):
        blocks.append(values[j // 2][:, (j % 2) * 64 : (j % 2 + 1) * 64])
    write_owner_rows(jnp.concatenate(blocks, axis=0), out)


BY_PRODUCT = 6


def potential_kernel(recv, where, weight, out, turned, left):
    read_owner_rows(recv, turned)
    for high in range(4):
        block = jnp.concatenate(
            [turned[(4 * low + high) * ROWS : (4 * low + high + 1) * ROWS, :] for low in range(4)],
            axis=1,
        )
        left[high * 2 * ROWS : (high + 1) * 2 * ROWS, :] = halves(block)
    boxes = [
        jnp.concatenate(
            [
                turned[(2 * tile) * ROWS : (2 * tile + 1) * ROWS, :],
                turned[(2 * tile + 1) * ROWS : (2 * tile + 2) * ROWS, :],
            ],
            axis=1,
        )
        for tile in range(8)
    ]
    lows = where[:64]
    highs = where[64:]
    lanes = (highs & 1) * 64 + (lows & 63)
    tiles = (lows >> 6) * 2 + (highs >> 1)
    row_b = rows_bf16((256, BY_PRODUCT * 128), 0)

    def put(picked, at):
        terms = picked * doubled(weight[:, at])
        for step in range(2):
            out[step : step + 1, at] = jnp.sum(
                terms[step * KROWS : (step + 1) * KROWS], axis=0, keepdims=True
            )

    for first in range(0, 64, 8):
        pages = range(first, first + BY_PRODUCT)
        low = jnp.concatenate([lows[page : page + 1, :] for page in pages], axis=1)
        high = jnp.concatenate([highs[page : page + 1, :] for page in pages], axis=1)
        lines = dot(left[...], one_hot(row_b == wide(low, 256)))
        for page in range(first + BY_PRODUCT, first + 8):
            lane = jnp.broadcast_to(lanes[page : page + 1, :], (ROWS, 128))
            tile = tiles[page : page + 1, :]
            picked = jnp.take_along_axis(boxes[0], lane, axis=1)
            for other in range(1, 8):
                picked = jnp.where(
                    tile == other, jnp.take_along_axis(boxes[other], lane, axis=1), picked
                )
            put(picked, slice(page * 128, page * 128 + 128))
        picked = lines[: 2 * ROWS]
        for quarter in range(1, 4):
            at_row = quarter * 2 * ROWS
            picked = jnp.where(high == quarter, lines[at_row : at_row + 2 * ROWS], picked)
        put(picked[:ROWS] + picked[ROWS:], slice(first * 128, (first + BY_PRODUCT) * 128))


PARAMS = pltpu.CompilerParams(vmem_limit_bytes=48 * 1024 * 1024)


def f32(*shape):
    return jax.ShapeDtypeStruct(shape, F32)


def i32(*shape):
    return jax.ShapeDtypeStruct(shape, jnp.int32)


def run_panels(source, weight, slots, count, cell):
    return pl.pallas_call(
        panels_kernel,
        out_shape=(f32(64 * WIDTH, 128), i32(128, 128)),
        in_specs=[pl.BlockSpec(memory_space=pltpu.HBM)] * 5,
        scratch_shapes=[
            pltpu.VMEM((2, PDEV), F32),
            pltpu.VMEM((STEN, PDEV), F32),
            pltpu.VMEM((16, BOXES), jnp.int32),
            pltpu.VMEM((1, BOXES), jnp.int32),
            pltpu.VMEM((1, BOXES), jnp.int32),
            pltpu.VMEM((PDEV, 256), BF16),
            pltpu.VMEM((8 * ROWS, PDEV), BF16),
            pltpu.SemaphoreType.DMA((5,)),
        ],
        compiler_params=PARAMS,
        name="panels",
    )(*(pltpu.with_memory_space_constraint(x, pltpu.HBM) for x in (source, weight, slots, count, cell)))


def run_slab(recv, fz, fy):
    return pl.pallas_call(
        slab_kernel,
        out_shape=(f32(512, 128), i32(8, 128)),
        in_specs=[pl.BlockSpec(memory_space=pltpu.VMEM)]
        + [pl.BlockSpec(memory_space=pltpu.HBM)] * 2,
        scratch_shapes=[
            pltpu.VMEM((384, 256), BF16),
            pltpu.VMEM((2, 128, 384), BF16),
            pltpu.VMEM((16 * ROWS, 64), F32),
            pltpu.VMEM((2, 8, ROWS, 128), F32),
            pltpu.VMEM((4 * HALF, 3 * BOXES), BF16),
            pltpu.VMEM((4 * HALF, 3 * BOXES), BF16),
            pltpu.VMEM((3 * BOXES, 256), BF16),
            pltpu.SemaphoreType.DMA((2,)),
        ],
        compiler_params=PARAMS,
        name="slab",
    )(recv, fz, fy)


def run_column(place, recv, decay, fx, gx, lz, lx):
    return pl.pallas_call(
        column_kernel,
        out_shape=f32(512, 128),
        in_specs=[pl.BlockSpec(memory_space=pltpu.SMEM)]
        + [pl.BlockSpec(memory_space=pltpu.VMEM)] * 6,
        scratch_shapes=[
            pltpu.VMEM((128, 128), F32),
            pltpu.VMEM((272, 256), F32),
            pltpu.VMEM((272, 256), F32),
        ],
        compiler_params=PARAMS,
        name="column",
    )(place, recv, decay, fx, gx, lz, lx)


def run_field(recv, cells, gz, gy, cs):
    return pl.pallas_call(
        field_kernel,
        out_shape=f32(64 * WIDTH, 128),
        scratch_shapes=[pltpu.VMEM((4 * READ, 512), BF16)],
        compiler_params=PARAMS,
        name="field",
    )(recv, cells, gz, gy, cs)


def run_potential(recv, where, weight):
    return pl.pallas_call(
        potential_kernel,
        out_shape=f32(2, PDEV),
        scratch_shapes=[pltpu.VMEM((16 * ROWS, 64), F32), pltpu.VMEM((8 * ROWS, 256), BF16)],
        compiler_params=PARAMS,
        name="potential",
    )(recv, where, weight)


def exchange(rows, parts, axes):
    pieces = rows.reshape(parts, 1, rows.size // parts)
    pieces = lax.all_to_all(pieces, axes, split_axis=0, concat_axis=0, tiled=True)
    return pieces.reshape(rows.shape)


def body(panel_source, proj_weight, box_slots, box_count, box_cell, decay):
    table = {name: jnp.asarray(value) for name, value in tables().items()}
    place = jnp.stack([lax.axis_index("tm"), lax.axis_index("grid")]).astype(jnp.int32)
    box_count, place = lax.optimization_barrier((box_count, place))
    out, where = run_panels(
        panel_source, proj_weight, box_slots, box_count.reshape(1, -1), box_cell.reshape(1, -1)
    )
    recv = exchange(out, 64, "grid")
    out, cells = run_slab(recv, table["fz"], table["fy"])
    recv = exchange(out, 512, ("tm", "grid"))
    out = run_column(
        place, recv, decay.reshape(2 * N, N), table["fx"], table["gx"], table["lz"], table["lx"]
    )
    recv = exchange(out, 512, ("tm", "grid"))
    out = run_field(recv, cells, table["gz"], table["gy"], table["cs"])
    recv = exchange(out, 64, "grid")
    return run_potential(recv, where, proj_weight)


def solution(mesh):
    return jax.shard_map(
        body,
        mesh=mesh,
        in_specs=(
            P("tm", "grid"),
            P(None, "grid"),
            P(None, "grid"),
            P("grid"),
            P("grid"),
            P(None, "grid", None),
        ),
        out_specs=P("tm", "grid"),
        check_vma=False,
    )
```

```python
import jax
import jax.numpy as jnp
import ml_dtypes
import numpy as np
from jax import lax
from jax.experimental import pallas as pl
from jax.experimental.pallas import tpu as pltpu
from jax.sharding import PartitionSpec as P

N = 128
STEN = 18
KROWS = 20
CELL_ROW = 18
ROWS = 2 * KROWS
WIDTH = 16 * ROWS // 128
PDEV = 8192
BOXES = 1024
F32 = jnp.float32
BF16 = jnp.bfloat16


def stacked(table, axis):
    table = np.asarray(table, np.float64).astype(np.float32)
    high = table.astype(ml_dtypes.bfloat16)
    low = (table - high.astype(np.float32)).astype(ml_dtypes.bfloat16)
    return np.concatenate([high, high, low], axis=axis)


def angle(rows, cols):
    return 2.0 * np.pi * (np.outer(rows, cols) % N) / N


def tables():
    index = np.arange(N)
    slot = (index // 32) * 16 + index % 16
    imag = (index // 16) % 2 == 1
    ang = angle(index, slot)
    real_z = np.cos(ang)
    imag_z = np.where(slot[None] == 0, np.cos(np.pi * index)[:, None], -np.sin(ang))
    fz = np.concatenate(
        [np.where(imag[None], imag_z, real_z), np.where(imag[None], -real_z, imag_z)], axis=1
    )
    ky = np.concatenate([2 * np.arange(64), 2 * np.arange(64) + 1])
    ay = angle(ky, index)
    fy = np.stack([np.cos(ay), np.sin(ay)])

    grid = np.arange(64)
    fx = np.zeros((2, 2, 64, 2, N))
    gx = np.zeros((2, N, 2, 2, 64))
    for dx in range(2):
        ax = angle(2 * grid + dx, index)
        cos, sin = np.cos(ax), np.sin(ax)
        fx[0, dx, :, 0] = cos
        fx[0, dx, :, 1] = -sin
        fx[1, dx, :, 0] = sin
        fx[1, dx, :, 1] = cos
        gx[0, :, 0, dx] = cos.T / N
        gx[0, :, 1, dx] = sin.T / N
        gx[1, :, 0, dx] = -sin.T / N
        gx[1, :, 1, dx] = cos.T / N
    fx = fx.reshape(256, 256)
    gx = gx.reshape(256, 256)

    weight = np.where(slot == 0, 0.0, 2.0)[:, None] / N
    cz = np.cos(ang.T) * weight
    sz = np.sin(ang.T) * weight
    gz = np.concatenate(
        [np.where(imag[:, None], -sz, cz), np.where(imag[:, None], -cz, -sz)], axis=1
    )
    gy = np.concatenate([np.cos(ay.T), np.sin(ay.T)], axis=1) / N
    self_row = (ky == 0) | (ky == 64)
    pattern = np.where((ky <= 64)[:, None], 1.0, np.cos(np.pi * index)[None])
    c1 = np.where(self_row, 1.0, 2.0)[:, None] * pattern / N
    c2 = np.where(self_row[:, None], np.cos(np.pi * index)[None], 0.0) / N
    c3 = np.where(self_row[:, None], 0.0, -2.0 * pattern) / N
    cs = np.stack([c1, c2, c3]).astype(np.float32)

    lam = 4.0 * np.sin(np.pi * index / N) ** 2
    lz = np.broadcast_to(lam[:, None], (N, N)).astype(np.float32)
    lx = np.broadcast_to(lam[None], (8, N)).astype(np.float32)
    return dict(
        fz=stacked(fz, 0), fy=stacked(fy, 2), fx=stacked(fx, 0), gx=stacked(gx, 0),
        gz=stacked(gz, 0), gy=stacked(gy, 1),
        cs=cs, lz=lz, lx=lx,
    )


def split(values):
    high = values.astype(BF16)
    return high, (values - high.astype(F32)).astype(BF16)


def halves(values):
    high = values.astype(BF16).astype(F32)
    return jnp.concatenate([high, values - high], axis=0).astype(BF16)


def doubled(tile):
    tile = jnp.concatenate([tile, jnp.zeros((KROWS - STEN, tile.shape[1]), F32)], axis=0)
    return jnp.concatenate([tile, tile], axis=0)


def dot(left, right):
    return lax.dot_general(left, right, (((1,), (0,)), ((), ())), preferred_element_type=F32)


def dot_nt(left, right):
    return lax.dot_general(left, right, (((1,), (1,)), ((), ())), preferred_element_type=F32)


def dot_right(values, table):
    high, low = split(values)
    return dot(jnp.concatenate([high, low, high], axis=1), table[...])


def dot_left(table, values):
    high, low = split(values)
    return dot(table, jnp.concatenate([high, low, high], axis=0))


def iota(shape, axis):
    return lax.broadcasted_iota(jnp.int32, shape, axis)


def rows_bf16(shape, axis):
    return iota(shape, axis).astype(F32).astype(BF16)


def wide(row, size):
    sixteen = jnp.broadcast_to(row.astype(F32), (16, row.shape[1])).astype(BF16)
    return jnp.concatenate([sixteen] * (size // 16), axis=0)


def one_hot(mask):
    return jnp.where(mask, jnp.ones((), BF16), jnp.zeros((), BF16))


def write_owner_rows(turned, out_ref):
    for part in range(WIDTH):
        out_ref[pl.ds(part, 64, stride=WIDTH), :] = turned[part * 128 : (part + 1) * 128, :].T


def read_owner_rows(in_ref, turned_ref):
    for part in range(WIDTH):
        turned_ref[part * 128 : (part + 1) * 128, :] = in_ref[pl.ds(part, 64, stride=WIDTH), :].T


PAGES = 8


def panels_kernel(
    source_hbm, weight_hbm, slots_hbm, count_hbm, cell_hbm, out, where,
    source, weight, slots, count, cell, oh_ref, left_ref, sems,
):
    pairs = (
        (slots_hbm, slots), (count_hbm, count), (cell_hbm, cell), (weight_hbm, weight),
        (source_hbm, source),
    )
    copies = [pltpu.make_async_copy(a, b, sems.at[i]) for i, (a, b) in enumerate(pairs)]
    for copy in copies:
        copy.start()
    copies[0].wait()
    copies[1].wait()
    box = iota((1, BOXES), 1)
    low_value = wide(((box >> 2) & 3) * 64 + (box >> 4), 64)
    high_value = wide(box & 3, 64)
    row64 = rows_bf16((64, BOXES), 0)
    row128 = rows_bf16((128, BOXES), 0)
    none = jnp.zeros((), BF16)

    def invert(s, total):
        panel = slots[pl.ds(s, 1), :]
        page = jnp.where(s < count[...], panel >> 7, 200)
        hit = row64 == wide(page, 64)
        left = jnp.concatenate(
            [jnp.where(hit, low_value, none), jnp.where(hit, high_value, none)], axis=0
        )
        return total + dot_nt(left, one_hot(row128 == wide(panel & 127, 128)))

    total = lax.fori_loop(0, 16, invert, jnp.zeros((128, 128), F32), unroll=True)
    where_now = (total + 0.5).astype(jnp.int32)
    where[...] = where_now
    copies[3].wait()
    copies[4].wait()
    lane256 = rows_bf16((128, 256), 1)
    low_columns = where_now[:64].astype(F32).T.astype(BF16)
    first_step = iota((ROWS, 128), 0) < KROWS

    def spread(page):
        at = page * 128
        low = jnp.broadcast_to(low_columns[:, page : page + 1], (128, 256))
        high = wide(where_now[64 + page : 65 + page, :], 2 * ROWS)
        oh_ref[at : at + 128, :] = one_hot(lane256 == low)
        both = doubled(weight[:, at : at + 128]) * jnp.where(
            first_step, source[0:1, at : at + 128], source[1:2, at : at + 128]
        )
        pieces = halves(both)
        for quarter in range(4):
            left_ref[quarter * 2 * ROWS : (quarter + 1) * 2 * ROWS, at : at + 128] = jnp.where(
                high == jnp.full((), quarter, BF16), pieces, none
            )

    sums = jnp.zeros((8 * ROWS, 256), F32)
    for chunk in range(64 // PAGES):
        for page in range(PAGES):
            spread(chunk * PAGES + page)
        at = slice(chunk * PAGES * 128, (chunk + 1) * PAGES * 128)
        sums = sums + dot(left_ref[:, at], oh_ref[at, :])

    copies[2].wait()
    cells = cell[...]
    match = rows_bf16((16, BOXES), 0) == wide(box & 15, 16)
    left = jnp.concatenate(
        [
            jnp.where(match, wide(cells >> 7, 16), none),
            jnp.where(match, wide(cells & 127, 16), none),
        ],
        axis=0,
    )
    owned = dot_nt(left, one_hot(row64 == wide(box >> 4, 64)))
    cell_rows = owned[:16] * 128.0 + owned[16:]

    blocks = []
    at_cell = iota((ROWS, 64), 0) == CELL_ROW
    for j in range(16):
        at = (j % 4) * 2 * ROWS
        block = sums[at : at + 2 * ROWS, (j // 4) * 64 : (j // 4 + 1) * 64]
        block = block[:ROWS] + block[ROWS:]
        blocks.append(jnp.where(at_cell, cell_rows[j : j + 1, :], block))
    write_owner_rows(jnp.concatenate(blocks, axis=0), out)


PAIRS = 2
HALF = 80


def slab_kernel(recv, fz, fy, out, cell_out, turned, values, left_h, left_l, right):
    read_owner_rows(recv, turned)
    lane = iota((128, 128), 1)
    row = iota((128, 128), 0)
    row_b = rows_bf16((HALF, 128), 0)
    lane_b = rows_bf16((128, 256), 1)
    none = jnp.zeros((HALF, 128), BF16)
    spots = []
    for pair in range(8):
        value = jnp.concatenate(
            [
                turned[(2 * pair) * ROWS : (2 * pair + 1) * ROWS, :],
                turned[(2 * pair + 1) * ROWS : (2 * pair + 2) * ROWS, :],
            ],
            axis=1,
        )
        high = value.astype(BF16).astype(F32)
        values[0, pair] = high
        values[1, pair] = value - high
        cell = value[CELL_ROW : CELL_ROW + 1, :].astype(jnp.int32)
        cell_out[pair : pair + 1, :] = cell
        for dz in range(3):
            spots.append((cell >> 13) * 128 + ((cell + (dz - 1)) & 127))
    spots = jnp.concatenate(spots, axis=0).astype(F32).T.astype(BF16)

    def fill(pair):
        cell_y = (cell_out[pair : pair + 1, :] >> 7) & 63
        at_y = [jnp.where(cell_y == 0, 65, cell_y - 1), cell_y, cell_y + 1]
        hits = [row_b == wide(y, HALF) for y in at_y]
        for dz in range(3):
            column = pair * 3 + dz
            at = column * 128
            right[at : at + 128, :] = one_hot(
                lane_b == jnp.broadcast_to(spots[:, column : column + 1], (128, 256))
            )
            for step in range(2):
                for dx in range(2):
                    at_row = (2 * step + dx) * HALF
                    for part, target in ((0, left_h), (1, left_l)):
                        block = none
                        for dy in range(3):
                            k = step * KROWS + 9 * dx + 3 * dy + dz
                            block = jnp.where(
                                hits[dy], wide(values[part, pair, k : k + 1, :], HALF), block
                            )
                        target[at_row : at_row + HALF, at : at + 128] = block

    halved = jnp.zeros((4 * HALF, 256), F32)
    for group in range(8 // PAIRS):
        for pair in range(PAIRS):
            fill(PAIRS * group + pair)
        at = slice(group * PAIRS * 384, (group + 1) * PAIRS * 384)
        halved = halved + (dot(left_h[:, at], right[at, :]) + dot(left_l[:, at], right[at, :]))
    row64 = iota((64, 128), 0)
    planes = []
    for t in range(4):
        for half in range(2):
            here = slice(half * 128, half * 128 + 128)
            other = slice(128 - half * 128, 256 - half * 128)
            part = halved[t * HALF : t * HALF + 64, here]
            part = part + jnp.where(
                row64 == 0, halved[t * HALF + 64 : t * HALF + 65, other], 0.0
            )
            part = part + jnp.where(
                row64 == 63, halved[t * HALF + 65 : t * HALF + 66, other], 0.0
            )
            planes.append(part)
    density = jnp.concatenate(planes, axis=0)
    both = dot_right(density, fz)

    def beside(at):
        return jnp.concatenate(
            [both[t * 128 : (t + 1) * 128, at : at + 128] for t in range(4)], axis=1
        )

    even = dot_left(fy[0], beside(0))
    odd = dot_left(fy[1], beside(128))
    ky = (row & 63) * 2 + (row >> 6)
    own = (ky == 0) | (ky == 64)
    pencils = []
    for t in range(4):
        a = even[:, t * 128 : (t + 1) * 128]
        b = odd[:, t * 128 : (t + 1) * 128]
        full = a + b
        full = jnp.where(lane == 0, jnp.where(ky <= 64, a, pltpu.roll(a, 112, 1)), full)
        second = jnp.where(own, a, jnp.where(ky < 64, b, -pltpu.roll(b, 16, 1)))
        pencils.append(jnp.where(lane == 16, second, full))
    for q in range(4):
        piece = jnp.concatenate([p[:, q * 32 : (q + 1) * 32] for p in pencils], axis=1)
        out[q * 64 : (q + 1) * 64, :] = piece[:64]
        out[(4 + q) * 64 : (5 + q) * 64, :] = piece[64:]


def column_kernel(place, recv, decay, fx, gx, lz, lx, out, turned_decay, spectra, fields):
    block = place[0]
    column = place[1]
    ky_low = block // 4
    q = block % 4
    ky = 2 * column + ky_low
    special = ((block == 0) & ((column == 0) | (column == 32))).astype(jnp.int32)
    below = iota((16, 128), 1) < 64
    first_row = iota((16, 128), 0) == 0
    mains, extras = [], []
    for mp in range(4):
        part = recv[mp * 128 : (mp + 1) * 128, :].T
        for half in range(2):
            for n in range(2):
                pieces = []
                for ri in range(2):
                    near = part[(2 * n) * 32 + ri * 16 : (2 * n) * 32 + ri * 16 + 16, :]
                    far = part[(2 * n + 1) * 32 + ri * 16 : (2 * n + 1) * 32 + ri * 16 + 16, :]
                    if half == 0:
                        far = pltpu.roll(far, 64, 1)
                    else:
                        near = pltpu.roll(near, 64, 1)
                    pieces.append(jnp.where(below, near, far))
                extras.append(jnp.where(special == 1, pieces[1][0:1], 0.0))
                pieces[1] = jnp.where(first_row & (special == 1), 0.0, pieces[1])
                mains.append(jnp.concatenate(pieces, axis=1))
    extra = jnp.concatenate(extras, axis=0)
    mains.append(jnp.concatenate([extra, jnp.zeros_like(extra)], axis=1))
    spectra[...] = dot_right(jnp.concatenate(mains, axis=0), fx)

    here = jnp.where(
        ky_low == 1, decay[pl.ds(1, 128, stride=2), :], decay[pl.ds(0, 128, stride=2), :]
    )
    turned_decay[...] = here.T
    slots_at = pl.multiple_of(q * 16, 16)
    moved = jnp.where((q == 0) & (ky > 64), 1, 0)
    at_first = iota((16, 128), 0) + (1 - moved) == 0
    damp_last = turned_decay[64:65, :]
    damp_main = jnp.where(at_first, damp_last, turned_decay[pl.ds(slots_at, 16), :])
    lam_xy = lx[0:1, :] + lz[pl.ds(ky, 1), :]
    lam_main = lam_xy + jnp.where(at_first, lz[64:65, :], lz[pl.ds(slots_at, 16), :])
    lam_last = lam_xy + lz[64:65, :]

    for damp, lam, base, size in ((damp_main, lam_main, 0, 16), (damp_last, lam_last, 256, 1)):
        theta = 0.5 * jnp.sqrt(lam)
        rate_cos = damp * jnp.cos(theta)
        rate_sin = damp * jnp.sin(theta)
        kernel = 1.0 / (1.0 + lam)
        state = [[jnp.zeros_like(lam)] * 2 for _ in range(2)]
        for step in range(16):
            at_row = base + step * size
            for ri in range(2):
                at = ri * 128
                re, im = state[ri]
                state[ri] = [
                    rate_cos * re - rate_sin * im + spectra[at_row : at_row + size, at : at + 128],
                    rate_cos * im + rate_sin * re,
                ]
                fields[at_row : at_row + size, at : at + 128] = kernel * state[ri][0]
    back = dot_right(fields[...], gx)
    for mp in range(4):
        rows = []
        for n in range(2):
            steps = [4 * mp + 2 * half + n for half in range(2)]
            pieces = []
            for ri in range(2):
                both = []
                for step in steps:
                    piece = back[step * 16 : step * 16 + 16, ri * 128 : ri * 128 + 128]
                    if ri == 1:
                        added = back[256 + step : 257 + step, 0:128]
                        piece = piece + jnp.where(first_row, added, 0.0)
                    both.append(piece)
                pieces.append(
                    (
                        jnp.where(below, both[0], pltpu.roll(both[1], 64, 1)),
                        jnp.where(below, pltpu.roll(both[0], 64, 1), both[1]),
                    )
                )
            for dx in range(2):
                for ri in range(2):
                    rows.append(pieces[ri][dx])
        out[mp * 128 : (mp + 1) * 128, :] = jnp.concatenate(rows, axis=0).T


READ = 72
BY_GATHER = (1, 3, 6)


def field_kernel(recv, cells, gz, gy, cs, out, left):
    pencils = []
    for t in range(4):
        halves_y = [
            jnp.concatenate(
                [
                    recv[(4 * low + q) * 64 : (4 * low + q + 1) * 64, :][:, t * 32 : (t + 1) * 32]
                    for q in range(4)
                ],
                axis=1,
            )
            for low in range(2)
        ]
        pencils.append(jnp.concatenate(halves_y, axis=0))
    both = dot_right(jnp.concatenate(pencils, axis=0), gz)
    tops, bottoms = [], []
    for t in range(4):
        real = pencils[t][:, 0:1]
        imag = pencils[t][:, 16:17]
        tops.append(both[t * 128 : (t + 1) * 128, :128] + (real * cs[0] + imag * cs[1]))
        bottoms.append(both[t * 128 : (t + 1) * 128, 128:] + imag * cs[2])
    tall = jnp.concatenate(
        [jnp.concatenate(tops, axis=1), jnp.concatenate(bottoms, axis=1)], axis=0
    )
    field = dot_left(gy[...], tall)
    rows = []
    for t in range(4):
        plane = field[:, t * 128 : (t + 1) * 128]
        tops = jnp.concatenate([plane[:64], plane[64:]], axis=1)
        after = jnp.concatenate([plane[64:65], plane[0:1]], axis=1)
        before = jnp.concatenate([plane[127:128], plane[63:64]], axis=1)
        rows += [tops, after, before, jnp.zeros((READ - 66, 256), F32)]
    table = jnp.concatenate(rows, axis=0)
    left[...] = jnp.concatenate(split(table), axis=1)
    row = iota((READ, 128), 0)
    row_b = rows_bf16((256, 128), 0)

    def read(pair):
        cell = cells[pair : pair + 1, :]
        cell_y = (cell >> 7) & 63
        gathered = (1,) if pair in BY_GATHER else ()
        products = [dz for dz in range(3) if dz not in gathered]
        hot = jnp.concatenate(
            [
                one_hot(row_b == wide((cell >> 13) * 128 + ((cell + (dz - 1)) & 127), 256))
                for dz in products
            ],
            axis=1,
        )
        lines = dot(left[...], jnp.concatenate([hot, hot], axis=0))
        columns = [None] * 3
        for place, dz in enumerate(products):
            columns[dz] = lines[:, place * 128 : (place + 1) * 128]
        for dz in gathered:
            lane = jnp.broadcast_to((cell + (dz - 1)) & 127, (4 * READ, 128))
            columns[dz] = jnp.where(
                (cell >> 13) == 1,
                jnp.take_along_axis(table[:, 128:], lane, axis=1),
                jnp.take_along_axis(table[:, :128], lane, axis=1),
            )
        hits = [row == y for y in (jnp.where(cell_y == 0, 65, cell_y - 1), cell_y, cell_y + 1)]
        rows = []
        for step in range(2):
            for dx in range(2):
                t = 2 * step + dx
                for dy in range(3):
                    for dz in range(3):
                        line = columns[dz][t * READ : (t + 1) * READ, :]
                        rows.append(
                            jnp.sum(jnp.where(hits[dy], line, 0.0), axis=0, keepdims=True)
                        )
            rows.append(jnp.zeros((KROWS - STEN, 128), F32))
        return jnp.concatenate(rows, axis=0)

    values = [read(pair) for pair in range(8)]
    blocks = []
    for j in range(16):
        blocks.append(values[j // 2][:, (j % 2) * 64 : (j % 2 + 1) * 64])
    write_owner_rows(jnp.concatenate(blocks, axis=0), out)


BY_PRODUCT = 6


def potential_kernel(recv, where, weight, out, turned, left):
    read_owner_rows(recv, turned)
    for high in range(4):
        block = jnp.concatenate(
            [turned[(4 * low + high) * ROWS : (4 * low + high + 1) * ROWS, :] for low in range(4)],
            axis=1,
        )
        left[high * 2 * ROWS : (high + 1) * 2 * ROWS, :] = halves(block)
    boxes = [
        jnp.concatenate(
            [
                turned[(2 * tile) * ROWS : (2 * tile + 1) * ROWS, :],
                turned[(2 * tile + 1) * ROWS : (2 * tile + 2) * ROWS, :],
            ],
            axis=1,
        )
        for tile in range(8)
    ]
    lows = where[:64]
    highs = where[64:]
    lanes = (highs & 1) * 64 + (lows & 63)
    tiles = (lows >> 6) * 2 + (highs >> 1)
    row_b = rows_bf16((256, BY_PRODUCT * 128), 0)

    def put(picked, at):
        terms = picked * doubled(weight[:, at])
        for step in range(2):
            out[step : step + 1, at] = jnp.sum(
                terms[step * KROWS : (step + 1) * KROWS], axis=0, keepdims=True
            )

    for first in range(0, 64, 8):
        pages = range(first, first + BY_PRODUCT)
        low = jnp.concatenate([lows[page : page + 1, :] for page in pages], axis=1)
        high = jnp.concatenate([highs[page : page + 1, :] for page in pages], axis=1)
        lines = dot(left[...], one_hot(row_b == wide(low, 256)))
        for page in range(first + BY_PRODUCT, first + 8):
            lane = jnp.broadcast_to(lanes[page : page + 1, :], (ROWS, 128))
            tile = tiles[page : page + 1, :]
            picked = jnp.take_along_axis(boxes[0], lane, axis=1)
            for other in range(1, 8):
                picked = jnp.where(
                    tile == other, jnp.take_along_axis(boxes[other], lane, axis=1), picked
                )
            put(picked, slice(page * 128, page * 128 + 128))
        picked = lines[: 2 * ROWS]
        for quarter in range(1, 4):
            at_row = quarter * 2 * ROWS
            picked = jnp.where(high == quarter, lines[at_row : at_row + 2 * ROWS], picked)
        put(picked[:ROWS] + picked[ROWS:], slice(first * 128, (first + BY_PRODUCT) * 128))


PARAMS = pltpu.CompilerParams(vmem_limit_bytes=48 * 1024 * 1024)


def f32(*shape):
    return jax.ShapeDtypeStruct(shape, F32)


def i32(*shape):
    return jax.ShapeDtypeStruct(shape, jnp.int32)


def run_panels(source, weight, slots, count, cell):
    return pl.pallas_call(
        panels_kernel,
        out_shape=(f32(64 * WIDTH, 128), i32(128, 128)),
        in_specs=[pl.BlockSpec(memory_space=pltpu.HBM)] * 5,
        scratch_shapes=[
            pltpu.VMEM((2, PDEV), F32),
            pltpu.VMEM((STEN, PDEV), F32),
            pltpu.VMEM((16, BOXES), jnp.int32),
            pltpu.VMEM((1, BOXES), jnp.int32),
            pltpu.VMEM((1, BOXES), jnp.int32),
            pltpu.VMEM((PDEV, 256), BF16),
            pltpu.VMEM((8 * ROWS, PDEV), BF16),
            pltpu.SemaphoreType.DMA((5,)),
        ],
        compiler_params=PARAMS,
        name="panels",
    )(*(pltpu.with_memory_space_constraint(x, pltpu.HBM) for x in (source, weight, slots, count, cell)))


def run_slab(recv, fz, fy):
    return pl.pallas_call(
        slab_kernel,
        out_shape=(f32(512, 128), i32(8, 128)),
        scratch_shapes=[
            pltpu.VMEM((16 * ROWS, 64), F32),
            pltpu.VMEM((2, 8, ROWS, 128), F32),
            pltpu.VMEM((4 * HALF, 3 * BOXES), BF16),
            pltpu.VMEM((4 * HALF, 3 * BOXES), BF16),
            pltpu.VMEM((3 * BOXES, 256), BF16),
        ],
        compiler_params=PARAMS,
        name="slab",
    )(recv, fz, fy)


def run_column(place, recv, decay, fx, gx, lz, lx):
    return pl.pallas_call(
        column_kernel,
        out_shape=f32(512, 128),
        in_specs=[pl.BlockSpec(memory_space=pltpu.SMEM)]
        + [pl.BlockSpec(memory_space=pltpu.VMEM)] * 6,
        scratch_shapes=[
            pltpu.VMEM((128, 128), F32),
            pltpu.VMEM((272, 256), F32),
            pltpu.VMEM((272, 256), F32),
        ],
        compiler_params=PARAMS,
        name="column",
    )(place, recv, decay, fx, gx, lz, lx)


def run_field(recv, cells, gz, gy, cs):
    return pl.pallas_call(
        field_kernel,
        out_shape=f32(64 * WIDTH, 128),
        scratch_shapes=[pltpu.VMEM((4 * READ, 512), BF16)],
        compiler_params=PARAMS,
        name="field",
    )(recv, cells, gz, gy, cs)


def run_potential(recv, where, weight):
    return pl.pallas_call(
        potential_kernel,
        out_shape=f32(2, PDEV),
        scratch_shapes=[pltpu.VMEM((16 * ROWS, 64), F32), pltpu.VMEM((8 * ROWS, 256), BF16)],
        compiler_params=PARAMS,
        name="potential",
    )(recv, where, weight)


def exchange(rows, parts, axes):
    pieces = rows.reshape(parts, 1, rows.size // parts)
    pieces = lax.all_to_all(pieces, axes, split_axis=0, concat_axis=0, tiled=True)
    return pieces.reshape(rows.shape)


def body(panel_source, proj_weight, box_slots, box_count, box_cell, decay):
    table = {name: jnp.asarray(value) for name, value in tables().items()}
    place = jnp.stack([lax.axis_index("tm"), lax.axis_index("grid")]).astype(jnp.int32)
    box_count, place = lax.optimization_barrier((box_count, place))
    out, where = run_panels(
        panel_source, proj_weight, box_slots, box_count.reshape(1, -1), box_cell.reshape(1, -1)
    )
    recv = exchange(out, 64, "grid")
    out, cells = run_slab(recv, table["fz"], table["fy"])
    recv = exchange(out, 512, ("tm", "grid"))
    out = run_column(
        place, recv, decay.reshape(2 * N, N), table["fx"], table["gx"], table["lz"], table["lx"]
    )
    recv = exchange(out, 512, ("tm", "grid"))
    out = run_field(recv, cells, table["gz"], table["gy"], table["cs"])
    recv = exchange(out, 64, "grid")
    return run_potential(recv, where, proj_weight)


def solution(mesh):
    return jax.shard_map(
        body,
        mesh=mesh,
        in_specs=(
            P("tm", "grid"),
            P(None, "grid"),
            P(None, "grid"),
            P("grid"),
            P("grid"),
            P(None, "grid", None),
        ),
        out_specs=P("tm", "grid"),
        check_vma=False,
    )
```

```python
import jax
import jax.numpy as jnp
import ml_dtypes
import numpy as np
from jax import lax
from jax.experimental import pallas as pl
from jax.experimental.pallas import tpu as pltpu
from jax.sharding import PartitionSpec as P

N = 128
STEN = 18
KROWS = 20
CELL_ROW = 18
ROWS = 2 * KROWS
WIDTH = 16 * ROWS // 128
PDEV = 8192
BOXES = 1024
F32 = jnp.float32
BF16 = jnp.bfloat16


def stacked(table, axis):
    table = np.asarray(table, np.float64).astype(np.float32)
    high = table.astype(ml_dtypes.bfloat16)
    low = (table - high.astype(np.float32)).astype(ml_dtypes.bfloat16)
    return np.concatenate([high, high, low], axis=axis)


def angle(rows, cols):
    return 2.0 * np.pi * (np.outer(rows, cols) % N) / N


def tables():
    index = np.arange(N)
    slot = (index // 32) * 16 + index % 16
    imag = (index // 16) % 2 == 1
    ang = angle(index, slot)
    real_z = np.cos(ang)
    imag_z = np.where(slot[None] == 0, np.cos(np.pi * index)[:, None], -np.sin(ang))
    fz = np.concatenate(
        [np.where(imag[None], imag_z, real_z), np.where(imag[None], -real_z, imag_z)], axis=1
    )
    ky = np.concatenate([2 * np.arange(64), 2 * np.arange(64) + 1])
    ay = angle(ky, index)
    fy = np.stack([np.cos(ay), np.sin(ay)])

    grid = np.arange(64)
    fx = np.zeros((2, 2, 64, 2, N))
    gx = np.zeros((2, N, 2, 2, 64))
    for dx in range(2):
        ax = angle(2 * grid + dx, index)
        cos, sin = np.cos(ax), np.sin(ax)
        fx[0, dx, :, 0] = cos
        fx[0, dx, :, 1] = -sin
        fx[1, dx, :, 0] = sin
        fx[1, dx, :, 1] = cos
        gx[0, :, 0, dx] = cos.T / N
        gx[0, :, 1, dx] = sin.T / N
        gx[1, :, 0, dx] = -sin.T / N
        gx[1, :, 1, dx] = cos.T / N
    fx = fx.reshape(256, 256)
    gx = gx.reshape(256, 256)

    weight = np.where(slot == 0, 0.0, 2.0)[:, None] / N
    cz = np.cos(ang.T) * weight
    sz = np.sin(ang.T) * weight
    gz = np.concatenate(
        [np.where(imag[:, None], -sz, cz), np.where(imag[:, None], -cz, -sz)], axis=1
    )
    gy = np.concatenate([np.cos(ay.T), np.sin(ay.T)], axis=1) / N
    self_row = (ky == 0) | (ky == 64)
    pattern = np.where((ky <= 64)[:, None], 1.0, np.cos(np.pi * index)[None])
    c1 = np.where(self_row, 1.0, 2.0)[:, None] * pattern / N
    c2 = np.where(self_row[:, None], np.cos(np.pi * index)[None], 0.0) / N
    c3 = np.where(self_row[:, None], 0.0, -2.0 * pattern) / N
    cs = np.stack([c1, c2, c3]).astype(np.float32)

    lam = 4.0 * np.sin(np.pi * index / N) ** 2
    lz = np.broadcast_to(lam[:, None], (N, N)).astype(np.float32)
    lx = np.broadcast_to(lam[None], (8, N)).astype(np.float32)
    return dict(
        fz=stacked(fz, 0), fy=stacked(fy, 2), fx=stacked(fx, 0), gx=stacked(gx, 0),
        gz=stacked(gz, 0), gy=stacked(gy, 1),
        cs=cs, lz=lz, lx=lx,
    )


def split(values):
    high = values.astype(BF16)
    return high, (values - high.astype(F32)).astype(BF16)


def halves(values):
    high = values.astype(BF16).astype(F32)
    return jnp.concatenate([high, values - high], axis=0).astype(BF16)


def doubled(tile):
    tile = jnp.concatenate([tile, jnp.zeros((KROWS - STEN, tile.shape[1]), F32)], axis=0)
    return jnp.concatenate([tile, tile], axis=0)


def dot(left, right):
    return lax.dot_general(left, right, (((1,), (0,)), ((), ())), preferred_element_type=F32)


def dot_nt(left, right):
    return lax.dot_general(left, right, (((1,), (1,)), ((), ())), preferred_element_type=F32)


def dot_right(values, table):
    high, low = split(values)
    return dot(jnp.concatenate([high, low, high], axis=1), table[...])


def dot_left(table, values):
    high, low = split(values)
    return dot(table, jnp.concatenate([high, low, high], axis=0))


def iota(shape, axis):
    return lax.broadcasted_iota(jnp.int32, shape, axis)


def rows_bf16(shape, axis):
    return iota(shape, axis).astype(F32).astype(BF16)


def wide(row, size):
    sixteen = jnp.broadcast_to(row.astype(F32), (16, row.shape[1])).astype(BF16)
    return jnp.concatenate([sixteen] * (size // 16), axis=0)


def one_hot(mask):
    return jnp.where(mask, jnp.ones((), BF16), jnp.zeros((), BF16))


def write_owner_rows(turned, out_ref):
    for part in range(WIDTH):
        out_ref[pl.ds(part, 64, stride=WIDTH), :] = turned[part * 128 : (part + 1) * 128, :].T


def read_owner_rows(in_ref, turned_ref):
    for part in range(WIDTH):
        turned_ref[part * 128 : (part + 1) * 128, :] = in_ref[pl.ds(part, 64, stride=WIDTH), :].T


PAGES = 8


def panels_kernel(
    source_hbm, weight_hbm, slots_hbm, count_hbm, cell_hbm, out, where,
    source, weight, slots, count, cell, oh_ref, left_ref, sems,
):
    pairs = (
        (cell_hbm, cell), (count_hbm, count), (slots_hbm, slots), (weight_hbm, weight),
        (source_hbm, source),
    )
    copies = [pltpu.make_async_copy(a, b, sems.at[i]) for i, (a, b) in enumerate(pairs)]
    for copy in copies:
        copy.start()
    box = iota((1, BOXES), 1)
    row64 = rows_bf16((64, BOXES), 0)
    none = jnp.zeros((), BF16)

    copies[0].wait()
    cells = cell[...]
    match = rows_bf16((16, BOXES), 0) == wide(box & 15, 16)
    left = jnp.concatenate(
        [
            jnp.where(match, wide(cells >> 7, 16), none),
            jnp.where(match, wide(cells & 127, 16), none),
        ],
        axis=0,
    )
    owned = dot_nt(left, one_hot(row64 == wide(box >> 4, 64)))
    cell_rows = owned[:16] * 128.0 + owned[16:]

    copies[1].wait()
    copies[2].wait()
    low_value = wide(((box >> 2) & 3) * 64 + (box >> 4), 64)
    high_value = wide(box & 3, 64)
    row128 = rows_bf16((128, BOXES), 0)

    def invert(s, total):
        panel = slots[pl.ds(s, 1), :]
        page = jnp.where(s < count[...], panel >> 7, 200)
        hit = row64 == wide(page, 64)
        left = jnp.concatenate(
            [jnp.where(hit, low_value, none), jnp.where(hit, high_value, none)], axis=0
        )
        return total + dot_nt(left, one_hot(row128 == wide(panel & 127, 128)))

    total = lax.fori_loop(0, 16, invert, jnp.zeros((128, 128), F32), unroll=True)
    where_now = (total + 0.5).astype(jnp.int32)
    where[...] = where_now
    copies[3].wait()
    copies[4].wait()
    lane256 = rows_bf16((128, 256), 1)
    low_columns = where_now[:64].astype(F32).T.astype(BF16)
    first_step = iota((ROWS, 128), 0) < KROWS

    def spread(page):
        at = page * 128
        low = jnp.broadcast_to(low_columns[:, page : page + 1], (128, 256))
        high = wide(where_now[64 + page : 65 + page, :], 2 * ROWS)
        oh_ref[at : at + 128, :] = one_hot(lane256 == low)
        both = doubled(weight[:, at : at + 128]) * jnp.where(
            first_step, source[0:1, at : at + 128], source[1:2, at : at + 128]
        )
        pieces = halves(both)
        for quarter in range(4):
            left_ref[quarter * 2 * ROWS : (quarter + 1) * 2 * ROWS, at : at + 128] = jnp.where(
                high == jnp.full((), quarter, BF16), pieces, none
            )

    sums = jnp.zeros((8 * ROWS, 256), F32)
    for chunk in range(64 // PAGES):
        for page in range(PAGES):
            spread(chunk * PAGES + page)
        at = slice(chunk * PAGES * 128, (chunk + 1) * PAGES * 128)
        sums = sums + dot(left_ref[:, at], oh_ref[at, :])

    blocks = []
    at_cell = iota((ROWS, 64), 0) == CELL_ROW
    for j in range(16):
        at = (j % 4) * 2 * ROWS
        block = sums[at : at + 2 * ROWS, (j // 4) * 64 : (j // 4 + 1) * 64]
        block = block[:ROWS] + block[ROWS:]
        blocks.append(jnp.where(at_cell, cell_rows[j : j + 1, :], block))
    write_owner_rows(jnp.concatenate(blocks, axis=0), out)


PAIRS = 2
HALF = 80


def slab_kernel(recv, fz, fy, out, cell_out, turned, values, left_h, left_l, right):
    read_owner_rows(recv, turned)
    lane = iota((128, 128), 1)
    row = iota((128, 128), 0)
    row_b = rows_bf16((HALF, 128), 0)
    lane_b = rows_bf16((128, 256), 1)
    none = jnp.zeros((HALF, 128), BF16)
    spots = []
    for pair in range(8):
        value = jnp.concatenate(
            [
                turned[(2 * pair) * ROWS : (2 * pair + 1) * ROWS, :],
                turned[(2 * pair + 1) * ROWS : (2 * pair + 2) * ROWS, :],
            ],
            axis=1,
        )
        high = value.astype(BF16).astype(F32)
        values[0, pair] = high
        values[1, pair] = value - high
        cell = value[CELL_ROW : CELL_ROW + 1, :].astype(jnp.int32)
        cell_out[pair : pair + 1, :] = cell
        for dz in range(3):
            spots.append((cell >> 13) * 128 + ((cell + (dz - 1)) & 127))
    spots = jnp.concatenate(spots, axis=0).astype(F32).T.astype(BF16)

    def fill(pair):
        cell_y = (cell_out[pair : pair + 1, :] >> 7) & 63
        at_y = [jnp.where(cell_y == 0, 65, cell_y - 1), cell_y, cell_y + 1]
        hits = [row_b == wide(y, HALF) for y in at_y]
        for dz in range(3):
            column = pair * 3 + dz
            at = column * 128
            right[at : at + 128, :] = one_hot(
                lane_b == jnp.broadcast_to(spots[:, column : column + 1], (128, 256))
            )
            for step in range(2):
                for dx in range(2):
                    at_row = (2 * step + dx) * HALF
                    for part, target in ((0, left_h), (1, left_l)):
                        block = none
                        for dy in range(3):
                            k = step * KROWS + 9 * dx + 3 * dy + dz
                            block = jnp.where(
                                hits[dy], wide(values[part, pair, k : k + 1, :], HALF), block
                            )
                        target[at_row : at_row + HALF, at : at + 128] = block

    halved = jnp.zeros((4 * HALF, 256), F32)
    for group in range(8 // PAIRS):
        for pair in range(PAIRS):
            fill(PAIRS * group + pair)
        at = slice(group * PAIRS * 384, (group + 1) * PAIRS * 384)
        halved = halved + (dot(left_h[:, at], right[at, :]) + dot(left_l[:, at], right[at, :]))
    row64 = iota((64, 128), 0)
    planes = []
    for t in range(4):
        for half in range(2):
            here = slice(half * 128, half * 128 + 128)
            other = slice(128 - half * 128, 256 - half * 128)
            part = halved[t * HALF : t * HALF + 64, here]
            part = part + jnp.where(
                row64 == 0, halved[t * HALF + 64 : t * HALF + 65, other], 0.0
            )
            part = part + jnp.where(
                row64 == 63, halved[t * HALF + 65 : t * HALF + 66, other], 0.0
            )
            planes.append(part)
    density = jnp.concatenate(planes, axis=0)
    both = dot_right(density, fz)

    def beside(at):
        return jnp.concatenate(
            [both[t * 128 : (t + 1) * 128, at : at + 128] for t in range(4)], axis=1
        )

    even = dot_left(fy[0], beside(0))
    odd = dot_left(fy[1], beside(128))
    ky = (row & 63) * 2 + (row >> 6)
    own = (ky == 0) | (ky == 64)
    pencils = []
    for t in range(4):
        a = even[:, t * 128 : (t + 1) * 128]
        b = odd[:, t * 128 : (t + 1) * 128]
        full = a + b
        full = jnp.where(lane == 0, jnp.where(ky <= 64, a, pltpu.roll(a, 112, 1)), full)
        second = jnp.where(own, a, jnp.where(ky < 64, b, -pltpu.roll(b, 16, 1)))
        pencils.append(jnp.where(lane == 16, second, full))
    for q in range(4):
        piece = jnp.concatenate([p[:, q * 32 : (q + 1) * 32] for p in pencils], axis=1)
        out[q * 64 : (q + 1) * 64, :] = piece[:64]
        out[(4 + q) * 64 : (5 + q) * 64, :] = piece[64:]


def column_kernel(place, recv, decay, fx, gx, lz, lx, out, turned_decay, spectra, fields):
    block = place[0]
    column = place[1]
    ky_low = block // 4
    q = block % 4
    ky = 2 * column + ky_low
    special = ((block == 0) & ((column == 0) | (column == 32))).astype(jnp.int32)
    below = iota((16, 128), 1) < 64
    first_row = iota((16, 128), 0) == 0
    mains, extras = [], []
    for mp in range(4):
        part = recv[mp * 128 : (mp + 1) * 128, :].T
        for half in range(2):
            for n in range(2):
                pieces = []
                for ri in range(2):
                    near = part[(2 * n) * 32 + ri * 16 : (2 * n) * 32 + ri * 16 + 16, :]
                    far = part[(2 * n + 1) * 32 + ri * 16 : (2 * n + 1) * 32 + ri * 16 + 16, :]
                    if half == 0:
                        far = pltpu.roll(far, 64, 1)
                    else:
                        near = pltpu.roll(near, 64, 1)
                    pieces.append(jnp.where(below, near, far))
                extras.append(jnp.where(special == 1, pieces[1][0:1], 0.0))
                pieces[1] = jnp.where(first_row & (special == 1), 0.0, pieces[1])
                mains.append(jnp.concatenate(pieces, axis=1))
    extra = jnp.concatenate(extras, axis=0)
    mains.append(jnp.concatenate([extra, jnp.zeros_like(extra)], axis=1))
    spectra[...] = dot_right(jnp.concatenate(mains, axis=0), fx)

    here = jnp.where(
        ky_low == 1, decay[pl.ds(1, 128, stride=2), :], decay[pl.ds(0, 128, stride=2), :]
    )
    turned_decay[...] = here.T
    slots_at = pl.multiple_of(q * 16, 16)
    moved = jnp.where((q == 0) & (ky > 64), 1, 0)
    at_first = iota((16, 128), 0) + (1 - moved) == 0
    damp_last = turned_decay[64:65, :]
    damp_main = jnp.where(at_first, damp_last, turned_decay[pl.ds(slots_at, 16), :])
    lam_xy = lx[0:1, :] + lz[pl.ds(ky, 1), :]
    lam_main = lam_xy + jnp.where(at_first, lz[64:65, :], lz[pl.ds(slots_at, 16), :])
    lam_last = lam_xy + lz[64:65, :]

    for damp, lam, base, size in ((damp_main, lam_main, 0, 16), (damp_last, lam_last, 256, 1)):
        theta = 0.5 * jnp.sqrt(lam)
        rate_cos = damp * jnp.cos(theta)
        rate_sin = damp * jnp.sin(theta)
        kernel = 1.0 / (1.0 + lam)
        state = [[jnp.zeros_like(lam)] * 2 for _ in range(2)]
        for step in range(16):
            at_row = base + step * size
            for ri in range(2):
                at = ri * 128
                re, im = state[ri]
                state[ri] = [
                    rate_cos * re - rate_sin * im + spectra[at_row : at_row + size, at : at + 128],
                    rate_cos * im + rate_sin * re,
                ]
                fields[at_row : at_row + size, at : at + 128] = kernel * state[ri][0]
    back = dot_right(fields[...], gx)
    for mp in range(4):
        rows = []
        for n in range(2):
            steps = [4 * mp + 2 * half + n for half in range(2)]
            pieces = []
            for ri in range(2):
                both = []
                for step in steps:
                    piece = back[step * 16 : step * 16 + 16, ri * 128 : ri * 128 + 128]
                    if ri == 1:
                        added = back[256 + step : 257 + step, 0:128]
                        piece = piece + jnp.where(first_row, added, 0.0)
                    both.append(piece)
                pieces.append(
                    (
                        jnp.where(below, both[0], pltpu.roll(both[1], 64, 1)),
                        jnp.where(below, pltpu.roll(both[0], 64, 1), both[1]),
                    )
                )
            for dx in range(2):
                for ri in range(2):
                    rows.append(pieces[ri][dx])
        out[mp * 128 : (mp + 1) * 128, :] = jnp.concatenate(rows, axis=0).T


READ = 72
BY_GATHER = (1, 3, 6)


def field_kernel(recv, cells, gz, gy, cs, out, left):
    pencils = []
    for t in range(4):
        halves_y = [
            jnp.concatenate(
                [
                    recv[(4 * low + q) * 64 : (4 * low + q + 1) * 64, :][:, t * 32 : (t + 1) * 32]
                    for q in range(4)
                ],
                axis=1,
            )
            for low in range(2)
        ]
        pencils.append(jnp.concatenate(halves_y, axis=0))
    both = dot_right(jnp.concatenate(pencils, axis=0), gz)
    tops, bottoms = [], []
    for t in range(4):
        real = pencils[t][:, 0:1]
        imag = pencils[t][:, 16:17]
        tops.append(both[t * 128 : (t + 1) * 128, :128] + (real * cs[0] + imag * cs[1]))
        bottoms.append(both[t * 128 : (t + 1) * 128, 128:] + imag * cs[2])
    tall = jnp.concatenate(
        [jnp.concatenate(tops, axis=1), jnp.concatenate(bottoms, axis=1)], axis=0
    )
    field = dot_left(gy[...], tall)
    rows = []
    for t in range(4):
        plane = field[:, t * 128 : (t + 1) * 128]
        tops = jnp.concatenate([plane[:64], plane[64:]], axis=1)
        after = jnp.concatenate([plane[64:65], plane[0:1]], axis=1)
        before = jnp.concatenate([plane[127:128], plane[63:64]], axis=1)
        rows += [tops, after, before, jnp.zeros((READ - 66, 256), F32)]
    table = jnp.concatenate(rows, axis=0)
    left[...] = jnp.concatenate(split(table), axis=1)
    row = iota((READ, 128), 0)
    row_b = rows_bf16((256, 128), 0)

    def read(pair):
        cell = cells[pair : pair + 1, :]
        cell_y = (cell >> 7) & 63
        gathered = (1,) if pair in BY_GATHER else ()
        products = [dz for dz in range(3) if dz not in gathered]
        hot = jnp.concatenate(
            [
                one_hot(row_b == wide((cell >> 13) * 128 + ((cell + (dz - 1)) & 127), 256))
                for dz in products
            ],
            axis=1,
        )
        lines = dot(left[...], jnp.concatenate([hot, hot], axis=0))
        columns = [None] * 3
        for place, dz in enumerate(products):
            columns[dz] = lines[:, place * 128 : (place + 1) * 128]
        for dz in gathered:
            lane = jnp.broadcast_to((cell + (dz - 1)) & 127, (4 * READ, 128))
            columns[dz] = jnp.where(
                (cell >> 13) == 1,
                jnp.take_along_axis(table[:, 128:], lane, axis=1),
                jnp.take_along_axis(table[:, :128], lane, axis=1),
            )
        hits = [row == y for y in (jnp.where(cell_y == 0, 65, cell_y - 1), cell_y, cell_y + 1)]
        rows = []
        for step in range(2):
            for dx in range(2):
                t = 2 * step + dx
                for dy in range(3):
                    for dz in range(3):
                        line = columns[dz][t * READ : (t + 1) * READ, :]
                        rows.append(
                            jnp.sum(jnp.where(hits[dy], line, 0.0), axis=0, keepdims=True)
                        )
            rows.append(jnp.zeros((KROWS - STEN, 128), F32))
        return jnp.concatenate(rows, axis=0)

    values = [read(pair) for pair in range(8)]
    blocks = []
    for j in range(16):
        blocks.append(values[j // 2][:, (j % 2) * 64 : (j % 2 + 1) * 64])
    write_owner_rows(jnp.concatenate(blocks, axis=0), out)


BY_PRODUCT = 6


def potential_kernel(recv, where, weight, out, turned, left):
    read_owner_rows(recv, turned)
    for high in range(4):
        block = jnp.concatenate(
            [turned[(4 * low + high) * ROWS : (4 * low + high + 1) * ROWS, :] for low in range(4)],
            axis=1,
        )
        left[high * 2 * ROWS : (high + 1) * 2 * ROWS, :] = halves(block)
    boxes = [
        jnp.concatenate(
            [
                turned[(2 * tile) * ROWS : (2 * tile + 1) * ROWS, :],
                turned[(2 * tile + 1) * ROWS : (2 * tile + 2) * ROWS, :],
            ],
            axis=1,
        )
        for tile in range(8)
    ]
    lows = where[:64]
    highs = where[64:]
    lanes = (highs & 1) * 64 + (lows & 63)
    tiles = (lows >> 6) * 2 + (highs >> 1)
    row_b = rows_bf16((256, BY_PRODUCT * 128), 0)

    def put(picked, at):
        terms = picked * doubled(weight[:, at])
        for step in range(2):
            out[step : step + 1, at] = jnp.sum(
                terms[step * KROWS : (step + 1) * KROWS], axis=0, keepdims=True
            )

    for first in range(0, 64, 8):
        pages = range(first, first + BY_PRODUCT)
        low = jnp.concatenate([lows[page : page + 1, :] for page in pages], axis=1)
        high = jnp.concatenate([highs[page : page + 1, :] for page in pages], axis=1)
        lines = dot(left[...], one_hot(row_b == wide(low, 256)))
        for page in range(first + BY_PRODUCT, first + 8):
            lane = jnp.broadcast_to(lanes[page : page + 1, :], (ROWS, 128))
            tile = tiles[page : page + 1, :]
            picked = jnp.take_along_axis(boxes[0], lane, axis=1)
            for other in range(1, 8):
                picked = jnp.where(
                    tile == other, jnp.take_along_axis(boxes[other], lane, axis=1), picked
                )
            put(picked, slice(page * 128, page * 128 + 128))
        picked = lines[: 2 * ROWS]
        for quarter in range(1, 4):
            at_row = quarter * 2 * ROWS
            picked = jnp.where(high == quarter, lines[at_row : at_row + 2 * ROWS], picked)
        put(picked[:ROWS] + picked[ROWS:], slice(first * 128, (first + BY_PRODUCT) * 128))


PARAMS = pltpu.CompilerParams(vmem_limit_bytes=48 * 1024 * 1024)


def f32(*shape):
    return jax.ShapeDtypeStruct(shape, F32)


def i32(*shape):
    return jax.ShapeDtypeStruct(shape, jnp.int32)


def run_panels(source, weight, slots, count, cell):
    return pl.pallas_call(
        panels_kernel,
        out_shape=(f32(64 * WIDTH, 128), i32(128, 128)),
        in_specs=[pl.BlockSpec(memory_space=pltpu.HBM)] * 5,
        scratch_shapes=[
            pltpu.VMEM((2, PDEV), F32),
            pltpu.VMEM((STEN, PDEV), F32),
            pltpu.VMEM((16, BOXES), jnp.int32),
            pltpu.VMEM((1, BOXES), jnp.int32),
            pltpu.VMEM((1, BOXES), jnp.int32),
            pltpu.VMEM((PDEV, 256), BF16),
            pltpu.VMEM((8 * ROWS, PDEV), BF16),
            pltpu.SemaphoreType.DMA((5,)),
        ],
        compiler_params=PARAMS,
        name="panels",
    )(*(pltpu.with_memory_space_constraint(x, pltpu.HBM) for x in (source, weight, slots, count, cell)))


def run_slab(recv, fz, fy):
    return pl.pallas_call(
        slab_kernel,
        out_shape=(f32(512, 128), i32(8, 128)),
        scratch_shapes=[
            pltpu.VMEM((16 * ROWS, 64), F32),
            pltpu.VMEM((2, 8, ROWS, 128), F32),
            pltpu.VMEM((4 * HALF, 3 * BOXES), BF16),
            pltpu.VMEM((4 * HALF, 3 * BOXES), BF16),
            pltpu.VMEM((3 * BOXES, 256), BF16),
        ],
        compiler_params=PARAMS,
        name="slab",
    )(recv, fz, fy)


def run_column(place, recv, decay, fx, gx, lz, lx):
    return pl.pallas_call(
        column_kernel,
        out_shape=f32(512, 128),
        in_specs=[pl.BlockSpec(memory_space=pltpu.SMEM)]
        + [pl.BlockSpec(memory_space=pltpu.VMEM)] * 6,
        scratch_shapes=[
            pltpu.VMEM((128, 128), F32),
            pltpu.VMEM((272, 256), F32),
            pltpu.VMEM((272, 256), F32),
        ],
        compiler_params=PARAMS,
        name="column",
    )(place, recv, decay, fx, gx, lz, lx)


def run_field(recv, cells, gz, gy, cs):
    return pl.pallas_call(
        field_kernel,
        out_shape=f32(64 * WIDTH, 128),
        scratch_shapes=[pltpu.VMEM((4 * READ, 512), BF16)],
        compiler_params=PARAMS,
        name="field",
    )(recv, cells, gz, gy, cs)


def run_potential(recv, where, weight):
    return pl.pallas_call(
        potential_kernel,
        out_shape=f32(2, PDEV),
        scratch_shapes=[pltpu.VMEM((16 * ROWS, 64), F32), pltpu.VMEM((8 * ROWS, 256), BF16)],
        compiler_params=PARAMS,
        name="potential",
    )(recv, where, weight)


def exchange(rows, parts, axes):
    pieces = rows.reshape(parts, 1, rows.size // parts)
    pieces = lax.all_to_all(pieces, axes, split_axis=0, concat_axis=0, tiled=True)
    return pieces.reshape(rows.shape)


def body(panel_source, proj_weight, box_slots, box_count, box_cell, decay):
    table = {name: jnp.asarray(value) for name, value in tables().items()}
    place = jnp.stack([lax.axis_index("tm"), lax.axis_index("grid")]).astype(jnp.int32)
    box_count, place = lax.optimization_barrier((box_count, place))
    out, where = run_panels(
        panel_source, proj_weight, box_slots, box_count.reshape(1, -1), box_cell.reshape(1, -1)
    )
    recv = exchange(out, 64, "grid")
    out, cells = run_slab(recv, table["fz"], table["fy"])
    recv = exchange(out, 512, ("tm", "grid"))
    out = run_column(
        place, recv, decay.reshape(2 * N, N), table["fx"], table["gx"], table["lz"], table["lx"]
    )
    recv = exchange(out, 512, ("tm", "grid"))
    out = run_field(recv, cells, table["gz"], table["gy"], table["cs"])
    recv = exchange(out, 64, "grid")
    return run_potential(recv, where, proj_weight)


def solution(mesh):
    return jax.shard_map(
        body,
        mesh=mesh,
        in_specs=(
            P("tm", "grid"),
            P(None, "grid"),
            P(None, "grid"),
            P("grid"),
            P("grid"),
            P(None, "grid", None),
        ),
        out_specs=P("tm", "grid"),
        check_vma=False,
    )
```
